32 devices in a mesh: fsdp: 4 (over z), ctx: 4 (over x, core), tp: 2 (over y).
Axes of the slice: x: 2, y: 2, z: 4, core: 2. Of those that a mesh axis runs over, the one named last changes fastest.
Arguments:
- tokens: bfloat16 [4, 2176, 1536], P('fsdp', ('ctx', 'tp')), may hold values from -30 to 30
- segment_ids: int32 [4, 2176], P('fsdp', 'ctx'), may hold values from 0 to 7, never falling along the last dimension, each value on 1 to 1088 neighbouring positions
- wq: bfloat16 [1536, 1536], P('fsdp', 'tp'), may hold values from -0.15625 to 0.15625
- wk: bfloat16 [1536, 1536], P('fsdp', 'tp'), may hold values from -0.15625 to 0.15625
- wv: bfloat16 [1536, 1536], P('fsdp', 'tp'), may hold values from -0.15625 to 0.15625
- wo: bfloat16 [1536, 1536], P('tp', 'fsdp'), may hold values from -0.875 to 0.875
- w_gate: bfloat16 [1536, 4096], P('fsdp', 'tp'), may hold values from -0.15625 to 0.15625
- w_up: bfloat16 [1536, 4096], P('fsdp', 'tp'), may hold values from -0.15625 to 0.15625
- w_down: bfloat16 [4096, 1536], P('tp', 'fsdp'), may hold values from -0.09375 to 0.09375
- gain_attn: bfloat16 [1536], P('fsdp'), may hold values from 0.099609375 to 1.8984375
- gain_ffn: bfloat16 [1536], P('fsdp'), may hold values from 0.099609375 to 1.8984375
- cotangent: bfloat16 [4, 2176, 1536], P('fsdp', ('ctx', 'tp')), may hold values from -6 to 6
Outputs:
- layer_out: bfloat16 [4, 2176, 1536], P('fsdp', ('ctx', 'tp'))
- grad_input: float32 [4, 2176, 1536], P('fsdp', ('ctx', 'tp'))
- query_weight_gradient: float32 [1536, 1536], P('fsdp', 'tp')
- key_weight_gradient: float32 [1536, 1536], P('fsdp', 'tp')
- value_weight_gradient: float32 [1536, 1536], P('fsdp', 'tp')
- output_weight_gradient: float32 [1536, 1536], P('tp', 'fsdp')
- gate_weight_gradient: float32 [1536, 4096], P('fsdp', 'tp')
- up_weight_gradient: float32 [1536, 4096], P('fsdp', 'tp')
- down_weight_gradient: float32 [4096, 1536], P('tp', 'fsdp')
- grad_gain_attn: float32 [1536], P('fsdp')
- grad_gain_ffn: float32 [1536], P('fsdp')
The draws below stay inside these ranges and needn't reach their ends.
Inputs may be any that keep to these rules, and one draw needn't show every extreme that they name: `segment_ids`: within each sequence the ids never fall; each document holds 1 to 1088 positions, and one document of every sequence holds exactly 1088.
All inputs are finite; a program needn't handle non-finite values.
Results may differ from the reference program's by a relative error of at most 0.024.
Values may be sent and summed in bfloat16 or wider, within the bound.
No kernel may reach another device: no remote copies, remote signals or barrier semaphores. Data moves between devices by JAX's collectives and lax.ppermute only.
A program may use at most 320 MiB of HBM per device.

```python
import math
import jax
import jax.numpy as jnp
import numpy as np
from jax import lax

D = 1536
HEADS = 24
HEAD_DIM = 64
FF = 4096
LEN = 2176
SEQS = 4


def draw_tokens(key, part):
    key_base, key_rows, key_cols = jax.random.split(jax.random.fold_in(key, 11), 3)
    base_draw = jnp.clip(jax.random.normal(key_base, (SEQS, LEN, D), jnp.float32), -5.0, 5.0)
    row_scale = jnp.exp(jax.random.uniform(key_rows, (SEQS, LEN, 1), jnp.float32, math.log(0.3), math.log(3.0)))
    col_scale = jnp.exp(jax.random.uniform(key_cols, (1, 1, D), jnp.float32, math.log(0.5), math.log(2.0)))
    return (base_draw * row_scale * col_scale).astype(jnp.bfloat16)


def steps_of(stream_key, dims, pieces, least, high):
    factor_of = 1.0
    for dim, shards_of in pieces:
        steps = jax.random.uniform(jax.random.fold_in(jax.random.fold_in(stream_key, 6), dim), (shards_of,), jnp.float32, least / len(pieces), high / len(pieces))
        factor_of = factor_of * jnp.repeat(jnp.exp(steps), dims[dim] // shards_of).reshape((-1,) + (1,) * (len(dims) - 1 - dim))
    return factor_of


def profile(count, total, bound, slope):
    weights = [(1 << 20) // math.isqrt(standing ** slope) + 1 for standing in range(2, count + 1)]
    spare, holding = total - bound - (count - 1), [1] * (count - 1)
    while spare > 0:
        candidates = [i for i in range(count - 1) if holding[i] < bound]
        pool, remaining = sum([weights[i] for i in candidates]), spare
        for i in candidates:
            addition = min(bound - holding[i], max(1, remaining * weights[i] // pool), spare)
            holding[i] = holding[i] + addition
            spare = spare - addition
    return np.array([bound] + holding)


def ragged_sizes(key, amount, total, limit, slope):
    if amount == 2:
        one = jax.random.randint(key, (), max(1, total - limit), min(limit, total - 1) + 1)
        return jnp.stack([one, total - one])
    sizes = jnp.asarray(profile(amount, total, limit, slope), jnp.int32)
    twos = (amount - 1) // 2
    giver, sink = sizes[1:1 + 2 * twos:2], sizes[2:2 + 2 * twos:2]
    room = jnp.minimum(giver - 1, limit - sink)
    moved = jax.random.randint(jax.random.fold_in(key, 1), (twos,), 0, 1 << 20) % (room + 1)
    sizes = sizes.at[1:1 + 2 * twos:2].set(giver - moved).at[2:2 + 2 * twos:2].set(sink + moved)
    return sizes[jax.random.permutation(jax.random.fold_in(key, 2), amount)]


def scatter_about(stream_key, dims, spread, most, shards=(), held_as=jnp.bfloat16):
    level = steps_of(stream_key, dims, shards, -0.22, 0.18) if shards else 1.0
    array = jax.random.normal(stream_key, dims, jnp.float32) * spread * level
    return jnp.minimum(jnp.maximum(array, -most), most).astype(held_as)


def setup_inputs(seed: int = 0) -> dict:
    streams_of = jax.random.split(jax.random.key(seed), 13)
    tokens = draw_tokens(jax.random.fold_in(streams_of[12], 71), 0)
    segment_ids = jax.vmap(lambda own: jnp.searchsorted(jnp.cumsum(ragged_sizes(own, max(4, LEN // 272), LEN, LEN // 2, 2)), jnp.arange(LEN), side="right"))(jax.random.split(streams_of[1], SEQS)).reshape((SEQS, LEN)).astype(jnp.int32)
    wq = scatter_about(streams_of[2], (D, D), D ** -0.5, 0.15625, ((0, 4), (1, 2)))
    wk = scatter_about(streams_of[3], (D, D), D ** -0.5, 0.15625, ((0, 4), (1, 2)))
    wv = scatter_about(streams_of[4], (D, D), D ** -0.5, 0.15625, ((0, 4), (1, 2)))
    wo = scatter_about(streams_of[5], (D, D), (D // 32) ** -0.5, 0.875, ((0, 2), (1, 4)))
    w_gate = scatter_about(streams_of[6], (D, FF), D ** -0.5, 0.15625, ((0, 4), (1, 2)))
    w_up = scatter_about(streams_of[7], (D, FF), D ** -0.5, 0.15625, ((0, 4), (1, 2)))
    w_down = scatter_about(streams_of[8], (FF, D), FF ** -0.5, 0.09375, ((0, 2), (1, 4)))
    gain_attn = jnp.clip(1.0 + 0.18 * jax.random.normal(streams_of[9], (D,), jnp.float32), 0.099609375, 1.8984375).astype(jnp.bfloat16)
    gain_ffn = jnp.clip(1.0 + 0.18 * jax.random.normal(streams_of[10], (D,), jnp.float32), 0.099609375, 1.8984375).astype(jnp.bfloat16)
    cotangent = scatter_about(streams_of[11], (SEQS, LEN, D), 1.0, 6.0, ((0, 4), (1, 8)))
    return dict(tokens=tokens, segment_ids=segment_ids, wq=wq, wk=wk, wv=wv, wo=wo, w_gate=w_gate, w_up=w_up, w_down=w_down, gain_attn=gain_attn, gain_ffn=gain_ffn, cotangent=cotangent)


epsilon = 1e-05
masked_score = -1e+30

@jax.custom_vjp
def low(v):
    return lax.optimization_barrier(v.astype(jnp.bfloat16)).astype(jnp.float32)

@jax.custom_vjp
def low_back(v):
    return v

def low_keep(v):
    return (low(v), None)

def low_pass(kept, grad):
    return (grad,)

def back_keep(v):
    return (v, None)

def back_low(kept, grad):
    return (low(grad),)
low.defvjp(low_keep, low_pass)
low_back.defvjp(back_keep, back_low)

def matmul(left, right):
    return jnp.dot(left, right, precision=lax.Precision.HIGHEST, preferred_element_type=jnp.float32)

def normalize(values, gain):
    inverse = lax.rsqrt(lax.optimization_barrier(jnp.mean(values * values, axis=-1, keepdims=True)) + epsilon)
    return values * inverse * gain

def rotate(values, cos_rows, sin_rows):
    half_dim = HEAD_DIM // 2
    first_half = values[..., :half_dim]
    second_half = values[..., half_dim:]
    cos_part = cos_rows[:, None, :]
    sin_part = sin_rows[:, None, :]
    return jnp.concatenate([first_half * cos_part - second_half * sin_part, second_half * cos_part + first_half * sin_part], axis=-1)

def one_sequence(params, inputs, segments):
    wq, wk, wv, wo, w_gate, w_up, w_down, gain_attn, gain_ffn = params
    where_at = jnp.arange(LEN, dtype=jnp.float32)
    inv_freq = 10000.0 ** (-jnp.arange(HEAD_DIM // 2, dtype=jnp.float32) * 2.0 / HEAD_DIM)
    angles = where_at[:, None] * inv_freq[None, :]
    cos_rows = jnp.cos(angles)
    sin_rows = jnp.sin(angles)
    normalized_input = low(normalize(inputs, gain_attn))
    queries = low(rotate(low_back(matmul(normalized_input, wq)).reshape(LEN, HEADS, HEAD_DIM), cos_rows, sin_rows))
    keys_rot = low(rotate(low_back(matmul(normalized_input, wk)).reshape(LEN, HEADS, HEAD_DIM), cos_rows, sin_rows))
    values_h = low(low_back(matmul(normalized_input, wv))).reshape(LEN, HEADS, HEAD_DIM)
    scores = jnp.einsum('qhd,khd->hqk', queries, keys_rot, precision=lax.Precision.HIGHEST) * HEAD_DIM ** (-0.5)
    scores = low_back(scores)
    positions = jnp.arange(LEN, dtype=jnp.int32)
    allowed = (segments[:, None] == segments[None, :]) & (positions[None, :] <= positions[:, None])
    scores = jnp.where(allowed[None], scores, masked_score)
    soft_weights = jax.nn.softmax(scores, axis=-1)
    attended = jnp.einsum('hqk,khd->qhd', low(soft_weights), values_h, precision=lax.Precision.HIGHEST).reshape(LEN, D)
    attn_out = low_back(matmul(low(low_back(attended)), wo))
    residual = inputs + attn_out
    normalized_second = low(normalize(residual, gain_ffn))
    gate_pre = low_back(matmul(normalized_second, w_gate))
    up_pre = low_back(matmul(normalized_second, w_up))
    hidden_state = low(jax.nn.silu(gate_pre) * up_pre)
    return residual + low_back(matmul(hidden_state, w_down))

def reference(tokens, segment_ids, wq, wk, wv, wo, w_gate, w_up, w_down, gain_attn, gain_ffn, cotangent):
    params = (wq.astype(jnp.float32), wk.astype(jnp.float32), wv.astype(jnp.float32), wo.astype(jnp.float32), w_gate.astype(jnp.float32), w_up.astype(jnp.float32), w_down.astype(jnp.float32), gain_attn.astype(jnp.float32), gain_ffn.astype(jnp.float32))
    inputs = tokens.astype(jnp.float32)
    per_sequence = jax.checkpoint(one_sequence)

    def forward(values, weights):
        return lax.map(lambda member: per_sequence(weights, member[0], member[1]), (values, segment_ids))
    result, pullback = jax.vjp(forward, inputs, params)
    grad_in, grad_list = pullback(cotangent.astype(jnp.float32))
    return (result.astype(jnp.bfloat16), grad_in, grad_list[0], grad_list[1], grad_list[2], grad_list[3], grad_list[4], grad_list[5], grad_list[6], grad_list[7], grad_list[8])
```

```python
import jax
import jax.numpy as jnp
from jax import lax
from jax.sharding import PartitionSpec as P

HEAD_DIM = 64
EPSILON = 1e-05
MASKED = -1e30
BF16 = jnp.bfloat16
F32 = jnp.float32


def pull_fsdp(values, step):
    count = lax.axis_size("fsdp")
    return lax.ppermute(values, "fsdp", [(i, (i - step) % count) for i in range(count)])


def push_fsdp(values, step):
    count = lax.axis_size("fsdp")
    return lax.ppermute(values, "fsdp", [(i, (i + step) % count) for i in range(count)])


def swap_chip(values):
    return lax.ppermute(values, "ctx", [(i, i ^ 2) for i in range(lax.axis_size("ctx"))])


def swap_core(values):
    return lax.ppermute(values, "ctx", [(i, i ^ 1) for i in range(lax.axis_size("ctx"))])


def widen_rows(values):
    if lax.axis_size("tp") != 2:
        return lax.all_gather(values, "tp", axis=0, tiled=True)
    other = lax.ppermute(values, "tp", [(0, 1), (1, 0)])
    first = lax.axis_index("tp") == 0
    return jnp.concatenate([jnp.where(first, values, other), jnp.where(first, other, values)], axis=0)


def narrow_rows(values):
    count = lax.axis_size("tp")
    if count != 2:
        return lax.psum_scatter(values.astype(BF16), "tp", scatter_dimension=0, tiled=True).astype(F32)
    rows = values.shape[0] // count
    me = lax.axis_index("tp")
    sent = lax.dynamic_slice_in_dim(values, (1 - me) * rows, rows, 0).astype(BF16)
    kept = lax.dynamic_slice_in_dim(values, me * rows, rows, 0)
    return kept + lax.ppermute(sent, "tp", [(0, 1), (1, 0)]).astype(F32)


def roll_columns(values, blocks):
    width = values.shape[-1]
    block = width // lax.axis_size("fsdp")
    twice = jnp.concatenate([values, values], axis=-1)
    return lax.dynamic_slice_in_dim(twice, blocks * block, width, values.ndim - 1)


def to_relative(values):
    return roll_columns(values, lax.axis_index("fsdp"))


def to_natural(values):
    count = lax.axis_size("fsdp")
    return roll_columns(values, (count - lax.axis_index("fsdp")) % count)


def after(values, earlier):
    return lax.optimization_barrier((values, earlier))[0]


def quarter(values, index, axis):
    size = values.shape[axis] // 4
    return lax.dynamic_slice_in_dim(values, index * size, size, axis)


def gather_quarters(shard, fsdp_axis, quarter_axis, earlier=None):
    count = lax.axis_size("fsdp")
    place = lax.axis_index("ctx")
    own = quarter(shard, place, quarter_axis)
    if earlier is not None:
        own = after(own, earlier)
    parts = [pull_fsdp(own, step) for step in range(1, count)]
    mine = jnp.concatenate([own] + parts, axis=fsdp_axis)
    crossed = swap_chip(jnp.concatenate(parts, axis=fsdp_axis))
    across = jnp.concatenate([quarter(shard, place ^ 2, quarter_axis), crossed], axis=fsdp_axis)
    return [mine, swap_core(mine), across, swap_core(across)], parts[-1]


def gather_plain(shard, fsdp_axis, earlier=None):
    count = lax.axis_size("fsdp")
    if earlier is not None:
        shard = after(shard, earlier)
    parts = [pull_fsdp(shard, step) for step in range(1, count)]
    return jnp.concatenate([shard] + parts, axis=fsdp_axis), parts[-1]


def add_halves(left, right):
    return (left.astype(F32) + right.astype(F32)).astype(BF16)


def fsdp_total(values, fsdp_axis):
    count = lax.axis_size("fsdp")
    pieces = jnp.split(values, count, axis=fsdp_axis)
    total = pieces[0].astype(F32)
    for step in range(1, count):
        total = total + push_fsdp(pieces[step], step).astype(F32)
    return total


def reduce_quarters(blocks, fsdp_axis, quarter_axis):
    place = lax.axis_index("ctx")
    came = swap_core(jnp.stack([blocks[1], blocks[3]]))
    near = add_halves(blocks[0], came[0])
    far = add_halves(blocks[2], came[1])
    mine = add_halves(near, swap_chip(far))
    own = fsdp_total(mine, fsdp_axis).astype(BF16)
    crossed = swap_chip(own)
    core_own, core_crossed = swap_core(own), swap_core(crossed)
    odd_core, odd_chip = place % 2 == 1, place >= 2
    pick = jnp.where
    a0, a1 = pick(odd_core, core_own, own), pick(odd_core, own, core_own)
    b0, b1 = pick(odd_core, core_crossed, crossed), pick(odd_core, crossed, core_crossed)
    order = [pick(odd_chip, b0, a0), pick(odd_chip, b1, a1), pick(odd_chip, a0, b0), pick(odd_chip, a1, b1)]
    return jnp.concatenate(order, axis=quarter_axis).astype(F32)


def reduce_plain(grad, fsdp_axis):
    return lax.psum(fsdp_total(grad, fsdp_axis).astype(BF16), "ctx").astype(F32)


def fetch_window(rows):
    count = lax.axis_size("ctx")
    even = lax.axis_index("ctx") % 2 == 0
    own = widen_rows(rows)
    far = widen_rows(lax.ppermute(rows, "ctx", [(i, i + 2) for i in range(count - 2)]))
    near = swap_core(jnp.where(even, own, far))
    return jnp.concatenate([far, near, own], axis=0)


def return_window(far, near, own):
    count = lax.axis_size("ctx")
    even = lax.axis_index("ctx") % 2 == 0
    came = swap_core(near.astype(BF16)).astype(F32)
    own = narrow_rows(own + jnp.where(even, came, 0.0))
    far = narrow_rows(far + jnp.where(even, 0.0, came)).astype(BF16)
    return own + lax.ppermute(far, "ctx", [(i, i - 2) for i in range(2, count)]).astype(F32)


def fetch_ids(ids):
    count = lax.axis_size("ctx")
    even = lax.axis_index("ctx") % 2 == 0
    far = lax.ppermute(ids, "ctx", [(i, i + 2) for i in range(count - 2)])
    return jnp.concatenate([far, swap_core(jnp.where(even, ids, far)), ids])


def rope_tables(offset, row_count, half_dim):
    where_at = (offset + jnp.arange(row_count, dtype=jnp.int32)).astype(F32)
    inv_freq = 10000.0 ** (-jnp.arange(half_dim, dtype=F32) * 2.0 / (2 * half_dim))
    angles = where_at[:, None] * inv_freq[None, :]
    return jnp.cos(angles), jnp.sin(angles)


def rotate(values, cos_rows, sin_rows, direction):
    half_dim = values.shape[-1] // 2
    first_half = values[..., :half_dim]
    second_half = values[..., half_dim:]
    cos_part = cos_rows[:, None, :]
    sin_part = sin_rows[:, None, :] * direction
    return jnp.concatenate(
        [
            first_half * cos_part - second_half * sin_part,
            second_half * cos_part + first_half * sin_part,
        ],
        axis=-1,
    )


def normalize_back(values, inverse, gain, grad_rows):
    scaled = grad_rows * gain
    return inverse * scaled - values * inverse**3 * jnp.mean(scaled * values, axis=-1, keepdims=True)


def dot(left, right):
    return jnp.dot(left, right, preferred_element_type=F32)


def dot_nt(left, right):
    return lax.dot_general(left, right, (((1,), (1,)), ((), ())), preferred_element_type=F32)


def dot_tn(left, right):
    return lax.dot_general(left, right, (((0,), (0,)), ((), ())), preferred_element_type=F32)


def shards(tokens, segment_ids, wq, wk, wv, wo, w_gate, w_up, w_down, gain_attn, gain_ffn, cotangent):
    tokens, cotangent, segment_ids = tokens[0], cotangent[0], segment_ids[0]
    ctx_rows = segment_ids.shape[0]
    head_count = wq.shape[1] // HEAD_DIM
    row_width = wq.shape[1]
    scale = HEAD_DIM ** (-0.5)
    by_heads = head_count % 4 == 0
    first_query = lax.axis_index("ctx") * ctx_rows
    cos_rows, sin_rows = rope_tables(first_query - 2 * ctx_rows, 3 * ctx_rows, HEAD_DIM // 2)

    qkv = jnp.stack([wq, wk, wv])
    if by_heads:
        qkv_parts, mark = gather_quarters(qkv, 1, 2)
        qkv_whole = jnp.concatenate(qkv_parts, axis=2)
        out_parts, mark = gather_quarters(wo, 1, 0, mark)
        out_whole = jnp.concatenate(out_parts, axis=0)
    else:
        qkv_whole, mark = gather_plain(qkv, 1)
        out_whole, mark = gather_plain(wo, 1, mark)
    wide_parts, mark = gather_quarters(jnp.stack([w_gate, w_up]), 1, 2, mark)
    wide_whole = jnp.concatenate(wide_parts, axis=2)
    gate_whole, up_whole = wide_whole[0], wide_whole[1]
    down_parts, mark = gather_quarters(w_down, 1, 0, mark)
    down_whole = jnp.concatenate(down_parts, axis=0)
    gains, _ = gather_plain(jnp.stack([gain_attn, gain_ffn]), 1)
    gain_one, gain_two = gains[0].astype(F32), gains[1].astype(F32)

    inputs = to_relative(tokens).astype(F32)
    dy_rows = to_relative(cotangent)
    inv_one = lax.rsqrt(jnp.mean(inputs * inputs, axis=-1, keepdims=True) + EPSILON)
    normed_window = fetch_window((inputs * inv_one * gain_one).astype(BF16))
    normed = normed_window[2 * ctx_rows :]
    dy_wide = widen_rows(dy_rows)

    def heads(values):
        return values.reshape(values.shape[0], head_count, HEAD_DIM)

    cos_own, sin_own = cos_rows[2 * ctx_rows :], sin_rows[2 * ctx_rows :]
    queries = rotate(heads(dot(normed, qkv_whole[0])), cos_own, sin_own, 1.0).astype(BF16)
    keys = rotate(heads(dot(normed_window, qkv_whole[1])), cos_rows, sin_rows, 1.0).astype(BF16)
    values = heads(dot(normed_window, qkv_whole[2]).astype(BF16))
    segment_window = fetch_ids(segment_ids)
    pos_query = first_query + jnp.arange(ctx_rows, dtype=jnp.int32)
    pos_key = first_query - 2 * ctx_rows + jnp.arange(3 * ctx_rows, dtype=jnp.int32)
    allowed = (
        (segment_ids[:, None] == segment_window[None, :])
        & (pos_key[None, :] <= pos_query[:, None])
        & (pos_key[None, :] >= 0)
    )[None]
    scores = jnp.einsum("qhd,khd->hqk", queries, keys, preferred_element_type=F32) * scale
    scores = jnp.where(allowed, scores, MASKED)
    top = jnp.max(scores, axis=-1, keepdims=True)
    powers = jnp.where(allowed, jnp.exp(scores - top), 0.0)
    sums = jnp.sum(powers, axis=-1, keepdims=True)
    weighted = jnp.einsum("hqk,khd->hqd", powers.astype(BF16), values, preferred_element_type=F32)
    attended = jnp.transpose(weighted / sums, (1, 0, 2))
    log_sums = top + jnp.log(sums)
    attended_low = attended.astype(BF16).reshape(ctx_rows, row_width)
    residual = inputs + narrow_rows(dot(attended_low, out_whole))

    inv_two = lax.rsqrt(jnp.mean(residual * residual, axis=-1, keepdims=True) + EPSILON)
    normed_two = widen_rows((residual * inv_two * gain_two).astype(BF16))
    gate = dot(normed_two, gate_whole)
    up = dot(normed_two, up_whole)
    sig = jax.nn.sigmoid(gate)
    silu = gate * sig
    hidden = (silu * up).astype(BF16)
    hidden_grad = dot_nt(dy_wide, down_whole)
    gate_grad = (hidden_grad * up * sig * (1.0 + gate * (1.0 - sig))).astype(BF16)
    up_grad = (hidden_grad * silu).astype(BF16)
    normed_two_grad = narrow_rows(dot_nt(gate_grad, gate_whole) + dot_nt(up_grad, up_whole))
    layer_out = residual + narrow_rows(dot(hidden, down_whole))
    down_grad = dot_tn(hidden, dy_wide).astype(BF16)
    wide_grad = jnp.stack(
        [dot_tn(normed_two, gate_grad).astype(BF16), dot_tn(normed_two, up_grad).astype(BF16)]
    )
    down_total = reduce_quarters(jnp.split(down_grad, 4, axis=0), 1, 0)
    wide_total = reduce_quarters(jnp.split(wide_grad, 4, axis=2), 1, 2)
    gain_two_grad = jnp.sum(normed_two_grad * residual * inv_two, axis=0)
    resid_grad = dy_rows.astype(F32) + normalize_back(residual, inv_two, gain_two, normed_two_grad)

    attention_grad = widen_rows(resid_grad.astype(BF16))
    out_weight_grad = dot_tn(attended_low, attention_grad).astype(BF16)
    out_grad = heads(dot_nt(attention_grad, out_whole).astype(BF16))
    delta = jnp.sum(out_grad.astype(F32) * attended, axis=-1)
    soft = jnp.where(allowed, jnp.exp(scores - log_sums), 0.0)
    prob_grad = jnp.einsum("qhd,khd->hqk", out_grad, values, preferred_element_type=F32)
    score_grad = (soft * (prob_grad - jnp.transpose(delta)[:, :, None])).astype(BF16)
    query_grad = jnp.einsum("hqk,khd->qhd", score_grad, keys, preferred_element_type=F32) * scale
    key_add = jnp.einsum("hqk,qhd->khd", score_grad, queries, preferred_element_type=F32) * scale
    value_add = jnp.einsum("hqk,qhd->khd", soft.astype(BF16), out_grad, preferred_element_type=F32)
    query_low = rotate(query_grad, cos_own, sin_own, -1.0).astype(BF16).reshape(ctx_rows, row_width)
    key_low = rotate(key_add, cos_rows, sin_rows, -1.0).astype(BF16).reshape(3 * ctx_rows, row_width)
    value_low = value_add.astype(BF16).reshape(3 * ctx_rows, row_width)
    qkv_grad = jnp.stack(
        [
            dot_tn(normed, query_low).astype(BF16),
            dot_tn(normed_window, key_low).astype(BF16),
            dot_tn(normed_window, value_low).astype(BF16),
        ]
    )
    if by_heads:
        out_total = reduce_quarters(jnp.split(out_weight_grad, 4, axis=0), 1, 0)
        qkv_total = reduce_quarters(jnp.split(qkv_grad, 4, axis=2), 1, 2)
    else:
        out_total = reduce_plain(out_weight_grad, 1)
        qkv_total = reduce_plain(qkv_grad, 1)
    normed_parts = dot_nt(key_low, qkv_whole[1]) + dot_nt(value_low, qkv_whole[2])
    far, near, own = (normed_parts[i * ctx_rows : (i + 1) * ctx_rows] for i in range(3))
    normed_grad = return_window(far, near, own + dot_nt(query_low, qkv_whole[0]))
    gain_one_grad = jnp.sum(normed_grad * inputs * inv_one, axis=0)
    grad_input = resid_grad + normalize_back(inputs, inv_one, gain_one, normed_grad)

    gain_grads = lax.psum(to_natural(jnp.stack([gain_one_grad, gain_two_grad])), ("fsdp", "ctx", "tp"))
    gain_rows = gain_attn.shape[0]
    gain_own = lax.dynamic_slice_in_dim(gain_grads, lax.axis_index("fsdp") * gain_rows, gain_rows, 1)
    return (
        to_natural(layer_out.astype(BF16))[None],
        to_natural(grad_input)[None],
        qkv_total[0],
        qkv_total[1],
        qkv_total[2],
        out_total,
        wide_total[0],
        wide_total[1],
        down_total,
        gain_own[0],
        gain_own[1],
    )


def solution(mesh):
    rows = P("fsdp", ("ctx", "tp"), None)
    into, outof, gain = P("fsdp", "tp"), P("tp", "fsdp"), P("fsdp")
    return jax.shard_map(
        shards,
        mesh=mesh,
        in_specs=(rows, P("fsdp", "ctx"), into, into, into, outof, into, into, outof, gain, gain, rows),
        out_specs=(rows, rows, into, into, into, outof, into, into, outof, gain, gain),
        check_vma=False,
    )
```

```python
import functools

import jax
import jax.numpy as jnp
from jax import lax
from jax.experimental import pallas as pl
from jax.experimental.pallas import tpu as pltpu
from jax.sharding import PartitionSpec as P

HEAD_DIM = 64
EPSILON = 1e-05
MASKED = -1e30
BF16 = jnp.bfloat16
F32 = jnp.float32
TILE = 256
LANES = 128
VMEM_BYTES = 60 * 1024 * 1024


def dot(left, right):
    return jnp.dot(left, right, preferred_element_type=F32)


def dot_nt(left, right):
    return lax.dot_general(left, right, (((1,), (1,)), ((), ())), preferred_element_type=F32)


def dot_tn(left, right):
    return lax.dot_general(left, right, (((0,), (0,)), ((), ())), preferred_element_type=F32)


def swap_chip(values):
    return lax.ppermute(values, "ctx", [(i, i ^ 2) for i in range(lax.axis_size("ctx"))])


def swap_core(values):
    return lax.ppermute(values, "ctx", [(i, i ^ 1) for i in range(lax.axis_size("ctx"))])


def to_later_chip(values):
    return lax.ppermute(values, "ctx", [(i, i + 2) for i in range(lax.axis_size("ctx") - 2)])


def to_earlier_chip(values):
    return lax.ppermute(values, "ctx", [(i, i - 2) for i in range(2, lax.axis_size("ctx"))])


def swap_tp(values):
    return lax.ppermute(values, "tp", [(0, 1), (1, 0)])


def in_order(mine, other, mine_first):
    return [jnp.where(mine_first, mine, other), jnp.where(mine_first, other, mine)]


def widen_chip(rows):
    if lax.axis_size("tp") == 2:
        rows = jnp.concatenate(in_order(rows, swap_tp(rows), lax.axis_index("tp") == 0), axis=0)
    else:
        rows = lax.all_gather(rows, "tp", axis=0, tiled=True)
    return in_order(rows, swap_core(rows), lax.axis_index("ctx") % 2 == 0)


def narrow_chip(partial):
    half = partial.shape[0] // 2
    core = lax.axis_index("ctx") % 2
    sent = lax.dynamic_slice_in_dim(partial, (1 - core) * half, half, 0)
    kept = lax.dynamic_slice_in_dim(partial, core * half, half, 0)
    pair = kept.astype(F32) + swap_core(sent.astype(BF16)).astype(F32)
    if lax.axis_size("tp") != 2:
        return lax.psum_scatter(pair.astype(BF16), "tp", scatter_dimension=0, tiled=True).astype(F32)
    rows = half // 2
    me = lax.axis_index("tp")
    sent = lax.dynamic_slice_in_dim(pair, (1 - me) * rows, rows, 0).astype(BF16)
    kept = lax.dynamic_slice_in_dim(pair, me * rows, rows, 0)
    return kept + swap_tp(sent).astype(F32)


def take_quarter(values, index, axis):
    size = values.shape[axis] // 4
    return lax.dynamic_slice_in_dim(values, index * size, size, axis)


def all_quarters(own):
    place = lax.axis_index("ctx")
    across = swap_chip(own)
    came = swap_core(jnp.stack([own, across]))
    low, high = in_order(jnp.stack([own, across]), came, place % 2 == 0)
    first = place < 2
    pick = jnp.where
    return [pick(first, low[0], low[1]), pick(first, high[0], high[1]), pick(first, low[1], low[0]), pick(first, high[1], high[0])]


def scatter_fsdp(values):
    return lax.psum_scatter(values, "fsdp", scatter_dimension=0, tiled=True)


def add_low(left, right):
    return (left.astype(F32) + right.astype(F32)).astype(BF16)


def call(kernel, name, flops, moved, **rest):
    return pl.pallas_call(
        kernel,
        name=name,
        cost_estimate=pl.CostEstimate(flops=flops, bytes_accessed=moved, transcendentals=0),
        compiler_params=pltpu.CompilerParams(vmem_limit_bytes=VMEM_BYTES),
        **rest,
    )


def whole():
    return pl.BlockSpec(memory_space=pltpu.VMEM)


def turn(values, cos, sin, direction):
    lane = lax.broadcasted_iota(jnp.int32, (1, LANES), 1)
    partner = jnp.where((lane // 32) % 2 == 0, pltpu.roll(values, 96, 1) * -direction, pltpu.roll(values, 32, 1) * direction)
    return values * cos + partner * sin


def project_kernel(first_query, rows_ref, weight_ref, cos_ref, sin_ref, q_ref, k_ref, v_ref):
    rows = rows_ref[...]
    cos, sin = cos_ref[...], sin_ref[...]
    width = q_ref.shape[1]

    def rotated(values, out_ref):
        for c in range(0, width, LANES):
            out_ref[:, c : c + LANES] = turn(values[:, c : c + LANES], cos, sin, 1.0).astype(BF16)

    rotated(dot_nt(rows, weight_ref[1]), k_ref)
    v_ref[...] = dot_nt(rows, weight_ref[2]).astype(BF16)

    @pl.when(pl.program_id(0) >= first_query)
    def _():
        rotated(dot_nt(rows, weight_ref[0]), q_ref)


def project(rows, weights, cos, sin, first_row):
    count, depth = rows.shape
    width = weights.shape[1]
    out = jax.ShapeDtypeStruct((count, width), BF16)
    tile = pl.BlockSpec((TILE, width), lambda i: (i, 0))
    return call(
        functools.partial(project_kernel, first_row // TILE),
        "project",
        count * depth * width * 5,
        count * depth * 2,
        grid=(count // TILE,),
        out_shape=(out, out, out),
        in_specs=[
            pl.BlockSpec((TILE, depth), lambda i: (i, 0)),
            pl.BlockSpec(weights.shape, lambda i: (0, 0, 0)),
            pl.BlockSpec((TILE, LANES), lambda i: (i, 0)),
            pl.BlockSpec((TILE, LANES), lambda i: (i, 0)),
        ],
        out_specs=[tile, tile, tile],
    )(rows, weights, cos, sin)


def lane_half(head):
    return (lax.broadcasted_iota(jnp.int32, (1, LANES), 1) // HEAD_DIM) == head % 2


def forward_kernel(rows, base, bounds, q_ref, k_ref, v_ref, start_ref, o_ref, lse_ref, q_buf, s_buf, top_buf, sum_buf, acc_buf):
    heads = q_buf.shape[0]
    zero = jnp.zeros((), BF16)
    for t in range(-(-rows // TILE)):
        low, high = bounds[0, t], bounds[1, t]
        n = min(TILE, rows - t * TILE)
        span = slice(t * TILE, (t + 1) * TILE)
        start = start_ref[:, span]
        row = base + t * TILE + lax.broadcasted_iota(jnp.int32, (1, TILE), 1)
        for h in range(heads):
            c = (h // 2) * LANES
            scaled = (q_ref[base + t * TILE : base + t * TILE + n, c : c + LANES].astype(F32) * HEAD_DIM**-0.5).astype(BF16)
            q_buf[h, :n, :] = jnp.where(lane_half(h), scaled, zero)
            if n < TILE:
                q_buf[h, n:, :] = jnp.zeros((TILE - n, LANES), BF16)
        top_buf[...] = jnp.full_like(top_buf, MASKED)
        sum_buf[...] = jnp.zeros_like(sum_buf)
        acc_buf[...] = jnp.zeros_like(acc_buf)

        @pl.loop(low, high)
        def _(i):
            at = pl.multiple_of(i * TILE, TILE)
            place = at + lax.broadcasted_iota(jnp.int32, (TILE, TILE), 0)
            allowed = (place >= start) & (place <= row)
            for h in range(heads):
                c = (h // 2) * LANES
                s = jnp.where(allowed, dot_nt(k_ref[pl.ds(at, TILE), c : c + LANES], q_buf[h]), MASKED)
                s_buf[h, pl.ds(at, TILE), :] = s
                top_buf[h] = jnp.maximum(top_buf[h], jnp.max(s.reshape(TILE // 8, 8, TILE), axis=0))

        tops = [jnp.max(top_buf[h], axis=0, keepdims=True) for h in range(heads)]

        @pl.loop(low, high)
        def _(i):
            at = pl.multiple_of(i * TILE, TILE)
            for h in range(heads):
                c = (h // 2) * LANES
                p = jnp.exp(s_buf[h, pl.ds(at, TILE), :] - tops[h])
                sum_buf[h] += jnp.sum(p.reshape(TILE // 8, 8, TILE), axis=0)
                both = dot_tn(v_ref[pl.ds(at, TILE), c : c + LANES], p.astype(BF16))
                acc_buf[h] += both[HEAD_DIM * (h % 2) : HEAD_DIM * (h % 2) + HEAD_DIM]

        for h in range(heads):
            total = jnp.sum(sum_buf[h], axis=0, keepdims=True)
            lse_ref[h : h + 1, span] = tops[h] + jnp.log(total)
            acc_buf[h] = acc_buf[h] / total
        for pair in range(heads // 2):
            o = jnp.transpose(jnp.concatenate([acc_buf[2 * pair], acc_buf[2 * pair + 1]], axis=0))
            o_ref[t * TILE : t * TILE + n, pair * LANES : (pair + 1) * LANES] = o[:n].astype(BF16)


def attend(bounds, q, k, v, start, rows, base):
    keys, width = k.shape
    heads = width // HEAD_DIM
    padded = -(-rows // TILE) * TILE
    return call(
        functools.partial(forward_kernel, rows, base),
        "attend",
        rows * rows * width * 8,
        keys * width * 8,
        out_shape=(jax.ShapeDtypeStruct((rows, width), BF16), jax.ShapeDtypeStruct((heads, padded), F32)),
        in_specs=[pl.BlockSpec(memory_space=pltpu.SMEM)] + [whole()] * 4,
        out_specs=[whole(), whole()],
        scratch_shapes=[
            pltpu.VMEM((heads, TILE, LANES), BF16),
            pltpu.VMEM((heads, keys, TILE), F32),
            pltpu.VMEM((heads, 8, TILE), F32),
            pltpu.VMEM((heads, 8, TILE), F32),
            pltpu.VMEM((heads, HEAD_DIM, TILE), F32),
        ],
    )(bounds, q, k, v, start)


def backward_kernel(
    rows, base, bounds, q_ref, k_ref, v_ref, o_ref, g_ref, lse_ref, start_ref, cos_ref, sin_ref,
    dq_ref, dk_ref, dv_ref, q_buf, g_buf, d_buf, dq_acc, dk_acc, dv_acc,
):
    heads = q_buf.shape[0]
    zero = jnp.zeros((), BF16)
    scale = HEAD_DIM**-0.5
    dk_acc[...] = jnp.zeros_like(dk_acc)
    dv_acc[...] = jnp.zeros_like(dv_acc)
    for t in range(-(-rows // TILE)):
        low, high = bounds[0, t], bounds[1, t]
        n = min(TILE, rows - t * TILE)
        span = slice(t * TILE, (t + 1) * TILE)
        here = slice(t * TILE, t * TILE + n)
        window = slice(base + t * TILE, base + t * TILE + n)
        start = start_ref[:, span]
        row = base + t * TILE + lax.broadcasted_iota(jnp.int32, (1, TILE), 1)
        for pair in range(heads // 2):
            c = pair * LANES
            scaled = (q_ref[window, c : c + LANES].astype(F32) * scale).astype(BF16)
            grad = g_ref[here, c : c + LANES]
            product = grad.astype(F32) * o_ref[here, c : c + LANES].astype(F32)
            if n < TILE:
                product = jnp.concatenate([product, jnp.zeros((TILE - n, LANES), F32)], axis=0)
            product = jnp.transpose(product)
            for h in (2 * pair, 2 * pair + 1):
                q_buf[h, :n, :] = jnp.where(lane_half(h), scaled, zero)
                g_buf[h, :n, :] = jnp.where(lane_half(h), grad, zero)
                if n < TILE:
                    q_buf[h, n:, :] = jnp.zeros((TILE - n, LANES), BF16)
                    g_buf[h, n:, :] = jnp.zeros((TILE - n, LANES), BF16)
                d_buf[h : h + 1, :] = jnp.sum(product[HEAD_DIM * (h % 2) : HEAD_DIM * (h % 2) + HEAD_DIM], axis=0, keepdims=True)
        dq_acc[...] = jnp.zeros_like(dq_acc)

        @pl.loop(low, high)
        def _(i):
            at = pl.multiple_of(i * TILE, TILE)
            place = at + lax.broadcasted_iota(jnp.int32, (TILE, TILE), 0)
            allowed = (place >= start) & (place <= row)
            for pair in range(heads // 2):
                c = pair * LANES
                k = k_ref[pl.ds(at, TILE), c : c + LANES]
                v = v_ref[pl.ds(at, TILE), c : c + LANES]
                dq = dk = dv = 0.0
                for h in (2 * pair, 2 * pair + 1):
                    p = jnp.where(allowed, jnp.exp(dot_nt(k, q_buf[h]) - lse_ref[h : h + 1, span]), 0.0)
                    ds = (p * (dot_nt(v, g_buf[h]) - d_buf[h : h + 1, :])).astype(BF16)
                    dv = dv + dot(p.astype(BF16), g_buf[h])
                    dk = dk + dot(ds, q_buf[h])
                    dq = dq + dot_tn(ds, jnp.where(lane_half(h), k, zero))
                dk_acc[pl.ds(at, TILE), c : c + LANES] += dk
                dv_acc[pl.ds(at, TILE), c : c + LANES] += dv
                dq_acc[:, c : c + LANES] += dq

        for c in range(0, heads * HEAD_DIM, LANES):
            dq = dq_acc[:n, c : c + LANES] * scale
            dq_ref[here, c : c + LANES] = turn(dq, cos_ref[window, :], sin_ref[window, :], -1.0).astype(BF16)
    for c in range(0, heads * HEAD_DIM, LANES):
        dk_ref[:, c : c + LANES] = turn(dk_acc[:, c : c + LANES], cos_ref[...], sin_ref[...], -1.0).astype(BF16)
    dv_ref[...] = dv_acc[...].astype(BF16)


def attend_back(bounds, q, k, v, o, grad, lse, start, cos, sin, rows, base):
    keys, width = k.shape
    heads = width // HEAD_DIM
    wide = jax.ShapeDtypeStruct((keys, width), BF16)
    return call(
        functools.partial(backward_kernel, rows, base),
        "attend_back",
        rows * rows * width * 20,
        keys * width * 16,
        out_shape=(jax.ShapeDtypeStruct((rows, width), BF16), wide, wide),
        in_specs=[pl.BlockSpec(memory_space=pltpu.SMEM)] + [whole()] * 9,
        out_specs=[whole()] * 3,
        scratch_shapes=[
            pltpu.VMEM((heads, TILE, LANES), BF16),
            pltpu.VMEM((heads, TILE, LANES), BF16),
            pltpu.VMEM((heads, TILE), F32),
            pltpu.VMEM((TILE, width), F32),
            pltpu.VMEM((keys, width), F32),
            pltpu.VMEM((keys, width), F32),
        ],
    )(bounds, q, k, v, o, grad, lse, start, cos, sin)


def hidden_kernel(row_tile, own_steps, n_ref, dy_ref, *refs):
    weights, (hidden_ref, gate_ref, up_ref, back_ref, acc) = refs[:6], refs[6:]
    step = pl.program_id(0)

    @pl.when(step == 0)
    def _():
        acc[...] = jnp.zeros_like(acc)

    def tile(gate_w, up_w, down_w):
        for r in range(0, n_ref.shape[0], row_tile):
            rows = slice(r, r + row_tile)
            gate = dot(n_ref[rows, :], gate_w[...])
            up = dot(n_ref[rows, :], up_w[...])
            grad = dot(dy_ref[rows, :], down_w[...])
            sig = 1.0 / (1.0 + jnp.exp(-gate))
            silu = gate * sig
            hidden_ref[rows, :] = (silu * up).astype(BF16)
            gate_grad = (grad * up * sig * (1.0 + gate * (1.0 - sig))).astype(BF16)
            up_grad = (grad * silu).astype(BF16)
            gate_ref[rows, :] = gate_grad
            up_ref[rows, :] = up_grad
            acc[rows, :] += dot_nt(gate_grad, gate_w[...]) + dot_nt(up_grad, up_w[...])

    @pl.when(step < own_steps)
    def _():
        tile(*weights[:3])

    @pl.when(step >= own_steps)
    def _():
        tile(*weights[3:])

    @pl.when(step == pl.num_programs(0) - 1)
    def _():
        back_ref[...] = acc[...].astype(BF16)


def feed(normed, dy, own, other):
    rows, depth = normed.shape
    units = own[0].shape[1]
    tile = min(TILE, units)
    steps = units // tile
    fixed = pl.BlockSpec((rows, depth), lambda i: (0, 0))
    first = pl.BlockSpec((depth, tile), lambda i: (0, jnp.minimum(i, steps - 1)))
    second = pl.BlockSpec((depth, tile), lambda i: (0, jnp.maximum(i - steps, 0)))
    out = pl.BlockSpec((rows, tile), lambda i: (0, i))
    wide = jax.ShapeDtypeStruct((rows, 2 * units), BF16)
    return call(
        functools.partial(hidden_kernel, rows // 4, steps),
        "feed",
        rows * depth * units * 20,
        depth * units * 12,
        grid=(2 * steps,),
        out_shape=(wide, wide, wide, jax.ShapeDtypeStruct((rows, depth), BF16)),
        in_specs=[fixed, fixed] + [first] * 3 + [second] * 3,
        out_specs=[out, out, out, fixed],
        scratch_shapes=[pltpu.VMEM((rows, depth), F32)],
    )(normed, dy, *own, *other)


def weights_kernel(n_ref, dy_ref, hidden_ref, gate_ref, up_ref, gate_out, up_out, down_out):
    gate_out[...] = dot_tn(n_ref[...], gate_ref[...]).astype(BF16)
    up_out[...] = dot_tn(n_ref[...], up_ref[...]).astype(BF16)
    down_out[...] = dot_tn(dy_ref[...], hidden_ref[...]).astype(BF16)


def feed_weights(normed, dy, hidden, gate_grad, up_grad, part):
    rows, depth = normed.shape
    units = hidden.shape[1] // 2
    tile = min(TILE, units)
    steps = units // tile
    fixed = pl.BlockSpec((rows, depth), lambda i: (0, 0))
    units_in = pl.BlockSpec((rows, tile), lambda i: (0, part * steps + i))
    out = pl.BlockSpec((depth, tile), lambda i: (0, i))
    shape = jax.ShapeDtypeStruct((depth, units), BF16)
    return call(
        weights_kernel,
        "feed_weights",
        rows * depth * units * 6,
        depth * units * 6,
        grid=(steps,),
        out_shape=(shape, shape, shape),
        in_specs=[fixed, fixed, units_in, units_in, units_in],
        out_specs=[out, out, out],
    )(normed, dy, hidden, gate_grad, up_grad)


def normalize_back(values, inverse, gain, grad_rows):
    scaled = grad_rows * gain
    return inverse * scaled - values * inverse**3 * jnp.mean(scaled * values, axis=-1, keepdims=True)


def inverse_rms(values):
    return lax.rsqrt(jnp.mean(values * values, axis=-1, keepdims=True) + EPSILON)


def shards(tokens, segment_ids, wq, wk, wv, wo, w_gate, w_up, w_down, gain_attn, gain_ffn, cotangent):
    tokens, cotangent, segment_ids = tokens[0], cotangent[0], segment_ids[0]
    fsdp = lax.axis_size("fsdp")
    place = lax.axis_index("ctx")
    chip, core = place // 2, place % 2
    rows = 2 * segment_ids.shape[0]
    real_width = wq.shape[1]
    shard_rows, depth = wq.shape[0], wq.shape[0] * fsdp
    width = -(-real_width // (4 * HEAD_DIM)) * 4 * HEAD_DIM
    part_width = width // 4
    keys = -(-2 * rows // TILE) * TILE

    def attention_piece():
        pad = ((0, 0), (0, width - real_width))
        pieces = [jnp.transpose(take_quarter(jnp.pad(w, pad), place, 1)) for w in (wq, wk, wv)]
        pieces.append(take_quarter(jnp.pad(wo, pad[::-1]), place, 0))
        return jnp.stack(pieces)

    attention_own = lax.all_gather(attention_piece(), "fsdp", axis=0, tiled=False)
    pieces = (take_quarter(w_gate, place, 1), take_quarter(w_up, place, 1), jnp.transpose(take_quarter(w_down, place, 0)))
    feed_own = [lax.all_gather(w, "fsdp", axis=0, tiled=True) for w in pieces]
    attention_both = jnp.stack([attention_own, swap_chip(attention_own)])
    attention_weights = jnp.transpose(attention_both, (2, 0, 3, 1, 4)).reshape(4, 2 * part_width, depth)
    feed_other = [swap_chip(w) for w in feed_own]
    gains = lax.all_gather(jnp.stack([gain_attn, gain_ffn]), "fsdp", axis=1, tiled=True).astype(F32)
    gain_one, gain_two = gains[0], gains[1]

    base = rows
    position = (chip * rows - rows + jnp.arange(keys, dtype=jnp.int32)).astype(F32)
    pair_index = (jnp.arange(LANES, dtype=jnp.int32) % (HEAD_DIM // 2)).astype(F32)
    angles = position[:, None] * (10000.0 ** (-pair_index * 2.0 / HEAD_DIM))[None, :]
    cos, sin = jnp.cos(angles), jnp.sin(angles)
    ids_own = jnp.concatenate(in_order(segment_ids, swap_core(segment_ids), core == 0))
    ids_before = jnp.where(chip > 0, to_later_chip(ids_own), -1)
    ids = jnp.concatenate([ids_before, ids_own])
    start = jnp.sum((ids[None, :] < ids_own[:, None]).astype(jnp.int32), axis=1)
    tiles = -(-rows // TILE)
    low = start[::TILE] // TILE
    ends = [-(-min(base + (t + 1) * TILE, base + rows) // TILE) for t in range(tiles)]
    bounds = jnp.stack([low, jnp.array(ends, jnp.int32)])
    start = jnp.pad(start, (0, tiles * TILE - rows), constant_values=2 * keys)[None]

    inputs = tokens.astype(F32)
    inv_one = inverse_rms(inputs)
    normed = (inputs * inv_one * gain_one).astype(BF16)
    before = widen_chip(to_later_chip(normed))
    window = jnp.concatenate(before + widen_chip(normed) + [jnp.zeros((keys - 2 * rows, depth), BF16)], axis=0)
    dy = jnp.concatenate(widen_chip(cotangent), axis=0)
    q, k, v = project(window, attention_weights, cos, sin, base)
    attended, lse = attend(bounds, q, k, v, start, rows, base)
    residual = inputs + narrow_chip(dot(attended, attention_weights[3]))

    inv_two = inverse_rms(residual)
    normed_two = jnp.concatenate(widen_chip((residual * inv_two * gain_two).astype(BF16)), axis=0)
    hidden, gate_grad, up_grad, back_two = feed(normed_two, dy, feed_own, feed_other)
    normed_two_grad = narrow_chip(back_two)
    grads_other = feed_weights(normed_two, dy, hidden, gate_grad, up_grad, 1)
    grads_own = feed_weights(normed_two, dy, hidden, gate_grad, up_grad, 0)
    feed_sums = [scatter_fsdp(add_low(own, swap_chip(other))) for own, other in zip(grads_own, grads_other)]
    units = feed_own[2].shape[1]
    out_partial = dot_nt(hidden[:, :units], feed_own[2]) + dot_nt(hidden[:, units:], feed_other[2])
    layer_out = residual + narrow_chip(out_partial)
    gain_two_grad = jnp.sum(normed_two_grad * residual * inv_two, axis=0)
    resid_grad = cotangent.astype(F32) + normalize_back(residual, inv_two, gain_two, normed_two_grad)

    grad = jnp.concatenate(widen_chip(resid_grad.astype(BF16)), axis=0)
    out_grad = dot_nt(grad, attention_weights[3]).astype(BF16)
    dq, dk, dv = attend_back(bounds, q, k, v, attended, out_grad, lse, start, cos, sin, rows, base)
    chip_rows = window[base : base + rows]
    weight_grads = jnp.stack(
        [
            dot_tn(dq, chip_rows).astype(BF16),
            dot_tn(dk, window).astype(BF16),
            dot_tn(dv, window).astype(BF16),
            dot_tn(attended, grad).astype(BF16),
        ]
    ).reshape(4, 2, part_width, fsdp, shard_rows)
    weight_grads = jnp.transpose(weight_grads, (1, 3, 0, 2, 4))
    attention_sum = scatter_fsdp(add_low(weight_grads[0], swap_chip(weight_grads[1])))[0]
    window_back = dot(dk, attention_weights[1]) + dot(dv, attention_weights[2])
    own_back = window_back[base : base + rows] + dot(dq, attention_weights[0])
    earlier_back = to_earlier_chip(narrow_chip(window_back[:base]).astype(BF16)).astype(F32)
    normed_grad = narrow_chip(own_back) + earlier_back
    gain_one_grad = jnp.sum(normed_grad * inputs * inv_one, axis=0)
    grad_input = resid_grad + normalize_back(inputs, inv_one, gain_one, normed_grad)

    attention_all = jnp.stack(all_quarters(attention_sum), axis=1).reshape(4, width, shard_rows)
    attention_all = attention_all[:, :real_width].astype(F32)
    feed_all = [all_quarters(total) for total in feed_sums]
    gain_grads = lax.psum(jnp.stack([gain_one_grad, gain_two_grad]), ("fsdp", "ctx", "tp"))
    gain_rows = gain_attn.shape[0]
    gain_own = lax.dynamic_slice_in_dim(gain_grads, lax.axis_index("fsdp") * gain_rows, gain_rows, 1)
    return (
        layer_out.astype(BF16)[None],
        grad_input[None],
        jnp.transpose(attention_all[0]),
        jnp.transpose(attention_all[1]),
        jnp.transpose(attention_all[2]),
        attention_all[3],
        jnp.concatenate(feed_all[0], axis=1).astype(F32),
        jnp.concatenate(feed_all[1], axis=1).astype(F32),
        jnp.transpose(jnp.concatenate(feed_all[2], axis=1)).astype(F32),
        gain_own[0],
        gain_own[1],
    )


def solution(mesh):
    rows = P("fsdp", ("ctx", "tp"), None)
    into, outof, gain = P("fsdp", "tp"), P("tp", "fsdp"), P("fsdp")
    return jax.shard_map(
        shards,
        mesh=mesh,
        in_specs=(rows, P("fsdp", "ctx"), into, into, into, outof, into, into, outof, gain, gain, rows),
        out_specs=(rows, rows, into, into, into, outof, into, into, outof, gain, gain),
        check_vma=False,
    )
```

```python
import functools

import jax
import jax.numpy as jnp
from jax import lax
from jax.experimental import pallas as pl
from jax.experimental.pallas import tpu as pltpu
from jax.sharding import PartitionSpec as P

HEAD_DIM = 64
EPSILON = 1e-05
MASKED = -1e30
BF16 = jnp.bfloat16
F32 = jnp.float32
TILE = 256
LANES = 128
VMEM_BYTES = 60 * 1024 * 1024


def dot(left, right):
    return jnp.dot(left, right, preferred_element_type=F32)


def dot_nt(left, right):
    return lax.dot_general(left, right, (((1,), (1,)), ((), ())), preferred_element_type=F32)


def dot_tn(left, right):
    return lax.dot_general(left, right, (((0,), (0,)), ((), ())), preferred_element_type=F32)


def swap_chip(values):
    return lax.ppermute(values, "ctx", [(i, i ^ 2) for i in range(lax.axis_size("ctx"))])


def swap_core(values):
    return lax.ppermute(values, "ctx", [(i, i ^ 1) for i in range(lax.axis_size("ctx"))])


def to_later_chip(values):
    return lax.ppermute(values, "ctx", [(i, i + 2) for i in range(lax.axis_size("ctx") - 2)])


def to_earlier_chip(values):
    return lax.ppermute(values, "ctx", [(i, i - 2) for i in range(2, lax.axis_size("ctx"))])


def swap_tp(values):
    return lax.ppermute(values, "tp", [(0, 1), (1, 0)])


def in_order(mine, other, mine_first):
    return [jnp.where(mine_first, mine, other), jnp.where(mine_first, other, mine)]


def after(values, *earlier):
    return lax.optimization_barrier((values, earlier))[0]


def widen_tp(rows):
    if lax.axis_size("tp") == 2:
        return [rows, swap_tp(rows)]
    return [lax.all_gather(rows, "tp", axis=0, tiled=True)]


def widen_chip(rows):
    mine = widen_tp(rows)
    return mine + [swap_core(block) for block in mine]


def block_offset(index, half):
    core = lax.axis_index("ctx") % 2
    if lax.axis_size("tp") != 2:
        return jnp.where(index == 0, core, 1 - core) * half
    place = lax.axis_index("tp")
    core = core if index < 2 else 1 - core
    place = place if index % 2 == 0 else 1 - place
    return core * half + place * (half // 2)


def narrow_core(kept, sent):
    return kept.astype(F32) + swap_core(sent).astype(F32)


def narrow_tp(pair):
    if lax.axis_size("tp") != 2:
        return lax.psum_scatter(pair.astype(BF16), "tp", scatter_dimension=0, tiled=True).astype(F32)
    rows = pair.shape[0] // 2
    return pair[:rows] + swap_tp(pair[rows:].astype(BF16)).astype(F32)


def take_quarter(values, index, axis):
    size = values.shape[axis] // 4
    return lax.dynamic_slice_in_dim(values, index * size, size, axis)


def all_quarters(own):
    place = lax.axis_index("ctx")
    across = swap_chip(own)
    came = swap_core(jnp.stack([own, across]))
    low, high = in_order(jnp.stack([own, across]), came, place % 2 == 0)
    first = place < 2
    pick = jnp.where
    return [pick(first, low[0], low[1]), pick(first, high[0], high[1]), pick(first, low[1], low[0]), pick(first, high[1], high[0])]


def add_low(left, right):
    return (left.astype(F32) + right.astype(F32)).astype(BF16)


def call(kernel, name, flops, moved, **rest):
    return pl.pallas_call(
        kernel,
        name=name,
        cost_estimate=pl.CostEstimate(flops=flops, bytes_accessed=moved, transcendentals=0),
        compiler_params=pltpu.CompilerParams(vmem_limit_bytes=VMEM_BYTES),
        **rest,
    )


def whole():
    return pl.BlockSpec(memory_space=pltpu.VMEM)


def turn(values, cos, sin, direction):
    lane = lax.broadcasted_iota(jnp.int32, (1, LANES), 1)
    partner = jnp.where((lane // 32) % 2 == 0, pltpu.roll(values, 96, 1) * -direction, pltpu.roll(values, 32, 1) * direction)
    return values * cos + partner * sin


def block_spans(count, half, base):
    block = 2 * half // count
    offsets = [pl.multiple_of(block_offset(i, half), 16) for i in range(count)]
    return [pl.ds(at, block) for at in offsets] + [pl.ds(pl.multiple_of(base + at, 16), block) for at in offsets]


def project_kernel(count, half, base, *refs):
    blocks = refs[: 2 * count]
    weight_ref, cos_ref, sin_ref, q_ref, k_ref, v_ref = refs[2 * count :]
    width = q_ref.shape[1]
    tail = k_ref.shape[0] - 2 * base
    block = 2 * half // count
    k_ref[2 * base :, :] = jnp.zeros((tail, width), BF16)
    v_ref[2 * base :, :] = jnp.zeros((tail, width), BF16)
    for i, span in enumerate(block_spans(count, half, base)):
        rows = blocks[i][...]
        cos, sin = cos_ref[span, :], sin_ref[span, :]

        def rotated(values, out_ref, where):
            for c in range(0, width, LANES):
                out_ref[where, c : c + LANES] = turn(values[:, c : c + LANES], cos, sin, 1.0).astype(BF16)

        rotated(dot_nt(rows, weight_ref[1]), k_ref, span)
        v_ref[span, :] = dot_nt(rows, weight_ref[2]).astype(BF16)
        if i >= count:
            own = pl.ds(pl.multiple_of(block_offset(i - count, half), 16), block)
            rotated(dot_nt(rows, weight_ref[0]), q_ref, own)


def project(blocks, weights, cos, sin, keys):
    count = len(blocks) // 2
    block, depth = blocks[0].shape
    rows = count * block
    width = weights.shape[1]
    wide = jax.ShapeDtypeStruct((keys, width), BF16)
    return call(
        functools.partial(project_kernel, count, rows // 2, rows),
        "project",
        keys * depth * width * 5,
        keys * depth * 2,
        out_shape=(jax.ShapeDtypeStruct((rows, width), BF16), wide, wide),
        in_specs=[whole()] * (2 * count + 3),
        out_specs=[whole()] * 3,
    )(*blocks, weights, cos, sin)


def place_kernel(fsdp, *refs):
    blocks, out_ref = refs[:-1], refs[-1]
    part, columns = blocks[0].shape[1:]
    me = lax.axis_index("fsdp")
    for i, block in enumerate(blocks):
        at = pl.multiple_of((me + i % fsdp) % fsdp * columns, LANES)
        first = i // fsdp * part
        out_ref[:, first : first + part, pl.ds(at, columns)] = block[...]


def place_weights(blocks, fsdp):
    kinds, part, columns = blocks[0].shape
    shape = (kinds, 2 * part, fsdp * columns)
    return call(
        functools.partial(place_kernel, fsdp),
        "place_weights",
        0,
        kinds * part * fsdp * columns * 8,
        out_shape=jax.ShapeDtypeStruct(shape, BF16),
        in_specs=[whole()] * len(blocks),
        out_specs=whole(),
    )(*blocks)


def out_kernel(half, count, o_ref, weight_ref, kept_ref, sent_ref):
    block = 2 * half // count
    for i in range(count):
        at = pl.multiple_of(block_offset(i, half), 16)
        part = dot(o_ref[pl.ds(at, block), :], weight_ref[3])
        if i < count // 2:
            kept_ref[i * block : (i + 1) * block, :] = part
        else:
            sent_ref[i * block - half : (i + 1) * block - half, :] = part.astype(BF16)


def out_project(attended, weights, count):
    rows, width = attended.shape
    depth = weights.shape[2]
    half = rows // 2
    return call(
        functools.partial(out_kernel, half, count),
        "out_project",
        rows * width * depth * 2,
        rows * depth * 3,
        out_shape=(jax.ShapeDtypeStruct((half, depth), F32), jax.ShapeDtypeStruct((half, depth), BF16)),
        in_specs=[whole(), whole()],
        out_specs=[whole(), whole()],
    )(attended, weights)


def out_back_kernel(half, count, fsdp, o_ref, weight_ref, *refs):
    blocks, (grad_ref, own_ref, other_ref, chip_rows) = refs[:count], refs[count:]
    block = 2 * half // count
    for i in range(count):
        at = pl.multiple_of(block_offset(i, half), 16)
        grad = blocks[i][...]
        grad_ref[pl.ds(at, block), :] = dot_nt(grad, weight_ref[3]).astype(BF16)
        chip_rows[pl.ds(at, block), :] = grad
    total = dot_tn(o_ref[...], chip_rows[...])
    part, columns = own_ref.shape[1], own_ref.shape[2]
    for z in range(fsdp):
        own_ref[z] = total[:part, z * columns : (z + 1) * columns].astype(BF16)
        other_ref[z] = total[part:, z * columns : (z + 1) * columns].astype(BF16)


def out_back(attended, weights, blocks, fsdp):
    rows, width = attended.shape
    depth = weights.shape[2]
    grads = jax.ShapeDtypeStruct((fsdp, width // 2, depth // fsdp), BF16)
    return call(
        functools.partial(out_back_kernel, rows // 2, len(blocks), fsdp),
        "out_back",
        rows * width * depth * 4,
        rows * depth * 3,
        out_shape=(jax.ShapeDtypeStruct((rows, width), BF16), grads, grads),
        in_specs=[whole()] * (2 + len(blocks)),
        out_specs=[whole()] * 3,
        scratch_shapes=[pltpu.VMEM((rows, depth), BF16)],
    )(attended, weights, *blocks)


def project_weights_kernel(count, half, base, dq_ref, dk_ref, dv_ref, *refs):
    blocks, out_refs, window = refs[: 2 * count], refs[2 * count : -1], refs[-1]
    window[2 * base :, :] = jnp.zeros((window.shape[0] - 2 * base, window.shape[1]), BF16)
    for block, span in zip(blocks, block_spans(count, half, base)):
        window[span, :] = block[...]
    part = out_refs[0].shape[1]
    results = (
        dot_tn(dv_ref[...], window[...]),
        dot_tn(dk_ref[...], window[...]),
        dot_tn(dq_ref[...], window[base : 2 * base, :]),
    )
    for i, result in enumerate(results):
        out_refs[2 * i][0] = result[:part].astype(BF16)
        out_refs[2 * i + 1][0] = result[part:].astype(BF16)


def project_weights(dq, dk, dv, blocks, fsdp):
    keys, width = dk.shape
    rows = dq.shape[0]
    block, depth = blocks[0].shape
    count = len(blocks) // 2
    columns = depth // fsdp
    fixed = lambda array: pl.BlockSpec(array.shape, lambda z: (0, 0))
    return call(
        functools.partial(project_weights_kernel, count, rows // 2, rows),
        "project_weights",
        keys * width * depth * 5,
        keys * depth * 2,
        grid=(fsdp,),
        out_shape=[jax.ShapeDtypeStruct((fsdp, width // 2, columns), BF16)] * 6,
        in_specs=[fixed(dq), fixed(dk), fixed(dv)] + [pl.BlockSpec((block, columns), lambda z: (0, z))] * (2 * count),
        out_specs=[pl.BlockSpec((1, width // 2, columns), lambda z: (z, 0, 0))] * 6,
        scratch_shapes=[pltpu.VMEM((keys, columns), BF16)],
    )(dq, dk, dv, *blocks)


def project_back_kernel(half, count, base, dq_ref, dk_ref, dv_ref, weight_ref, *out_refs):
    block = 2 * half // count
    for part in range(2):
        kept_ref, sent_ref = out_refs[2 * part : 2 * part + 2]
        for i in range(count):
            at = pl.multiple_of(block_offset(i, half), 16)
            where = pl.ds(part * base + at, block)
            total = dot(dk_ref[where, :], weight_ref[1]) + dot(dv_ref[where, :], weight_ref[2])
            if part == 1:
                total = total + dot(dq_ref[pl.ds(at, block), :], weight_ref[0])
            if i < count // 2:
                kept_ref[i * block : (i + 1) * block, :] = total
            else:
                sent_ref[i * block - half : (i + 1) * block - half, :] = total.astype(BF16)


def project_back(dq, dk, dv, weights, base, count):
    rows, width = dq.shape
    depth = weights.shape[2]
    half = rows // 2
    kept, sent = jax.ShapeDtypeStruct((half, depth), F32), jax.ShapeDtypeStruct((half, depth), BF16)
    return call(
        functools.partial(project_back_kernel, half, count, base),
        "project_back",
        rows * width * depth * 10,
        rows * depth * 6,
        out_shape=(kept, sent, kept, sent),
        in_specs=[whole()] * 4,
        out_specs=[whole()] * 4,
    )(dq, dk, dv, weights)


def lane_half(head):
    return (lax.broadcasted_iota(jnp.int32, (1, LANES), 1) // HEAD_DIM) == head % 2


def forward_kernel(rows, base, bounds, q_ref, k_ref, v_ref, start_ref, o_ref, lse_ref, q_buf, s_buf, top_buf, sum_buf, acc_buf):
    heads = q_buf.shape[0]
    zero = jnp.zeros((), BF16)
    for t in range(-(-rows // TILE)):
        low, high = bounds[0, t], bounds[1, t]
        n = min(TILE, rows - t * TILE)
        span = slice(t * TILE, (t + 1) * TILE)
        start = start_ref[:, span]
        row = base + t * TILE + lax.broadcasted_iota(jnp.int32, (1, TILE), 1)
        for h in range(heads):
            c = (h // 2) * LANES
            scaled = (q_ref[t * TILE : t * TILE + n, c : c + LANES].astype(F32) * HEAD_DIM**-0.5).astype(BF16)
            q_buf[h, :n, :] = jnp.where(lane_half(h), scaled, zero)
            if n < TILE:
                q_buf[h, n:, :] = jnp.zeros((TILE - n, LANES), BF16)
        top_buf[...] = jnp.full_like(top_buf, MASKED)
        sum_buf[...] = jnp.zeros_like(sum_buf)
        acc_buf[...] = jnp.zeros_like(acc_buf)

        @pl.loop(low, high)
        def _(i):
            at = pl.multiple_of(i * TILE, TILE)
            place = at + lax.broadcasted_iota(jnp.int32, (TILE, TILE), 0)
            allowed = (place >= start) & (place <= row)
            for h in range(heads):
                c = (h // 2) * LANES
                s = jnp.where(allowed, dot_nt(k_ref[pl.ds(at, TILE), c : c + LANES], q_buf[h]), MASKED)
                s_buf[h, pl.ds(at, TILE), :] = s
                top_buf[h] = jnp.maximum(top_buf[h], jnp.max(s.reshape(TILE // 8, 8, TILE), axis=0))

        tops = [jnp.max(top_buf[h], axis=0, keepdims=True) for h in range(heads)]

        @pl.loop(low, high)
        def _(i):
            at = pl.multiple_of(i * TILE, TILE)
            for h in range(heads):
                c = (h // 2) * LANES
                p = jnp.exp(s_buf[h, pl.ds(at, TILE), :] - tops[h])
                sum_buf[h] += jnp.sum(p.reshape(TILE // 8, 8, TILE), axis=0)
                both = dot_tn(v_ref[pl.ds(at, TILE), c : c + LANES], p.astype(BF16))
                acc_buf[h] += both[HEAD_DIM * (h % 2) : HEAD_DIM * (h % 2) + HEAD_DIM]

        for h in range(heads):
            total = jnp.sum(sum_buf[h], axis=0, keepdims=True)
            lse_ref[h : h + 1, span] = tops[h] + jnp.log(total)
            acc_buf[h] = acc_buf[h] / total
        for pair in range(heads // 2):
            o = jnp.transpose(jnp.concatenate([acc_buf[2 * pair], acc_buf[2 * pair + 1]], axis=0))
            o_ref[t * TILE : t * TILE + n, pair * LANES : (pair + 1) * LANES] = o[:n].astype(BF16)


def attend(bounds, q, k, v, start, rows, base):
    keys, width = k.shape
    heads = width // HEAD_DIM
    padded = -(-rows // TILE) * TILE
    return call(
        functools.partial(forward_kernel, rows, base),
        "attend",
        rows * rows * width * 8,
        keys * width * 8,
        out_shape=(jax.ShapeDtypeStruct((rows, width), BF16), jax.ShapeDtypeStruct((heads, padded), F32)),
        in_specs=[pl.BlockSpec(memory_space=pltpu.SMEM)] + [whole()] * 4,
        out_specs=[whole(), whole()],
        scratch_shapes=[
            pltpu.VMEM((heads, TILE, LANES), BF16),
            pltpu.VMEM((heads, keys, TILE), F32),
            pltpu.VMEM((heads, 8, TILE), F32),
            pltpu.VMEM((heads, 8, TILE), F32),
            pltpu.VMEM((heads, HEAD_DIM, TILE), F32),
        ],
    )(bounds, q, k, v, start)


def backward_kernel(
    rows, base, bounds, q_ref, k_ref, v_ref, o_ref, g_ref, lse_ref, start_ref, cos_ref, sin_ref,
    dq_ref, dk_ref, dv_ref, q_buf, g_buf, d_buf, dq_acc, dk_acc, dv_acc,
):
    heads = q_buf.shape[0]
    zero = jnp.zeros((), BF16)
    scale = HEAD_DIM**-0.5
    dk_acc[...] = jnp.zeros_like(dk_acc)
    dv_acc[...] = jnp.zeros_like(dv_acc)
    for t in range(-(-rows // TILE)):
        low, high = bounds[0, t], bounds[1, t]
        n = min(TILE, rows - t * TILE)
        span = slice(t * TILE, (t + 1) * TILE)
        here = slice(t * TILE, t * TILE + n)
        window = slice(base + t * TILE, base + t * TILE + n)
        start = start_ref[:, span]
        row = base + t * TILE + lax.broadcasted_iota(jnp.int32, (1, TILE), 1)
        for pair in range(heads // 2):
            c = pair * LANES
            scaled = (q_ref[here, c : c + LANES].astype(F32) * scale).astype(BF16)
            grad = g_ref[here, c : c + LANES]
            product = grad.astype(F32) * o_ref[here, c : c + LANES].astype(F32)
            if n < TILE:
                product = jnp.concatenate([product, jnp.zeros((TILE - n, LANES), F32)], axis=0)
            product = jnp.transpose(product)
            for h in (2 * pair, 2 * pair + 1):
                q_buf[h, :n, :] = jnp.where(lane_half(h), scaled, zero)
                g_buf[h, :n, :] = jnp.where(lane_half(h), grad, zero)
                if n < TILE:
                    q_buf[h, n:, :] = jnp.zeros((TILE - n, LANES), BF16)
                    g_buf[h, n:, :] = jnp.zeros((TILE - n, LANES), BF16)
                d_buf[h : h + 1, :] = jnp.sum(product[HEAD_DIM * (h % 2) : HEAD_DIM * (h % 2) + HEAD_DIM], axis=0, keepdims=True)
        dq_acc[...] = jnp.zeros_like(dq_acc)

        @pl.loop(low, high)
        def _(i):
            at = pl.multiple_of(i * TILE, TILE)
            place = at + lax.broadcasted_iota(jnp.int32, (TILE, TILE), 0)
            allowed = (place >= start) & (place <= row)
            for pair in range(heads // 2):
                c = pair * LANES
                k = k_ref[pl.ds(at, TILE), c : c + LANES]
                v = v_ref[pl.ds(at, TILE), c : c + LANES]
                dq = dk = dv = 0.0
                for h in (2 * pair, 2 * pair + 1):
                    p = jnp.where(allowed, jnp.exp(dot_nt(k, q_buf[h]) - lse_ref[h : h + 1, span]), 0.0)
                    ds = (p * (dot_nt(v, g_buf[h]) - d_buf[h : h + 1, :])).astype(BF16)
                    dv = dv + dot(p.astype(BF16), g_buf[h])
                    dk = dk + dot(ds, q_buf[h])
                    dq = dq + dot_tn(ds, jnp.where(lane_half(h), k, zero))
                dk_acc[pl.ds(at, TILE), c : c + LANES] += dk
                dv_acc[pl.ds(at, TILE), c : c + LANES] += dv
                dq_acc[:, c : c + LANES] += dq

        for c in range(0, heads * HEAD_DIM, LANES):
            dq = dq_acc[:n, c : c + LANES] * scale
            dq_ref[here, c : c + LANES] = turn(dq, cos_ref[window, :], sin_ref[window, :], -1.0).astype(BF16)
    for c in range(0, heads * HEAD_DIM, LANES):
        dk_ref[:, c : c + LANES] = turn(dk_acc[:, c : c + LANES], cos_ref[...], sin_ref[...], -1.0).astype(BF16)
    dv_ref[...] = dv_acc[...].astype(BF16)


def attend_back(bounds, q, k, v, o, grad, lse, start, cos, sin, rows, base):
    keys, width = k.shape
    heads = width // HEAD_DIM
    wide = jax.ShapeDtypeStruct((keys, width), BF16)
    return call(
        functools.partial(backward_kernel, rows, base),
        "attend_back",
        rows * rows * width * 20,
        keys * width * 16,
        out_shape=(jax.ShapeDtypeStruct((rows, width), BF16), wide, wide),
        in_specs=[pl.BlockSpec(memory_space=pltpu.SMEM)] + [whole()] * 9,
        out_specs=[whole()] * 3,
        scratch_shapes=[
            pltpu.VMEM((heads, TILE, LANES), BF16),
            pltpu.VMEM((heads, TILE, LANES), BF16),
            pltpu.VMEM((heads, TILE), F32),
            pltpu.VMEM((TILE, width), F32),
            pltpu.VMEM((keys, width), F32),
            pltpu.VMEM((keys, width), F32),
        ],
    )(bounds, q, k, v, o, grad, lse, start, cos, sin)


def feed_kernel(count, own_steps, *refs):
    n_refs, dy_refs, weights = refs[:count], refs[count : 2 * count], refs[2 * count : 2 * count + 6]
    hidden_ref, gate_ref, up_ref, kept_ref, sent_ref, acc = refs[2 * count + 6 :]
    step = pl.program_id(0)
    block = n_refs[0].shape[0]
    half = kept_ref.shape[0]

    @pl.when(step == 0)
    def _():
        acc[...] = jnp.zeros_like(acc)

    def tile(gate_w, up_w, down_w):
        for i in range(count):
            rows = slice(i * block, (i + 1) * block)
            normed = n_refs[i][...]
            gate = dot(normed, gate_w[...])
            up = dot(normed, up_w[...])
            grad = dot(dy_refs[i][...], down_w[...])
            sig = 1.0 / (1.0 + jnp.exp(-gate))
            silu = gate * sig
            hidden_ref[rows, :] = (silu * up).astype(BF16)
            gate_grad = (grad * up * sig * (1.0 + gate * (1.0 - sig))).astype(BF16)
            up_grad = (grad * silu).astype(BF16)
            gate_ref[rows, :] = gate_grad
            up_ref[rows, :] = up_grad
            acc[rows, :] += dot_nt(gate_grad, gate_w[...]) + dot_nt(up_grad, up_w[...])

    @pl.when(step < own_steps)
    def _():
        tile(*weights[:3])

    @pl.when(step >= own_steps)
    def _():
        tile(*weights[3:])

    @pl.when(step == pl.num_programs(0) - 1)
    def _():
        kept_ref[...] = acc[:half, :]
        sent_ref[...] = acc[half:, :].astype(BF16)


def feed(normed, dy, own, other):
    count = len(normed)
    block, depth = normed[0].shape
    rows = count * block
    units = own[0].shape[1]
    tile = min(TILE, units)
    steps = units // tile
    fixed = pl.BlockSpec((block, depth), lambda i: (0, 0))
    kept = pl.BlockSpec((rows // 2, depth), lambda i: (0, 0))
    first = pl.BlockSpec((depth, tile), lambda i: (0, jnp.minimum(i, steps - 1)))
    second = pl.BlockSpec((depth, tile), lambda i: (0, jnp.maximum(i - steps, 0)))
    out = pl.BlockSpec((rows, tile), lambda i: (0, i))
    wide = jax.ShapeDtypeStruct((rows, 2 * units), BF16)
    return call(
        functools.partial(feed_kernel, count, steps),
        "feed",
        rows * depth * units * 20,
        depth * units * 12,
        grid=(2 * steps,),
        out_shape=(wide, wide, wide, jax.ShapeDtypeStruct((rows // 2, depth), F32), jax.ShapeDtypeStruct((rows // 2, depth), BF16)),
        in_specs=[fixed] * (2 * count) + [first] * 3 + [second] * 3,
        out_specs=[out, out, out, kept, kept],
        scratch_shapes=[pltpu.VMEM((rows, depth), F32)],
    )(*normed, *dy, *own, *other)


def feed_weights_kernel(count, *refs):
    blocks = refs[: 2 * count]
    hidden_ref, gate_ref, up_ref, gate_out, up_out, down_out, normed, dy = refs[2 * count :]
    block = blocks[0].shape[0]

    @pl.when(pl.program_id(0) == 0)
    def _():
        for i in range(count):
            normed[i * block : (i + 1) * block, :] = blocks[i][...]
            dy[i * block : (i + 1) * block, :] = blocks[count + i][...]

    gate_out[...] = dot_tn(normed[...], gate_ref[...]).astype(BF16)
    up_out[...] = dot_tn(normed[...], up_ref[...]).astype(BF16)
    down_out[...] = dot_tn(dy[...], hidden_ref[...]).astype(BF16)


def feed_weights(normed, dy, hidden, gate_grad, up_grad, part):
    count = len(normed)
    block, depth = normed[0].shape
    rows = count * block
    units = hidden.shape[1] // 2
    tile = min(TILE, units)
    steps = units // tile
    fixed = pl.BlockSpec((block, depth), lambda i: (0, 0))
    units_in = pl.BlockSpec((rows, tile), lambda i: (0, part * steps + i))
    out = pl.BlockSpec((depth, tile), lambda i: (0, i))
    shape = jax.ShapeDtypeStruct((depth, units), BF16)
    return call(
        functools.partial(feed_weights_kernel, count),
        "feed_weights",
        rows * depth * units * 6,
        depth * units * 6,
        grid=(steps,),
        out_shape=(shape, shape, shape),
        in_specs=[fixed] * (2 * count) + [units_in] * 3,
        out_specs=[out, out, out],
        scratch_shapes=[pltpu.VMEM((rows, depth), BF16)] * 2,
    )(*normed, *dy, hidden, gate_grad, up_grad)


def feed_out_kernel(half, hidden_ref, own_ref, other_ref, kept_ref, sent_ref):
    units = own_ref.shape[1]
    tile = half // 2
    for r in range(0, 2 * half, tile):
        total = dot_nt(hidden_ref[r : r + tile, :units], own_ref[...]) + dot_nt(hidden_ref[r : r + tile, units:], other_ref[...])
        if r < half:
            kept_ref[r : r + tile, :] = total
        else:
            sent_ref[r - half : r - half + tile, :] = total.astype(BF16)


def feed_out(hidden, own, other):
    rows = hidden.shape[0]
    depth, units = own.shape
    half = rows // 2
    return call(
        functools.partial(feed_out_kernel, half),
        "feed_out",
        rows * depth * units * 4,
        rows * depth * 3,
        out_shape=(jax.ShapeDtypeStruct((half, depth), F32), jax.ShapeDtypeStruct((half, depth), BF16)),
        in_specs=[whole()] * 3,
        out_specs=[whole()] * 2,
    )(hidden, own, other)


def normalize_back(values, inverse, gain, grad_rows):
    scaled = grad_rows * gain
    return inverse * scaled - values * inverse**3 * jnp.mean(scaled * values, axis=-1, keepdims=True)


def inverse_rms(values):
    return lax.rsqrt(jnp.mean(values * values, axis=-1, keepdims=True) + EPSILON)


def pull_fsdp(values, step):
    count = lax.axis_size("fsdp")
    return lax.ppermute(values, "fsdp", [(i, (i - step) % count) for i in range(count)])


def gather_gains(gains):
    count = lax.axis_size("fsdp")
    rolled = jnp.concatenate([gains] + [pull_fsdp(gains, step) for step in range(1, count)], axis=1).astype(F32)
    twice = jnp.concatenate([rolled, rolled], axis=1)
    at = (count - lax.axis_index("fsdp")) % count * gains.shape[1]
    return lax.dynamic_slice_in_dim(twice, at, rolled.shape[1], 1)


def gain_totals(gains):
    if lax.axis_size("tp") == 2:
        gains = gains + swap_tp(gains)
    else:
        gains = lax.psum(gains, "tp")
    gains = gains + swap_core(gains)
    gains = gains + swap_chip(gains)
    count = lax.axis_size("fsdp")
    blocks = jnp.stack(jnp.split(gains, count, axis=1))
    return jnp.sum(lax.all_to_all(blocks, "fsdp", 0, 0, tiled=True), axis=0)


def sum_over_chips_and_fsdp(own, other):
    mine = add_low(own, swap_chip(other))
    return jnp.sum(lax.all_to_all(mine, "fsdp", 0, 0, tiled=True).astype(F32), axis=0).astype(BF16)


def shards(tokens, segment_ids, wq, wk, wv, wo, w_gate, w_up, w_down, gain_attn, gain_ffn, cotangent):
    tokens, cotangent, segment_ids = tokens[0], cotangent[0], segment_ids[0]
    fsdp = lax.axis_size("fsdp")
    place = lax.axis_index("ctx")
    chip, core = place // 2, place % 2
    half = segment_ids.shape[0]
    rows = 2 * half
    real_width = wq.shape[1]
    columns, depth = wq.shape[0], wq.shape[0] * fsdp
    width = -(-real_width // (4 * HEAD_DIM)) * 4 * HEAD_DIM
    part = width // 4
    keys = -(-2 * rows // TILE) * TILE
    base = rows

    pad = ((0, 0), (0, width - real_width))
    wide = [jnp.pad(w, pad) for w in (wq, wk, wv)] + [jnp.pad(wo, pad[::-1])]

    def attention_piece(index):
        pieces = [jnp.transpose(take_quarter(w, index, 1)) for w in wide[:3]]
        return jnp.stack(pieces + [take_quarter(wide[3], index, 0)])

    gain_one, gain_two = gather_gains(jnp.stack([gain_attn, gain_ffn]))
    inputs = tokens.astype(F32)
    inv_one = inverse_rms(inputs)
    normed = (inputs * inv_one * gain_one).astype(BF16)
    before = to_later_chip(normed)
    own_blocks = widen_chip(normed)
    before_blocks = widen_chip(before)
    count = len(own_blocks)
    blocks = before_blocks + own_blocks
    ring = [attention_piece(place)]
    ring.append(pull_fsdp(ring[0], 1))
    for step in range(2, fsdp):
        ring.append(pull_fsdp(after(ring[-1], normed if step == 2 else own_blocks[1]), 1))
    crossed = [attention_piece(place ^ 2)] + [swap_chip(block) for block in ring[1:]]
    weights = place_weights(ring + crossed, fsdp)

    pieces = (take_quarter(w_gate, place, 1), take_quarter(w_up, place, 1), jnp.transpose(take_quarter(w_down, place, 0)))
    feed_own = [lax.all_gather(after(w, ring[-2]), "fsdp", axis=0, tiled=True) for w in pieces]
    feed_other = [swap_chip(w) for w in feed_own]

    position = (chip * rows - rows + jnp.arange(keys, dtype=jnp.int32)).astype(F32)
    pair_index = (jnp.arange(LANES, dtype=jnp.int32) % (HEAD_DIM // 2)).astype(F32)
    angles = position[:, None] * (10000.0 ** (-pair_index * 2.0 / HEAD_DIM))[None, :]
    cos, sin = jnp.cos(angles), jnp.sin(angles)
    ids_own = jnp.concatenate(in_order(segment_ids, swap_core(segment_ids), core == 0))
    ids_before = jnp.where(chip > 0, to_later_chip(ids_own), -1)
    ids = jnp.concatenate([ids_before, ids_own])
    start = jnp.sum((ids[None, :] < ids_own[:, None]).astype(jnp.int32), axis=1)
    tiles = -(-rows // TILE)
    ends = [-(-min(base + (t + 1) * TILE, base + rows) // TILE) for t in range(tiles)]
    bounds = jnp.stack([start[::TILE] // TILE, jnp.array(ends, jnp.int32)])
    start = jnp.pad(start, (0, tiles * TILE - rows), constant_values=2 * keys)[None]

    q, k, v = project(blocks, weights, cos, sin, keys)
    dy = widen_chip(after(cotangent, before_blocks[1]))
    attended, lse = attend(bounds, after(q, feed_own[0]), after(k, *dy), v, start, rows, base)
    kept, sent = out_project(after(attended, feed_own[1], feed_other[0]), weights, count)
    residual = inputs + narrow_tp(narrow_core(kept, sent))

    inv_two = inverse_rms(residual)
    normed_two = widen_chip(after((residual * inv_two * gain_two).astype(BF16), feed_own[2], feed_other[1]))
    hidden, gate_grad, up_grad, kept, sent = feed(normed_two, dy, feed_own, feed_other)
    pair = narrow_core(kept, sent)
    normed_two_grad = narrow_tp(pair)
    grads_other = feed_weights(normed_two, dy, after(hidden, pair), gate_grad, up_grad, 1)
    gain_two_grad = jnp.sum(normed_two_grad * residual * inv_two, axis=0)
    resid_grad = cotangent.astype(F32) + normalize_back(residual, inv_two, gain_two, normed_two_grad)
    resid_low = resid_grad.astype(BF16)
    grads_own = feed_weights(normed_two, dy, after(hidden, resid_low), gate_grad, up_grad, 0)
    feed_mine = [add_low(own, swap_chip(other)) for own, other in zip(grads_own, grads_other)]
    feed_sums = [lax.psum_scatter(mine, "fsdp", scatter_dimension=0, tiled=True) for mine in feed_mine]
    kept, sent = feed_out(after(hidden, grads_own[0]), feed_own[2], feed_other[2])
    layer_out = residual + narrow_tp(narrow_core(kept, sent))

    grad_blocks = widen_chip(resid_low)
    out_grad, out_own, out_other = out_back(attended, weights, grad_blocks, fsdp)
    dq, dk, dv = attend_back(bounds, q, k, v, attended, after(out_grad, feed_mine[0]), lse, start, cos, sin, rows, base)
    out_sum = sum_over_chips_and_fsdp(out_own, out_other)
    v_own, v_other, k_own, k_other, q_own, q_other = project_weights(after(dq, feed_sums[0]), dk, dv, blocks, fsdp)
    v_sum, k_sum, q_sum = (
        sum_over_chips_and_fsdp(*pair) for pair in ((v_own, v_other), (k_own, k_other), (q_own, q_other))
    )
    early_kept, early_sent, kept, sent = project_back(after(dq, feed_sums[1], feed_mine[2]), dk, dv, weights, base, count)
    earlier_back = to_earlier_chip(narrow_tp(narrow_core(early_kept, early_sent)).astype(BF16)).astype(F32)
    normed_grad = narrow_tp(narrow_core(kept, sent)) + earlier_back
    gain_one_grad = jnp.sum(normed_grad * inputs * inv_one, axis=0)
    grad_input = resid_grad + normalize_back(inputs, inv_one, gain_one, normed_grad)

    attention_all = jnp.stack(all_quarters(jnp.stack([q_sum, k_sum, v_sum, out_sum])), axis=1).reshape(4, width, columns)
    attention_all = attention_all[:, :real_width].astype(F32)
    feed_all = [all_quarters(total) for total in feed_sums]
    gain_own = gain_totals(jnp.stack([gain_one_grad, gain_two_grad]))
    return (
        layer_out.astype(BF16)[None],
        grad_input[None],
        jnp.transpose(attention_all[0]),
        jnp.transpose(attention_all[1]),
        jnp.transpose(attention_all[2]),
        attention_all[3],
        jnp.concatenate(feed_all[0], axis=1).astype(F32),
        jnp.concatenate(feed_all[1], axis=1).astype(F32),
        jnp.transpose(jnp.concatenate(feed_all[2], axis=1)).astype(F32),
        gain_own[0],
        gain_own[1],
    )


def solution(mesh):
    rows = P("fsdp", ("ctx", "tp"), None)
    into, outof, gain = P("fsdp", "tp"), P("tp", "fsdp"), P("fsdp")
    return jax.shard_map(
        shards,
        mesh=mesh,
        in_specs=(rows, P("fsdp", "ctx"), into, into, into, outof, into, into, outof, gain, gain, rows),
        out_specs=(rows, rows, into, into, into, outof, into, into, outof, gain, gain),
        check_vma=False,
    )
```

```python
import functools

import jax
import jax.numpy as jnp
from jax import lax
from jax.experimental import pallas as pl
from jax.experimental.pallas import tpu as pltpu
from jax.sharding import PartitionSpec as P

HEAD_DIM = 64
EPSILON = 1e-05
MASKED = -1e30
BF16 = jnp.bfloat16
F32 = jnp.float32
TILE = 256
LANES = 128
VMEM_BYTES = 60 * 1024 * 1024


def dot(left, right):
    return jnp.dot(left, right, preferred_element_type=F32)


def dot_nt(left, right):
    return lax.dot_general(left, right, (((1,), (1,)), ((), ())), preferred_element_type=F32)


def dot_tn(left, right):
    return lax.dot_general(left, right, (((0,), (0,)), ((), ())), preferred_element_type=F32)


def swap_chip(values):
    return lax.ppermute(values, "chip", [(0, 1), (1, 0)])


def swap_core(values):
    return lax.ppermute(values, "core", [(0, 1), (1, 0)])


def to_later_chip(values):
    return lax.ppermute(values, "chip", [(0, 1)])


def to_earlier_chip(values):
    return lax.ppermute(values, "chip", [(1, 0)])


def swap_tp(values):
    return lax.ppermute(values, "tp", [(0, 1), (1, 0)])


def in_order(mine, other, mine_first):
    return [jnp.where(mine_first, mine, other), jnp.where(mine_first, other, mine)]


def after(values, *earlier):
    return lax.optimization_barrier((values, earlier))[0]


def widen_tp(rows):
    if lax.axis_size("tp") == 2:
        return [rows, swap_tp(rows)]
    return [lax.all_gather(rows, "tp", axis=0, tiled=True)]


def widen_core(blocks):
    return blocks + [swap_core(block) for block in blocks]


def widen_chip(rows):
    return widen_core(widen_tp(rows))


def block_offset(index, half):
    core = lax.axis_index("core")
    if lax.axis_size("tp") != 2:
        return jnp.where(index == 0, core, 1 - core) * half
    place = lax.axis_index("tp")
    core = core if index < 2 else 1 - core
    place = place if index % 2 == 0 else 1 - place
    return core * half + place * (half // 2)


def narrow_chip(kept, sent):
    came = swap_core(sent)
    if lax.axis_size("tp") != 2:
        pair = (kept + came.astype(F32)).astype(BF16)
        return lax.psum_scatter(pair, "tp", scatter_dimension=0, tiled=True).astype(F32), came
    rows = kept.shape[0] // 2
    other = swap_tp((kept[rows:] + came[rows:].astype(F32)).astype(BF16))
    return kept[:rows] + came[:rows].astype(F32) + other.astype(F32), came


def take_quarter(values, index, axis):
    size = values.shape[axis] // 4
    return lax.dynamic_slice_in_dim(values, index * size, size, axis)


def all_quarters(own):
    across = swap_chip(own)
    return own, across, swap_core(jnp.stack([own, across]))


def add_low(left, right):
    return (left.astype(F32) + right.astype(F32)).astype(BF16)


def call(kernel, name, flops, moved, **rest):
    return pl.pallas_call(
        kernel,
        name=name,
        cost_estimate=pl.CostEstimate(flops=flops, bytes_accessed=moved, transcendentals=0),
        compiler_params=pltpu.CompilerParams(vmem_limit_bytes=VMEM_BYTES),
        **rest,
    )


def whole():
    return pl.BlockSpec(memory_space=pltpu.VMEM)


def turn(values, cos, sin, direction):
    lane = lax.broadcasted_iota(jnp.int32, (1, LANES), 1)
    partner = jnp.where((lane // 32) % 2 == 0, pltpu.roll(values, 96, 1) * -direction, pltpu.roll(values, 32, 1) * direction)
    return values * cos + partner * sin


def block_spans(count, half, base):
    block = 2 * half // count
    offsets = [pl.multiple_of(block_offset(i, half), 16) for i in range(count)]
    return [pl.ds(at, block) for at in offsets] + [pl.ds(pl.multiple_of(base + at, 16), block) for at in offsets]


def project_kernel(count, half, base, *refs):
    blocks = refs[: 2 * count]
    weight_ref, cos_ref, sin_ref, q_ref, k_ref, v_ref = refs[2 * count :]
    width = q_ref.shape[1]
    tail = k_ref.shape[0] - 2 * base
    block = 2 * half // count
    k_ref[2 * base :, :] = jnp.zeros((tail, width), BF16)
    v_ref[2 * base :, :] = jnp.zeros((tail, width), BF16)
    for i, span in enumerate(block_spans(count, half, base)):
        rows = blocks[i][...]
        cos, sin = cos_ref[span, :], sin_ref[span, :]

        def rotated(values, out_ref, where):
            for c in range(0, width, LANES):
                out_ref[where, c : c + LANES] = turn(values[:, c : c + LANES], cos, sin, 1.0).astype(BF16)

        rotated(dot_nt(rows, weight_ref[1]), k_ref, span)
        v_ref[span, :] = dot_nt(rows, weight_ref[2]).astype(BF16)
        if i >= count:
            own = pl.ds(pl.multiple_of(block_offset(i - count, half), 16), block)
            rotated(dot_nt(rows, weight_ref[0]), q_ref, own)


def project(blocks, weights, cos, sin, keys):
    count = len(blocks) // 2
    block, depth = blocks[0].shape
    rows = count * block
    width = weights.shape[1]
    wide = jax.ShapeDtypeStruct((keys, width), BF16)
    return call(
        functools.partial(project_kernel, count, rows // 2, rows),
        "project",
        keys * depth * width * 5,
        keys * depth * 2,
        out_shape=(jax.ShapeDtypeStruct((rows, width), BF16), wide, wide),
        in_specs=[whole()] * (2 * count + 3),
        out_specs=[whole()] * 3,
    )(*blocks, weights, cos, sin)


def place_kernel(fsdp, *refs):
    blocks, out_ref = refs[:-1], refs[-1]
    part, columns = blocks[0].shape[1:]
    me = lax.axis_index("fsdp")
    for i, block in enumerate(blocks):
        at = pl.multiple_of((me + i % fsdp) % fsdp * columns, LANES)
        first = i // fsdp * part
        out_ref[:, first : first + part, pl.ds(at, columns)] = block[...]


def place_weights(blocks, fsdp):
    kinds, part, columns = blocks[0].shape
    shape = (kinds, 2 * part, fsdp * columns)
    return call(
        functools.partial(place_kernel, fsdp),
        "place_weights",
        0,
        kinds * part * fsdp * columns * 8,
        out_shape=jax.ShapeDtypeStruct(shape, BF16),
        in_specs=[whole()] * len(blocks),
        out_specs=whole(),
    )(*blocks)


def out_kernel(half, count, o_ref, weight_ref, kept_ref, sent_ref):
    block = 2 * half // count
    for i in range(count):
        at = pl.multiple_of(block_offset(i, half), 16)
        part = dot(o_ref[pl.ds(at, block), :], weight_ref[3])
        if i < count // 2:
            kept_ref[i * block : (i + 1) * block, :] = part
        else:
            sent_ref[i * block - half : (i + 1) * block - half, :] = part.astype(BF16)


def out_project(attended, weights, count):
    rows, width = attended.shape
    depth = weights.shape[2]
    half = rows // 2
    return call(
        functools.partial(out_kernel, half, count),
        "out_project",
        rows * width * depth * 2,
        rows * depth * 3,
        out_shape=(jax.ShapeDtypeStruct((half, depth), F32), jax.ShapeDtypeStruct((half, depth), BF16)),
        in_specs=[whole(), whole()],
        out_specs=[whole(), whole()],
    )(attended, weights)


def out_back_kernel(half, count, fsdp, o_ref, weight_ref, *refs):
    blocks, (grad_ref, own_ref, other_ref, chip_rows) = refs[:count], refs[count:]
    block = 2 * half // count
    for i in range(count):
        at = pl.multiple_of(block_offset(i, half), 16)
        grad = blocks[i][...]
        grad_ref[pl.ds(at, block), :] = dot_nt(grad, weight_ref[3]).astype(BF16)
        chip_rows[pl.ds(at, block), :] = grad
    total = dot_tn(o_ref[...], chip_rows[...])
    part, columns = own_ref.shape[1], own_ref.shape[2]
    for z in range(fsdp):
        own_ref[z] = total[:part, z * columns : (z + 1) * columns].astype(BF16)
        other_ref[z] = total[part:, z * columns : (z + 1) * columns].astype(BF16)


def out_back(attended, weights, blocks, fsdp):
    rows, width = attended.shape
    depth = weights.shape[2]
    grads = jax.ShapeDtypeStruct((fsdp, width // 2, depth // fsdp), BF16)
    return call(
        functools.partial(out_back_kernel, rows // 2, len(blocks), fsdp),
        "out_back",
        rows * width * depth * 4,
        rows * depth * 3,
        out_shape=(jax.ShapeDtypeStruct((rows, width), BF16), grads, grads),
        in_specs=[whole()] * (2 + len(blocks)),
        out_specs=[whole()] * 3,
        scratch_shapes=[pltpu.VMEM((rows, depth), BF16)],
    )(attended, weights, *blocks)


def project_weights_kernel(count, half, base, dq_ref, dk_ref, dv_ref, *refs):
    blocks, out_refs, window = refs[: 2 * count], refs[2 * count : -1], refs[-1]
    window[2 * base :, :] = jnp.zeros((window.shape[0] - 2 * base, window.shape[1]), BF16)
    for block, span in zip(blocks, block_spans(count, half, base)):
        window[span, :] = block[...]
    part = out_refs[0].shape[1]
    results = (
        dot_tn(dv_ref[...], window[...]),
        dot_tn(dk_ref[...], window[...]),
        dot_tn(dq_ref[...], window[base : 2 * base, :]),
    )
    for i, result in enumerate(results):
        out_refs[2 * i][0] = result[:part].astype(BF16)
        out_refs[2 * i + 1][0] = result[part:].astype(BF16)


def project_weights(dq, dk, dv, blocks, fsdp):
    keys, width = dk.shape
    rows = dq.shape[0]
    block, depth = blocks[0].shape
    count = len(blocks) // 2
    columns = depth // fsdp
    fixed = lambda array: pl.BlockSpec(array.shape, lambda z: (0, 0))
    return call(
        functools.partial(project_weights_kernel, count, rows // 2, rows),
        "project_weights",
        keys * width * depth * 5,
        keys * depth * 2,
        grid=(fsdp,),
        out_shape=[jax.ShapeDtypeStruct((fsdp, width // 2, columns), BF16)] * 6,
        in_specs=[fixed(dq), fixed(dk), fixed(dv)] + [pl.BlockSpec((block, columns), lambda z: (0, z))] * (2 * count),
        out_specs=[pl.BlockSpec((1, width // 2, columns), lambda z: (z, 0, 0))] * 6,
        scratch_shapes=[pltpu.VMEM((keys, columns), BF16)],
    )(dq, dk, dv, *blocks)


def project_back_kernel(half, count, base, dq_ref, dk_ref, dv_ref, weight_ref, *out_refs):
    block = 2 * half // count
    for part in range(2):
        kept_ref, sent_ref = out_refs[2 * part : 2 * part + 2]
        for i in range(count):
            at = pl.multiple_of(block_offset(i, half), 16)
            where = pl.ds(part * base + at, block)
            total = dot(dk_ref[where, :], weight_ref[1]) + dot(dv_ref[where, :], weight_ref[2])
            if part == 1:
                total = total + dot(dq_ref[pl.ds(at, block), :], weight_ref[0])
            if i < count // 2:
                kept_ref[i * block : (i + 1) * block, :] = total
            else:
                sent_ref[i * block - half : (i + 1) * block - half, :] = total.astype(BF16)


def project_back(dq, dk, dv, weights, base, count):
    rows, width = dq.shape
    depth = weights.shape[2]
    half = rows // 2
    kept, sent = jax.ShapeDtypeStruct((half, depth), F32), jax.ShapeDtypeStruct((half, depth), BF16)
    return call(
        functools.partial(project_back_kernel, half, count, base),
        "project_back",
        rows * width * depth * 10,
        rows * depth * 6,
        out_shape=(kept, sent, kept, sent),
        in_specs=[whole()] * 4,
        out_specs=[whole()] * 4,
    )(dq, dk, dv, weights)


def lane_half(head):
    return (lax.broadcasted_iota(jnp.int32, (1, LANES), 1) // HEAD_DIM) == head % 2


def forward_kernel(rows, base, bounds, q_ref, k_ref, v_ref, start_ref, o_ref, lse_ref, q_buf, s_buf, top_buf, sum_buf, acc_buf):
    heads = q_buf.shape[0]
    zero = jnp.zeros((), BF16)
    for t in range(-(-rows // TILE)):
        low, high = bounds[0, t], bounds[1, t]
        n = min(TILE, rows - t * TILE)
        span = slice(t * TILE, (t + 1) * TILE)
        start = start_ref[:, span]
        row = base + t * TILE + lax.broadcasted_iota(jnp.int32, (1, TILE), 1)
        for h in range(heads):
            c = (h // 2) * LANES
            scaled = (q_ref[t * TILE : t * TILE + n, c : c + LANES].astype(F32) * HEAD_DIM**-0.5).astype(BF16)
            q_buf[h, :n, :] = jnp.where(lane_half(h), scaled, zero)
            if n < TILE:
                q_buf[h, n:, :] = jnp.zeros((TILE - n, LANES), BF16)
        top_buf[...] = jnp.full_like(top_buf, MASKED)
        sum_buf[...] = jnp.zeros_like(sum_buf)
        acc_buf[...] = jnp.zeros_like(acc_buf)

        @pl.loop(low, high)
        def _(i):
            at = pl.multiple_of(i * TILE, TILE)
            place = at + lax.broadcasted_iota(jnp.int32, (TILE, TILE), 0)
            allowed = (place >= start) & (place <= row)
            for h in range(heads):
                c = (h // 2) * LANES
                s = jnp.where(allowed, dot_nt(k_ref[pl.ds(at, TILE), c : c + LANES], q_buf[h]), MASKED)
                s_buf[h, pl.ds(at, TILE), :] = s
                top_buf[h] = jnp.maximum(top_buf[h], jnp.max(s.reshape(TILE // 8, 8, TILE), axis=0))

        tops = [jnp.max(top_buf[h], axis=0, keepdims=True) for h in range(heads)]

        @pl.loop(low, high)
        def _(i):
            at = pl.multiple_of(i * TILE, TILE)
            for h in range(heads):
                c = (h // 2) * LANES
                p = jnp.exp(s_buf[h, pl.ds(at, TILE), :] - tops[h])
                sum_buf[h] += jnp.sum(p.reshape(TILE // 8, 8, TILE), axis=0)
                both = dot_tn(v_ref[pl.ds(at, TILE), c : c + LANES], p.astype(BF16))
                acc_buf[h] += both[HEAD_DIM * (h % 2) : HEAD_DIM * (h % 2) + HEAD_DIM]

        for h in range(heads):
            total = jnp.sum(sum_buf[h], axis=0, keepdims=True)
            lse_ref[h : h + 1, span] = tops[h] + jnp.log(total)
            acc_buf[h] = acc_buf[h] / total
        for pair in range(heads // 2):
            o = jnp.transpose(jnp.concatenate([acc_buf[2 * pair], acc_buf[2 * pair + 1]], axis=0))
            o_ref[t * TILE : t * TILE + n, pair * LANES : (pair + 1) * LANES] = o[:n].astype(BF16)


def attend(bounds, q, k, v, start, rows, base):
    keys, width = k.shape
    heads = width // HEAD_DIM
    padded = -(-rows // TILE) * TILE
    return call(
        functools.partial(forward_kernel, rows, base),
        "attend",
        rows * rows * width * 8,
        keys * width * 8,
        out_shape=(jax.ShapeDtypeStruct((rows, width), BF16), jax.ShapeDtypeStruct((heads, padded), F32)),
        in_specs=[pl.BlockSpec(memory_space=pltpu.SMEM)] + [whole()] * 4,
        out_specs=[whole(), whole()],
        scratch_shapes=[
            pltpu.VMEM((heads, TILE, LANES), BF16),
            pltpu.VMEM((heads, keys, TILE), F32),
            pltpu.VMEM((heads, 8, TILE), F32),
            pltpu.VMEM((heads, 8, TILE), F32),
            pltpu.VMEM((heads, HEAD_DIM, TILE), F32),
        ],
    )(bounds, q, k, v, start)


def backward_kernel(
    rows, base, bounds, q_ref, k_ref, v_ref, o_ref, g_ref, lse_ref, start_ref, cos_ref, sin_ref,
    dq_ref, dk_ref, dv_ref, q_buf, g_buf, d_buf, dq_acc, dk_acc, dv_acc,
):
    heads = q_buf.shape[0]
    zero = jnp.zeros((), BF16)
    scale = HEAD_DIM**-0.5
    dk_acc[...] = jnp.zeros_like(dk_acc)
    dv_acc[...] = jnp.zeros_like(dv_acc)
    for t in range(-(-rows // TILE)):
        low, high = bounds[0, t], bounds[1, t]
        n = min(TILE, rows - t * TILE)
        span = slice(t * TILE, (t + 1) * TILE)
        here = slice(t * TILE, t * TILE + n)
        window = slice(base + t * TILE, base + t * TILE + n)
        start = start_ref[:, span]
        row = base + t * TILE + lax.broadcasted_iota(jnp.int32, (1, TILE), 1)
        for pair in range(heads // 2):
            c = pair * LANES
            scaled = (q_ref[here, c : c + LANES].astype(F32) * scale).astype(BF16)
            grad = g_ref[here, c : c + LANES]
            product = grad.astype(F32) * o_ref[here, c : c + LANES].astype(F32)
            if n < TILE:
                product = jnp.concatenate([product, jnp.zeros((TILE - n, LANES), F32)], axis=0)
            product = jnp.transpose(product)
            for h in (2 * pair, 2 * pair + 1):
                q_buf[h, :n, :] = jnp.where(lane_half(h), scaled, zero)
                g_buf[h, :n, :] = jnp.where(lane_half(h), grad, zero)
                if n < TILE:
                    q_buf[h, n:, :] = jnp.zeros((TILE - n, LANES), BF16)
                    g_buf[h, n:, :] = jnp.zeros((TILE - n, LANES), BF16)
                d_buf[h : h + 1, :] = jnp.sum(product[HEAD_DIM * (h % 2) : HEAD_DIM * (h % 2) + HEAD_DIM], axis=0, keepdims=True)
        dq_acc[...] = jnp.zeros_like(dq_acc)

        @pl.loop(low, high)
        def _(i):
            at = pl.multiple_of(i * TILE, TILE)
            place = at + lax.broadcasted_iota(jnp.int32, (TILE, TILE), 0)
            allowed = (place >= start) & (place <= row)
            for pair in range(heads // 2):
                c = pair * LANES
                k = k_ref[pl.ds(at, TILE), c : c + LANES]
                v = v_ref[pl.ds(at, TILE), c : c + LANES]
                dq = dk = dv = 0.0
                for h in (2 * pair, 2 * pair + 1):
                    p = jnp.where(allowed, jnp.exp(dot_nt(k, q_buf[h]) - lse_ref[h : h + 1, span]), 0.0)
                    ds = (p * (dot_nt(v, g_buf[h]) - d_buf[h : h + 1, :])).astype(BF16)
                    dv = dv + dot(p.astype(BF16), g_buf[h])
                    dk = dk + dot(ds, q_buf[h])
                    dq = dq + dot_tn(ds, jnp.where(lane_half(h), k, zero))
                dk_acc[pl.ds(at, TILE), c : c + LANES] += dk
                dv_acc[pl.ds(at, TILE), c : c + LANES] += dv
                dq_acc[:, c : c + LANES] += dq

        for c in range(0, heads * HEAD_DIM, LANES):
            dq = dq_acc[:n, c : c + LANES] * scale
            dq_ref[here, c : c + LANES] = turn(dq, cos_ref[window, :], sin_ref[window, :], -1.0).astype(BF16)
    for c in range(0, heads * HEAD_DIM, LANES):
        dk_ref[:, c : c + LANES] = turn(dk_acc[:, c : c + LANES], cos_ref[...], sin_ref[...], -1.0).astype(BF16)
    dv_ref[...] = dv_acc[...].astype(BF16)


def attend_back(bounds, q, k, v, o, grad, lse, start, cos, sin, rows, base):
    keys, width = k.shape
    heads = width // HEAD_DIM
    wide = jax.ShapeDtypeStruct((keys, width), BF16)
    return call(
        functools.partial(backward_kernel, rows, base),
        "attend_back",
        rows * rows * width * 20,
        keys * width * 16,
        out_shape=(jax.ShapeDtypeStruct((rows, width), BF16), wide, wide),
        in_specs=[pl.BlockSpec(memory_space=pltpu.SMEM)] + [whole()] * 9,
        out_specs=[whole()] * 3,
        scratch_shapes=[
            pltpu.VMEM((heads, TILE, LANES), BF16),
            pltpu.VMEM((heads, TILE, LANES), BF16),
            pltpu.VMEM((heads, TILE), F32),
            pltpu.VMEM((TILE, width), F32),
            pltpu.VMEM((keys, width), F32),
            pltpu.VMEM((keys, width), F32),
        ],
    )(bounds, q, k, v, o, grad, lse, start, cos, sin)


def joined(ref):
    shape = ref.shape
    return ref[...].reshape(shape[0] * shape[3], shape[4])


def feed_kernel(count, *refs):
    n_refs, dy_refs, weights = refs[:count], refs[count : 2 * count], refs[2 * count : 2 * count + 3]
    hidden_ref, gate_ref, up_ref, kept_ref, sent_ref, acc = refs[2 * count + 3 :]
    step = pl.program_id(0)
    block = n_refs[0].shape[0]
    half = kept_ref.shape[0]

    @pl.when(step == 0)
    def _():
        acc[...] = jnp.zeros_like(acc)

    gate_w, up_w, down_w = (joined(ref) for ref in weights)
    for i in range(count):
        rows = slice(i * block, (i + 1) * block)
        normed = n_refs[i][...]
        gate = dot(normed, gate_w)
        up = dot(normed, up_w)
        grad = dot(dy_refs[i][...], down_w)
        sig = 1.0 / (1.0 + jnp.exp(-gate))
        silu = gate * sig
        hidden_ref[rows, :] = (silu * up).astype(BF16)
        gate_grad = (grad * up * sig * (1.0 + gate * (1.0 - sig))).astype(BF16)
        up_grad = (grad * silu).astype(BF16)
        gate_ref[rows, :] = gate_grad
        up_ref[rows, :] = up_grad
        acc[rows, :] += dot_nt(gate_grad, gate_w) + dot_nt(up_grad, up_w)

    @pl.when(step == pl.num_programs(0) - 1)
    def _():
        kept_ref[...] = acc[:half, :]
        sent_ref[...] = acc[half:, :].astype(BF16)


def feed(normed, dy, weights):
    count = len(normed)
    block, depth = normed[0].shape
    rows = count * block
    fsdp, chips, _, columns, units = weights.shape
    tile = min(TILE, units)
    steps = units // tile
    fixed = pl.BlockSpec((block, depth), lambda i: (0, 0))
    kept = pl.BlockSpec((rows // 2, depth), lambda i: (0, 0))
    kind = lambda k: pl.BlockSpec((fsdp, 1, 1, columns, tile), lambda i: (0, i // steps, k, 0, i % steps))
    out = pl.BlockSpec((rows, tile), lambda i: (0, i))
    wide = jax.ShapeDtypeStruct((rows, chips * units), BF16)
    return call(
        functools.partial(feed_kernel, count),
        "feed",
        rows * depth * units * 20,
        depth * units * 12,
        grid=(chips * steps,),
        out_shape=(wide, wide, wide, jax.ShapeDtypeStruct((rows // 2, depth), F32), jax.ShapeDtypeStruct((rows // 2, depth), BF16)),
        in_specs=[fixed] * (2 * count) + [kind(0), kind(1), kind(2)],
        out_specs=[out, out, out, kept, kept],
        scratch_shapes=[pltpu.VMEM((rows, depth), F32)],
    )(*normed, *dy, weights, weights, weights)


def feed_weights_kernel(count, *refs):
    blocks = refs[: 2 * count]
    hidden_ref, gate_ref, up_ref, out_ref, normed, dy = refs[2 * count :]
    block = blocks[0].shape[0]
    fsdp, _, _, columns, tile = out_ref.shape

    @pl.when(pl.program_id(0) == 0)
    def _():
        for i in range(count):
            normed[i * block : (i + 1) * block, :] = blocks[i][...]
            dy[i * block : (i + 1) * block, :] = blocks[count + i][...]

    for k, (left, right) in enumerate(((normed, gate_ref), (normed, up_ref), (dy, hidden_ref))):
        out_ref[:, 0, k] = dot_tn(left[...], right[...]).astype(BF16).reshape(fsdp, columns, tile)


def feed_weights(normed, dy, hidden, gate_grad, up_grad, fsdp, chips):
    count = len(normed)
    block, depth = normed[0].shape
    rows = count * block
    units = hidden.shape[1] // chips
    columns = depth // fsdp
    tile = min(TILE, units)
    steps = units // tile
    fixed = pl.BlockSpec((block, depth), lambda i: (0, 0))
    units_in = pl.BlockSpec((rows, tile), lambda i: (0, i))
    return call(
        functools.partial(feed_weights_kernel, count),
        "feed_weights",
        rows * depth * units * 12,
        depth * units * 12,
        grid=(chips * steps,),
        out_shape=jax.ShapeDtypeStruct((fsdp, chips, 3, columns, units), BF16),
        in_specs=[fixed] * (2 * count) + [units_in] * 3,
        out_specs=pl.BlockSpec((fsdp, 1, 3, columns, tile), lambda i: (0, i // steps, 0, 0, i % steps)),
        scratch_shapes=[pltpu.VMEM((rows, depth), BF16)] * 2,
    )(*normed, *dy, hidden, gate_grad, up_grad)


def feed_out_kernel(hidden_ref, weight_ref, kept_ref, sent_ref, acc):
    step = pl.program_id(0)
    half = kept_ref.shape[0]
    weight = joined(weight_ref)

    @pl.when(step == 0)
    def _():
        acc[...] = dot_nt(hidden_ref[...], weight)

    @pl.when(step > 0)
    def _():
        acc[...] += dot_nt(hidden_ref[...], weight)

    @pl.when(step == pl.num_programs(0) - 1)
    def _():
        kept_ref[...] = acc[:half, :]
        sent_ref[...] = acc[half:, :].astype(BF16)


def feed_out(hidden, weights):
    rows = hidden.shape[0]
    fsdp, chips, _, columns, units = weights.shape
    depth = fsdp * columns
    half = rows // 2
    out = pl.BlockSpec((half, depth), lambda i: (0, 0))
    return call(
        feed_out_kernel,
        "feed_out",
        rows * depth * units * 4,
        rows * depth * 3,
        grid=(chips,),
        out_shape=(jax.ShapeDtypeStruct((half, depth), F32), jax.ShapeDtypeStruct((half, depth), BF16)),
        in_specs=[
            pl.BlockSpec((rows, units), lambda i: (0, i)),
            pl.BlockSpec((fsdp, 1, 1, columns, units), lambda i: (0, i, 2, 0, 0)),
        ],
        out_specs=[out, out],
        scratch_shapes=[pltpu.VMEM((rows, depth), F32)],
    )(hidden, weights)


def quarter_places():
    place = 2 * lax.axis_index("chip") + lax.axis_index("core")
    return place, place ^ 2, place ^ 1, place ^ 3


def finish_feed_kernel(own_ref, across_ref, came_ref, gate_ref, up_ref, down_ref):
    units = own_ref.shape[2]
    for place, piece in zip(quarter_places(), (own_ref, across_ref, came_ref.at[0], came_ref.at[1])):
        span = pl.ds(pl.multiple_of(place * units, LANES), units)
        gate_ref[:, span] = piece[0].astype(F32)
        up_ref[:, span] = piece[1].astype(F32)
        down_ref[span, :] = jnp.transpose(piece[2].astype(F32))


def finish_feed(own, across, came):
    _, columns, units = own.shape
    wide = jax.ShapeDtypeStruct((columns, 4 * units), F32)
    return call(
        finish_feed_kernel,
        "finish_feed",
        0,
        own.size * 24,
        out_shape=(wide, wide, jax.ShapeDtypeStruct((4 * units, columns), F32)),
        in_specs=[whole()] * 3,
        out_specs=[whole()] * 3,
    )(own, across, came)


def finish_attention_kernel(real, own_ref, across_ref, came_ref, q_ref, k_ref, v_ref, out_ref, buf):
    part = own_ref.shape[1]
    pieces = (own_ref, across_ref, came_ref.at[0], came_ref.at[1])
    for kind, ref in enumerate((q_ref, k_ref, v_ref, out_ref)):
        for place, piece in zip(quarter_places(), pieces):
            buf[pl.ds(pl.multiple_of(place * part, 16), part), :] = piece[kind].astype(F32)
        ref[...] = buf[:real, :] if kind == 3 else jnp.transpose(buf[...])[:, :real]


def finish_attention(own, across, came, real):
    _, part, columns = own.shape
    into = jax.ShapeDtypeStruct((columns, real), F32)
    return call(
        functools.partial(finish_attention_kernel, real),
        "finish_attention",
        0,
        own.size * 24,
        out_shape=(into, into, into, jax.ShapeDtypeStruct((real, columns), F32)),
        in_specs=[whole()] * 3,
        out_specs=[whole()] * 4,
        scratch_shapes=[pltpu.VMEM((4 * part, columns), F32)],
    )(own, across, came)


def normalize_back(values, inverse, gain, grad_rows):
    scaled = grad_rows * gain
    return inverse * scaled - values * inverse**3 * jnp.mean(scaled * values, axis=-1, keepdims=True)


def inverse_rms(values):
    return lax.rsqrt(jnp.mean(values * values, axis=-1, keepdims=True) + EPSILON)


def pull_fsdp(values, step):
    count = lax.axis_size("fsdp")
    return lax.ppermute(values, "fsdp", [(i, (i - step) % count) for i in range(count)])


def gather_gains(gains):
    count = lax.axis_size("fsdp")
    rolled = jnp.concatenate([gains] + [pull_fsdp(gains, step) for step in range(1, count)], axis=1).astype(F32)
    twice = jnp.concatenate([rolled, rolled], axis=1)
    at = (count - lax.axis_index("fsdp")) % count * gains.shape[1]
    return lax.dynamic_slice_in_dim(twice, at, rolled.shape[1], 1)


def gain_totals(gains):
    if lax.axis_size("tp") == 2:
        gains = gains + swap_tp(gains)
    else:
        gains = lax.psum(gains, "tp")
    gains = gains + swap_core(gains)
    gains = gains + swap_chip(gains)
    count = lax.axis_size("fsdp")
    blocks = jnp.stack(jnp.split(gains, count, axis=1))
    return jnp.sum(lax.all_to_all(blocks, "fsdp", 0, 0, tiled=True), axis=0)


def sum_over_chips_and_fsdp(own, other):
    mine = add_low(own, swap_chip(other))
    return jnp.sum(lax.all_to_all(mine, "fsdp", 0, 0, tiled=True).astype(F32), axis=0).astype(BF16)


def together(*values):
    return lax.optimization_barrier(values)


def shards(tokens, segment_ids, wq, wk, wv, wo, w_gate, w_up, w_down, gain_attn, gain_ffn, cotangent):
    tokens, cotangent, segment_ids = tokens[0], cotangent[0], segment_ids[0]
    fsdp = lax.axis_size("fsdp")
    chips = lax.axis_size("chip")
    chip, core = lax.axis_index("chip"), lax.axis_index("core")
    place = 2 * chip + core
    half = segment_ids.shape[0]
    rows = 2 * half
    real_width = wq.shape[1]
    columns, depth = wq.shape[0], wq.shape[0] * fsdp
    width = -(-real_width // (4 * HEAD_DIM)) * 4 * HEAD_DIM
    part = width // 4
    keys = -(-2 * rows // TILE) * TILE
    base = rows

    pad = ((0, 0), (0, width - real_width))
    wide = [jnp.pad(w, pad) for w in (wq, wk, wv)] + [jnp.pad(wo, pad[::-1])]

    def attention_piece(index):
        pieces = [jnp.transpose(take_quarter(w, index, 1)) for w in wide[:3]]
        return jnp.stack(pieces + [take_quarter(wide[3], index, 0)])

    feed_piece = jnp.stack([take_quarter(w_gate, place, 1), take_quarter(w_up, place, 1), jnp.transpose(take_quarter(w_down, place, 0))])

    ring, crossed = [attention_piece(place)], [attention_piece(place ^ 2)]
    gain_one, gain_two = gather_gains(jnp.stack([gain_attn, gain_ffn]))
    ids_other = swap_core(segment_ids)
    block, own, before = together(pull_fsdp(ring[0], 1), widen_tp(tokens), to_later_chip(tokens))
    ring.append(block)
    ids_own = jnp.concatenate(in_order(segment_ids, ids_other, core == 0))
    ids_before = jnp.where(chip > 0, to_later_chip(ids_own), -1)
    block, over, before, own = together(pull_fsdp(ring[-1], 1), swap_chip(ring[-1]), widen_tp(before), widen_core(own))
    ring.append(block)
    crossed.append(over)
    feed_weight = lax.all_gather(after(feed_piece, block), ("fsdp", "chip"), axis=0, tiled=False)
    feed_weight = feed_weight.reshape((fsdp, chips) + feed_piece.shape)
    dy = cotangent
    for step in range(2, fsdp - 1):
        moves = [pull_fsdp(ring[-1], 1), swap_chip(ring[-1])]
        if step == 2:
            moves += [widen_core(before), widen_tp(after(cotangent, block))]
        moves = together(*moves)
        ring.append(moves[0])
        crossed.append(moves[1])
        if step == 2:
            before, dy = moves[2], moves[3]
    crossed.append(swap_chip(ring[-1]))
    dy = widen_core(dy)
    weights = place_weights(ring + crossed, fsdp)

    def normed(values):
        values = values.astype(F32)
        return (values * inverse_rms(values) * gain_one).astype(BF16)

    blocks = [normed(values) for values in before + own]
    count = len(own)
    position = (chip * rows - rows + jnp.arange(keys, dtype=jnp.int32)).astype(F32)
    pair_index = (jnp.arange(LANES, dtype=jnp.int32) % (HEAD_DIM // 2)).astype(F32)
    angles = position[:, None] * (10000.0 ** (-pair_index * 2.0 / HEAD_DIM))[None, :]
    cos, sin = jnp.cos(angles), jnp.sin(angles)
    ids = jnp.concatenate([ids_before, ids_own])
    start = jnp.sum((ids[None, :] < ids_own[:, None]).astype(jnp.int32), axis=1)
    tiles = -(-rows // TILE)
    ends = [-(-min(base + (t + 1) * TILE, base + rows) // TILE) for t in range(tiles)]
    bounds = jnp.stack([start[::TILE] // TILE, jnp.array(ends, jnp.int32)])
    start = jnp.pad(start, (0, tiles * TILE - rows), constant_values=2 * keys)[None]

    inputs = tokens.astype(F32)
    inv_one = inverse_rms(inputs)
    q, k, v = project(blocks, weights, cos, sin, keys)
    attended, lse = attend(bounds, q, after(k, *dy), v, start, rows, base)
    attn_out, _ = narrow_chip(*out_project(attended, weights, count))
    residual = inputs + attn_out

    inv_two = inverse_rms(residual)
    normed_two = widen_chip((residual * inv_two * gain_two).astype(BF16))
    hidden, gate_grad, up_grad, kept, sent = feed(normed_two, dy, feed_weight)
    normed_two_grad, came = narrow_chip(kept, sent)
    feed_grads = feed_weights(normed_two, dy, after(hidden, came), gate_grad, up_grad, fsdp, chips)
    feed_sums = lax.psum_scatter(
        feed_grads.reshape((fsdp * chips,) + feed_piece.shape), ("fsdp", "chip"), scatter_dimension=0, tiled=True
    )[0]
    gain_two_grad = jnp.sum(normed_two_grad * residual * inv_two, axis=0)
    resid_grad = cotangent.astype(F32) + normalize_back(residual, inv_two, gain_two, normed_two_grad)
    resid_low = resid_grad.astype(BF16)

    grad_blocks = widen_chip(resid_low)
    out_grad, out_own, out_other = out_back(attended, weights, grad_blocks, fsdp)
    dq, dk, dv = attend_back(bounds, q, k, v, attended, out_grad, lse, start, cos, sin, rows, base)
    out_sum = sum_over_chips_and_fsdp(out_own, out_other)
    v_own, v_other, k_own, k_other, q_own, q_other = project_weights(dq, dk, dv, blocks, fsdp)
    v_sum, k_sum, q_sum = (
        sum_over_chips_and_fsdp(*pair) for pair in ((v_own, v_other), (k_own, k_other), (q_own, q_other))
    )
    early_kept, early_sent, kept, sent = project_back(dq, dk, dv, weights, base, count)
    earlier_back = to_earlier_chip(narrow_chip(early_kept, early_sent)[0].astype(BF16)).astype(F32)
    normed_grad = narrow_chip(kept, sent)[0] + earlier_back
    gain_one_grad = jnp.sum(normed_grad * inputs * inv_one, axis=0)
    grad_input = resid_grad + normalize_back(inputs, inv_one, gain_one, normed_grad)
    kept, sent = feed_out(after(hidden, came), feed_weight)
    layer_out = residual + narrow_chip(kept, sent)[0]

    gate_all, up_all, down_all = finish_feed(*all_quarters(feed_sums))
    q_all, k_all, v_all, out_all = finish_attention(*all_quarters(jnp.stack([q_sum, k_sum, v_sum, out_sum])), real_width)
    gain_own = gain_totals(jnp.stack([gain_one_grad, gain_two_grad]))
    return (
        layer_out.astype(BF16)[None],
        grad_input[None],
        q_all,
        k_all,
        v_all,
        out_all,
        gate_all,
        up_all,
        down_all,
        gain_own[0],
        gain_own[1],
    )


def solution(mesh):
    devices = mesh.devices.reshape(mesh.shape["fsdp"], mesh.shape["ctx"] // 2, 2, mesh.shape["tp"])
    split = jax.sharding.Mesh(devices, ("fsdp", "chip", "core", "tp"))
    rows = P("fsdp", ("chip", "core", "tp"), None)
    into, outof, gain = P("fsdp", "tp"), P("tp", "fsdp"), P("fsdp")
    return jax.shard_map(
        shards,
        mesh=split,
        in_specs=(rows, P("fsdp", ("chip", "core")), into, into, into, outof, into, into, outof, gain, gain, rows),
        out_specs=(rows, rows, into, into, into, outof, into, into, outof, gain, gain),
        check_vma=False,
    )
```

```python
import functools

import jax
import jax.numpy as jnp
from jax import lax
from jax.experimental import pallas as pl
from jax.experimental.pallas import tpu as pltpu
from jax.sharding import PartitionSpec as P

HEAD_DIM = 64
EPSILON = 1e-05
MASKED = -1e30
BF16 = jnp.bfloat16
F32 = jnp.float32
TILE = 256
LANES = 128
VMEM_BYTES = 60 * 1024 * 1024


def dot(left, right):
    return jnp.dot(left, right, preferred_element_type=F32)


def dot_nt(left, right):
    return lax.dot_general(left, right, (((1,), (1,)), ((), ())), preferred_element_type=F32)


def dot_tn(left, right):
    return lax.dot_general(left, right, (((0,), (0,)), ((), ())), preferred_element_type=F32)


def swap_chip(values):
    return lax.ppermute(values, "chip", [(0, 1), (1, 0)])


def swap_core(values):
    return lax.ppermute(values, "core", [(0, 1), (1, 0)])


def swap_tp(values):
    return lax.ppermute(values, "tp", [(0, 1), (1, 0)])


def in_order(mine, other, mine_first):
    return [jnp.where(mine_first, mine, other), jnp.where(mine_first, other, mine)]


def together(*values):
    return lax.optimization_barrier(values)


def after(values, *earlier):
    return lax.optimization_barrier((values, earlier))[0]


def widen_planes(rows, meanwhile=None):
    if lax.axis_size("tp") != 2:
        gathered = lax.all_gather(rows, "tp", axis=0, tiled=True)
        return [gathered, swap_chip(gathered)]
    return far_block(rows, *meet(swap_tp(rows), swap_chip(rows), meanwhile))


def meet(beside, across, meanwhile):
    return (beside, across) if meanwhile is None else after((beside, across), meanwhile)


def far_block(rows, beside, across):
    cut = rows.shape[0] // 32 * 16
    far = jnp.concatenate([swap_tp(across[:cut]), swap_chip(beside[cut:])], axis=0)
    return [rows, beside, across, far]


def widen_core(blocks):
    return blocks + [swap_core(block) for block in blocks]


def widen(rows):
    return widen_core(widen_planes(rows))


def block_offset(index, half):
    chip, core = lax.axis_index("chip"), lax.axis_index("core")
    if lax.axis_size("tp") != 2:
        return (chip ^ index % 2) * 2 * half + (core ^ index // 2) * half
    place = lax.axis_index("tp")
    return (chip ^ index // 2 % 2) * 2 * half + (core ^ index // 4) * half + (place ^ index % 2) * (half // 2)


def narrow_first(kept, sent, meanwhile=None):
    came = swap_core(sent)
    if lax.axis_size("tp") != 2:
        rows = kept.shape[0] // 2
        total = kept.astype(F32) + came.astype(F32)
        return ((total[:rows] + swap_chip(total[rows:].astype(BF16)).astype(F32)).astype(BF16),)
    rows = kept.shape[0] // 4
    cut = rows // 32 * 16

    def block(index, first, last):
        where = slice(index * rows + first, index * rows + last)
        return kept[where].astype(F32) + came[where].astype(F32)

    top, bottom = meet(swap_chip(block(3, 0, cut).astype(BF16)), swap_tp(block(3, cut, rows).astype(BF16)), meanwhile)
    beside = jnp.concatenate([block(1, 0, cut) + top.astype(F32), block(1, cut, rows)], axis=0).astype(BF16)
    across = jnp.concatenate([block(2, 0, cut), block(2, cut, rows) + bottom.astype(F32)], axis=0).astype(BF16)
    return beside, across, block(0, 0, rows)


def narrow_second(leaving, meanwhile=None):
    done = None
    if len(leaving) == 1:
        if meanwhile is not None:
            done = meanwhile(leaving)
        return lax.psum_scatter(leaving[0], "tp", scatter_dimension=0, tiled=True).astype(F32), done
    from_tp, from_chip = swap_tp(leaving[0]), swap_chip(leaving[1])
    if meanwhile is not None:
        (from_tp, from_chip), done = together((from_tp, from_chip), meanwhile(leaving[:2]))
    return leaving[2] + from_tp.astype(F32) + from_chip.astype(F32), done


def narrow(kept, sent, meanwhile=None):
    return narrow_second(narrow_first(kept, sent), meanwhile)


def take_quarter(values, index, axis):
    size = values.shape[axis] // 4
    return lax.dynamic_slice_in_dim(values, index * size, size, axis)


def all_quarters(own):
    across = swap_chip(own)
    return own, across, swap_core(jnp.stack([own, across]))


def call(kernel, name, flops, moved, **rest):
    return pl.pallas_call(
        kernel,
        name=name,
        cost_estimate=pl.CostEstimate(flops=flops, bytes_accessed=moved, transcendentals=0),
        compiler_params=pltpu.CompilerParams(vmem_limit_bytes=VMEM_BYTES),
        **rest,
    )


def whole():
    return pl.BlockSpec(memory_space=pltpu.VMEM)


def turn(values, cos, sin, direction):
    lane = lax.broadcasted_iota(jnp.int32, (1, LANES), 1)
    partner = jnp.where((lane // 32) % 2 == 0, pltpu.roll(values, 96, 1) * -direction, pltpu.roll(values, 32, 1) * direction)
    return values * cos + partner * sin


def block_spans(count, rows):
    block = rows // count
    return [pl.ds(pl.multiple_of(block_offset(i, rows // 4), 16), block) for i in range(count)]


def project_kernel(count, rows, *refs):
    blocks = refs[:count]
    weight_ref, cos_ref, sin_ref, q_ref, k_ref, v_ref = refs[count:]
    width = q_ref.shape[1]
    for ref in (k_ref, v_ref):
        ref[rows:, :] = jnp.zeros((ref.shape[0] - rows, width), BF16)
    for block, span in zip(blocks, block_spans(count, rows)):
        cos, sin = cos_ref[span, :], sin_ref[span, :]
        for kind, out_ref in ((0, q_ref), (1, k_ref)):
            values = dot_nt(block[...], weight_ref[kind])
            for c in range(0, width, LANES):
                out_ref[span, c : c + LANES] = turn(values[:, c : c + LANES], cos, sin, 1.0).astype(BF16)
        v_ref[span, :] = dot_nt(block[...], weight_ref[2]).astype(BF16)


def project(blocks, weights, cos, sin, keys):
    count = len(blocks)
    block, depth = blocks[0].shape
    rows = count * block
    width = weights.shape[1]
    tall = jax.ShapeDtypeStruct((keys, width), BF16)
    return call(
        functools.partial(project_kernel, count, rows),
        "project",
        rows * depth * width * 6,
        rows * depth * 2,
        out_shape=(jax.ShapeDtypeStruct((rows, width), BF16), tall, tall),
        in_specs=[whole()] * (count + 3),
        out_specs=[whole()] * 3,
    )(*blocks, weights, cos, sin)


def cut_kernel(q_ref, k_ref, v_ref, out_ref, piece_ref, buf):
    part = piece_ref.shape[1]
    span = pl.ds(pl.multiple_of(quarter_places()[0] * part, 16), part)
    for kind, ref in enumerate((q_ref, k_ref, v_ref)):
        buf[...] = jnp.transpose(ref[...])
        piece_ref[kind] = buf[span, :]
    piece_ref[3] = out_ref[span, :]


def cut_attention(wq, wk, wv, wo):
    width, columns = wo.shape
    return call(
        cut_kernel,
        "cut_attention",
        0,
        width * columns * 8,
        out_shape=jax.ShapeDtypeStruct((4, width // 4, columns), BF16),
        in_specs=[whole()] * 4,
        out_specs=whole(),
        scratch_shapes=[pltpu.VMEM((width, columns), BF16)],
    )(wq, wk, wv, wo)


def place_kernel(*refs):
    blocks, out_ref = refs[:-1], refs[-1]
    kinds, part, columns = blocks[0].shape
    me = lax.axis_index("fsdp")
    if part < out_ref.shape[1]:
        out_ref[:, part:, :] = jnp.zeros((kinds, out_ref.shape[1] - part, out_ref.shape[2]), BF16)
    for i, block in enumerate(blocks):
        at = pl.multiple_of((me + i) % len(blocks) * columns, LANES)
        out_ref[:, :part, pl.ds(at, columns)] = block[...]


def place_weights(blocks, width):
    kinds, _, columns = blocks[0].shape
    depth = len(blocks) * columns
    return call(
        place_kernel,
        "place_weights",
        0,
        kinds * width * depth * 4,
        out_shape=jax.ShapeDtypeStruct((kinds, width, depth), BF16),
        in_specs=[whole()] * len(blocks),
        out_specs=whole(),
    )(*blocks)


def store_block(kept_ref, sent_ref, i, block, values):
    half = kept_ref.shape[0]
    at = i * block
    if at < half:
        kept_ref[at : at + block, :] = values.astype(BF16)
    else:
        sent_ref[at - half : at - half + block, :] = values.astype(BF16)


def halves(rows, depth):
    return [jax.ShapeDtypeStruct((rows // 2, depth), BF16)] * 2


def out_kernel(count, o_ref, weight_ref, kept_ref, sent_ref):
    rows = o_ref.shape[0]
    for i, span in enumerate(block_spans(count, rows)):
        store_block(kept_ref, sent_ref, i, rows // count, dot(o_ref[span, :], weight_ref[3]))


def out_project(attended, weights, count):
    rows, width = attended.shape
    depth = weights.shape[2]
    return call(
        functools.partial(out_kernel, count),
        "out_project",
        rows * width * depth * 2,
        rows * depth * 2,
        out_shape=halves(rows, depth),
        in_specs=[whole(), whole()],
        out_specs=[whole(), whole()],
    )(attended, weights)


def out_back_kernel(count, o_ref, weight_ref, *refs):
    blocks, (grad_ref, out_ref, all_rows) = refs[:count], refs[count:]
    rows = o_ref.shape[0]
    for block, span in zip(blocks, block_spans(count, rows)):
        grad = block[...]
        grad_ref[span, :] = dot_nt(grad, weight_ref[3]).astype(BF16)
        all_rows[span, :] = grad
    total = dot_tn(o_ref[...], all_rows[...])
    fsdp, _, part, columns = out_ref.shape
    for z in range(fsdp):
        out_ref[z, 0] = total[:part, z * columns : (z + 1) * columns].astype(BF16)


def out_back(attended, weights, blocks, fsdp, part):
    rows, width = attended.shape
    depth = weights.shape[2]
    return call(
        functools.partial(out_back_kernel, len(blocks)),
        "out_back",
        rows * width * depth * 4,
        rows * depth * 2,
        out_shape=(
            jax.ShapeDtypeStruct((rows, width), BF16),
            jax.ShapeDtypeStruct((fsdp, 1, part, depth // fsdp), BF16),
        ),
        in_specs=[whole()] * (2 + len(blocks)),
        out_specs=[whole()] * 2,
        scratch_shapes=[pltpu.VMEM((rows, depth), BF16)],
    )(attended, weights, *blocks)


def project_weights_kernel(count, dq_ref, dk_ref, dv_ref, done_ref, *refs):
    blocks, (out_ref, all_rows) = refs[:count], refs[count:]
    rows = all_rows.shape[0]
    for block, span in zip(blocks, block_spans(count, rows)):
        all_rows[span, :] = block[...]
    part = out_ref.shape[2]
    for kind, grad in enumerate((dq_ref, dk_ref, dv_ref)):
        out_ref[0, kind] = dot_tn(grad[:rows, :], all_rows[...])[:part].astype(BF16)
    out_ref[0, 3] = done_ref[0, 0]


def project_weights(dq, dk, dv, out_grads, blocks):
    rows, width = dq.shape
    fsdp, _, part, _ = out_grads.shape
    block, depth = blocks[0].shape
    columns = depth // fsdp
    fixed = lambda array: pl.BlockSpec(array.shape, lambda z: (0, 0))
    return call(
        functools.partial(project_weights_kernel, len(blocks)),
        "project_weights",
        rows * width * depth * 6,
        rows * depth * 2,
        grid=(fsdp,),
        out_shape=jax.ShapeDtypeStruct((fsdp, 4, part, columns), BF16),
        in_specs=[fixed(dq), fixed(dk), fixed(dv), pl.BlockSpec((1, 1, part, columns), lambda z: (z, 0, 0, 0))]
        + [pl.BlockSpec((block, columns), lambda z: (0, z))] * len(blocks),
        out_specs=pl.BlockSpec((1, 4, part, columns), lambda z: (z, 0, 0, 0)),
        scratch_shapes=[pltpu.VMEM((rows, columns), BF16)],
    )(dq, dk, dv, out_grads, *blocks)


def column_sums(grads, normed):
    product = grads * normed.astype(F32)
    return jnp.sum(product.reshape(product.shape[0] // 8, 8, product.shape[1]), axis=0)


def project_back_kernel(count, dq_ref, dk_ref, dv_ref, weight_ref, *refs):
    blocks, (kept_ref, sent_ref, gain_ref) = refs[:count], refs[count:]
    rows = dq_ref.shape[0]
    sums = 0.0
    for i, (block, span) in enumerate(zip(blocks, block_spans(count, rows))):
        total = dot(dq_ref[span, :], weight_ref[0]) + dot(dk_ref[span, :], weight_ref[1]) + dot(dv_ref[span, :], weight_ref[2])
        sums = sums + column_sums(total, block[...])
        store_block(kept_ref, sent_ref, i, rows // count, total)
    gain_ref[...] = sums


def project_back(dq, dk, dv, weights, blocks):
    rows, width = dq.shape
    depth = weights.shape[2]
    return call(
        functools.partial(project_back_kernel, len(blocks)),
        "project_back",
        rows * width * depth * 6,
        rows * depth * 4,
        out_shape=halves(rows, depth) + [jax.ShapeDtypeStruct((8, depth), F32)],
        in_specs=[whole()] * (4 + len(blocks)),
        out_specs=[whole()] * 3,
    )(dq, dk, dv, weights, *blocks)


def lane_half(head):
    return (lax.broadcasted_iota(jnp.int32, (1, LANES), 1) // HEAD_DIM) == head % 2


def forward_kernel(rows, bounds, q_ref, k_ref, v_ref, start_ref, o_ref, lse_ref, q_buf, s_buf, top_buf, sum_buf, acc_buf):
    heads = q_buf.shape[0]
    zero = jnp.zeros((), BF16)
    for t in range(-(-rows // TILE)):
        low, high = bounds[0, t], bounds[1, t]
        n = min(TILE, rows - t * TILE)
        span = slice(t * TILE, (t + 1) * TILE)
        start = start_ref[:, span]
        row = t * TILE + lax.broadcasted_iota(jnp.int32, (1, TILE), 1)
        for h in range(heads):
            c = (h // 2) * LANES
            scaled = (q_ref[t * TILE : t * TILE + n, c : c + LANES].astype(F32) * HEAD_DIM**-0.5).astype(BF16)
            q_buf[h, :n, :] = jnp.where(lane_half(h), scaled, zero)
            if n < TILE:
                q_buf[h, n:, :] = jnp.zeros((TILE - n, LANES), BF16)
        top_buf[...] = jnp.full_like(top_buf, MASKED)
        sum_buf[...] = jnp.zeros_like(sum_buf)
        acc_buf[...] = jnp.zeros_like(acc_buf)

        @pl.loop(low, high)
        def _(i):
            at = pl.multiple_of(i * TILE, TILE)
            place = at + lax.broadcasted_iota(jnp.int32, (TILE, TILE), 0)
            allowed = (place >= start) & (place <= row)
            for h in range(heads):
                c = (h // 2) * LANES
                s = jnp.where(allowed, dot_nt(k_ref[pl.ds(at, TILE), c : c + LANES], q_buf[h]), MASKED)
                s_buf[h, pl.ds(at, TILE), :] = s
                top_buf[h] = jnp.maximum(top_buf[h], jnp.max(s.reshape(TILE // 8, 8, TILE), axis=0))

        tops = [jnp.max(top_buf[h], axis=0, keepdims=True) for h in range(heads)]

        @pl.loop(low, high)
        def _(i):
            at = pl.multiple_of(i * TILE, TILE)
            for h in range(heads):
                c = (h // 2) * LANES
                p = jnp.exp(s_buf[h, pl.ds(at, TILE), :] - tops[h])
                sum_buf[h] += jnp.sum(p.reshape(TILE // 8, 8, TILE), axis=0)
                both = dot_tn(v_ref[pl.ds(at, TILE), c : c + LANES], p.astype(BF16))
                acc_buf[h] += both[HEAD_DIM * (h % 2) : HEAD_DIM * (h % 2) + HEAD_DIM]

        for h in range(heads):
            total = jnp.sum(sum_buf[h], axis=0, keepdims=True)
            lse_ref[h : h + 1, span] = tops[h] + jnp.log(total)
            acc_buf[h] = acc_buf[h] / total
        for pair in range(o_ref.shape[1] // LANES):
            second = acc_buf[2 * pair + 1] if 2 * pair + 1 < heads else jnp.zeros((HEAD_DIM, TILE), F32)
            o = jnp.transpose(jnp.concatenate([acc_buf[2 * pair], second], axis=0))
            o_ref[t * TILE : t * TILE + n, pair * LANES : (pair + 1) * LANES] = o[:n].astype(BF16)


def attend(bounds, q, k, v, start, heads):
    rows = q.shape[0]
    keys, width = k.shape
    padded = -(-rows // TILE) * TILE
    return call(
        functools.partial(forward_kernel, rows),
        "attend",
        rows * rows * heads * HEAD_DIM * 2,
        keys * width * 8,
        out_shape=(jax.ShapeDtypeStruct((rows, width), BF16), jax.ShapeDtypeStruct((heads, padded), F32)),
        in_specs=[pl.BlockSpec(memory_space=pltpu.SMEM)] + [whole()] * 4,
        out_specs=[whole(), whole()],
        scratch_shapes=[
            pltpu.VMEM((heads, TILE, LANES), BF16),
            pltpu.VMEM((heads, keys, TILE), F32),
            pltpu.VMEM((heads, 8, TILE), F32),
            pltpu.VMEM((heads, 8, TILE), F32),
            pltpu.VMEM((heads, HEAD_DIM, TILE), F32),
        ],
    )(bounds, q, k, v, start)


def backward_kernel(
    rows, bounds, q_ref, k_ref, v_ref, o_ref, g_ref, lse_ref, start_ref, cos_ref, sin_ref,
    dq_ref, dk_ref, dv_ref, q_buf, g_buf, d_buf, dq_acc, dk_acc, dv_acc,
):
    heads = q_buf.shape[0]
    zero = jnp.zeros((), BF16)
    scale = HEAD_DIM**-0.5
    dk_acc[...] = jnp.zeros_like(dk_acc)
    dv_acc[...] = jnp.zeros_like(dv_acc)
    for t in range(-(-rows // TILE)):
        low, high = bounds[0, t], bounds[1, t]
        n = min(TILE, rows - t * TILE)
        span = slice(t * TILE, (t + 1) * TILE)
        here = slice(t * TILE, t * TILE + n)
        start = start_ref[:, span]
        row = t * TILE + lax.broadcasted_iota(jnp.int32, (1, TILE), 1)
        for pair in range(-(-heads // 2)):
            c = pair * LANES
            scaled = (q_ref[here, c : c + LANES].astype(F32) * scale).astype(BF16)
            grad = g_ref[here, c : c + LANES]
            product = grad.astype(F32) * o_ref[here, c : c + LANES].astype(F32)
            if n < TILE:
                product = jnp.concatenate([product, jnp.zeros((TILE - n, LANES), F32)], axis=0)
            product = jnp.transpose(product)
            for h in range(2 * pair, min(heads, 2 * pair + 2)):
                q_buf[h, :n, :] = jnp.where(lane_half(h), scaled, zero)
                g_buf[h, :n, :] = jnp.where(lane_half(h), grad, zero)
                if n < TILE:
                    q_buf[h, n:, :] = jnp.zeros((TILE - n, LANES), BF16)
                    g_buf[h, n:, :] = jnp.zeros((TILE - n, LANES), BF16)
                d_buf[h : h + 1, :] = jnp.sum(product[HEAD_DIM * (h % 2) : HEAD_DIM * (h % 2) + HEAD_DIM], axis=0, keepdims=True)
        dq_acc[...] = jnp.zeros_like(dq_acc)

        @pl.loop(low, high)
        def _(i):
            at = pl.multiple_of(i * TILE, TILE)
            place = at + lax.broadcasted_iota(jnp.int32, (TILE, TILE), 0)
            allowed = (place >= start) & (place <= row)
            for pair in range(-(-heads // 2)):
                c = pair * LANES
                k = k_ref[pl.ds(at, TILE), c : c + LANES]
                v = v_ref[pl.ds(at, TILE), c : c + LANES]
                dq = dk = dv = 0.0
                for h in range(2 * pair, min(heads, 2 * pair + 2)):
                    p = jnp.where(allowed, jnp.exp(dot_nt(k, q_buf[h]) - lse_ref[h : h + 1, span]), 0.0)
                    ds = (p * (dot_nt(v, g_buf[h]) - d_buf[h : h + 1, :])).astype(BF16)
                    dv = dv + dot(p.astype(BF16), g_buf[h])
                    dk = dk + dot(ds, q_buf[h])
                    dq = dq + dot_tn(ds, jnp.where(lane_half(h), k, zero))
                dk_acc[pl.ds(at, TILE), c : c + LANES] += dk
                dv_acc[pl.ds(at, TILE), c : c + LANES] += dv
                dq_acc[:, c : c + LANES] += dq

        for c in range(0, dk_ref.shape[1], LANES):
            dq = dq_acc[:n, c : c + LANES] * scale
            dq_ref[here, c : c + LANES] = turn(dq, cos_ref[here, :], sin_ref[here, :], -1.0).astype(BF16)
    for c in range(0, dk_ref.shape[1], LANES):
        dk_ref[:, c : c + LANES] = turn(dk_acc[:, c : c + LANES], cos_ref[...], sin_ref[...], -1.0).astype(BF16)
    dv_ref[...] = dv_acc[...].astype(BF16)


def attend_back(bounds, q, k, v, o, grad, lse, start, cos, sin, heads):
    rows = q.shape[0]
    keys, width = k.shape
    tall = jax.ShapeDtypeStruct((keys, width), BF16)
    return call(
        functools.partial(backward_kernel, rows),
        "attend_back",
        rows * rows * heads * HEAD_DIM * 5,
        keys * width * 16,
        out_shape=(jax.ShapeDtypeStruct((rows, width), BF16), tall, tall),
        in_specs=[pl.BlockSpec(memory_space=pltpu.SMEM)] + [whole()] * 9,
        out_specs=[whole()] * 3,
        scratch_shapes=[
            pltpu.VMEM((heads, TILE, LANES), BF16),
            pltpu.VMEM((heads, TILE, LANES), BF16),
            pltpu.VMEM((heads, TILE), F32),
            pltpu.VMEM((TILE, width), F32),
            pltpu.VMEM((keys, width), F32),
            pltpu.VMEM((keys, width), F32),
        ],
    )(bounds, q, k, v, o, grad, lse, start, cos, sin)


def joined(ref):
    shape = ref.shape
    return ref[...].reshape(shape[0] * shape[2], shape[3])


def once(shape):
    return pl.BlockSpec(shape, lambda i: (0,) * len(shape), pipeline_mode=pl.Buffered(1))


def feed_kernel(count, *refs):
    n_refs, dy_refs, weights = refs[:count], refs[count : 2 * count], refs[2 * count : 2 * count + 3]
    hidden_ref, gate_ref, up_ref, kept_ref, sent_ref, gain_ref, acc = refs[2 * count + 3 :]
    step = pl.program_id(0)
    block = n_refs[0].shape[0]

    @pl.when(step == 0)
    def _():
        acc[...] = jnp.zeros_like(acc)

    gate_w, up_w, down_w = (joined(ref) for ref in weights)
    for i in range(count):
        rows = slice(i * block, (i + 1) * block)
        normed = n_refs[i][...]
        gate = dot(normed, gate_w)
        up = dot(normed, up_w)
        grad = dot(dy_refs[i][...], down_w)
        sig = 1.0 / (1.0 + jnp.exp(-gate))
        silu = gate * sig
        hidden_ref[rows, :] = (silu * up).astype(BF16)
        gate_grad = (grad * up * sig * (1.0 + gate * (1.0 - sig))).astype(BF16)
        up_grad = (grad * silu).astype(BF16)
        gate_ref[rows, :] = gate_grad
        up_ref[rows, :] = up_grad
        acc[rows, :] += dot_nt(gate_grad, gate_w) + dot_nt(up_grad, up_w)

    @pl.when(step == pl.num_programs(0) - 1)
    def _():
        total = 0.0
        for i in range(count):
            values = acc[i * block : (i + 1) * block, :]
            store_block(kept_ref, sent_ref, i, block, values)
            total = total + column_sums(values, n_refs[i][...])
        gain_ref[...] = total


def feed(normed, dy, weights):
    count = len(normed)
    block, depth = normed[0].shape
    rows = count * block
    fsdp, _, columns, units = weights.shape
    tile = min(TILE, units)
    kind = lambda k: pl.BlockSpec((fsdp, 1, columns, tile), lambda i: (0, k, 0, i))
    out = pl.BlockSpec((rows, tile), lambda i: (0, i))
    wide = jax.ShapeDtypeStruct((rows, units), BF16)
    half = once((rows // 2, depth))
    return call(
        functools.partial(feed_kernel, count),
        "feed",
        rows * depth * units * 10,
        depth * units * 6,
        grid=(units // tile,),
        out_shape=[wide, wide, wide] + halves(rows, depth) + [jax.ShapeDtypeStruct((8, depth), F32)],
        in_specs=[once((block, depth))] * (2 * count) + [kind(0), kind(1), kind(2)],
        out_specs=[out, out, out, half, half, once((8, depth))],
        scratch_shapes=[pltpu.VMEM((rows, depth), F32)],
    )(*normed, *dy, weights, weights, weights)


def feed_weights_kernel(count, *refs):
    blocks = refs[: 2 * count]
    gate_ref, up_ref, hidden_ref, out_ref, normed, dy = refs[2 * count :]
    block = blocks[0].shape[0]
    fsdp, _, columns, tile = out_ref.shape

    @pl.when(pl.program_id(0) == 0)
    def _():
        for i in range(count):
            normed[i * block : (i + 1) * block, :] = blocks[i][...]
            dy[i * block : (i + 1) * block, :] = blocks[count + i][...]

    for kind, (left, right) in enumerate(((normed, gate_ref), (normed, up_ref), (dy, hidden_ref))):
        out_ref[:, kind] = dot_tn(left[...], right[...]).astype(BF16).reshape(fsdp, columns, tile)


def feed_weights(normed, dy, gate_grad, up_grad, hidden, fsdp):
    count = len(normed)
    block, depth = normed[0].shape
    rows, units = hidden.shape
    columns = depth // fsdp
    tile = min(TILE, units)
    return call(
        functools.partial(feed_weights_kernel, count),
        "feed_weights",
        rows * depth * units * 6,
        depth * units * 6,
        grid=(units // tile,),
        out_shape=jax.ShapeDtypeStruct((fsdp, 3, columns, units), BF16),
        in_specs=[once((block, depth))] * (2 * count) + [pl.BlockSpec((rows, tile), lambda i: (0, i))] * 3,
        out_specs=pl.BlockSpec((fsdp, 3, columns, tile), lambda i: (0, 0, 0, i)),
        scratch_shapes=[pltpu.VMEM((rows, depth), BF16)] * 2,
    )(*normed, *dy, gate_grad, up_grad, hidden)


def feed_out_kernel(count, hidden_ref, weight_ref, kept_ref, sent_ref):
    weight = joined(weight_ref)
    block = hidden_ref.shape[0] // count
    for i in range(count):
        values = dot_nt(hidden_ref[i * block : (i + 1) * block, :], weight)
        store_block(kept_ref, sent_ref, i, block, values)


def feed_out(hidden, weights, count):
    rows = hidden.shape[0]
    fsdp, _, columns, units = weights.shape
    depth = fsdp * columns
    return call(
        functools.partial(feed_out_kernel, count),
        "feed_out",
        rows * depth * units * 2,
        rows * depth * 2,
        grid=(1,),
        out_shape=halves(rows, depth),
        in_specs=[once((rows, units)), pl.BlockSpec((fsdp, 1, columns, units), lambda i: (0, 2, 0, 0))],
        out_specs=[once((rows // 2, depth))] * 2,
    )(hidden, weights)


def quarter_places():
    place = 2 * lax.axis_index("chip") + lax.axis_index("core")
    return place, place ^ 2, place ^ 1, place ^ 3


def finish_feed_kernel(own_ref, across_ref, came_ref, gate_ref, up_ref, down_ref):
    units = own_ref.shape[2]
    for place, piece in zip(quarter_places(), (own_ref, across_ref, came_ref.at[0], came_ref.at[1])):
        span = pl.ds(pl.multiple_of(place * units, LANES), units)
        gate_ref[:, span] = piece[0].astype(F32)
        up_ref[:, span] = piece[1].astype(F32)
        down_ref[span, :] = jnp.transpose(piece[2].astype(F32))


def finish_feed(own, across, came):
    _, columns, units = own.shape
    wide = jax.ShapeDtypeStruct((columns, 4 * units), F32)
    return call(
        finish_feed_kernel,
        "finish_feed",
        0,
        own.size * 24,
        out_shape=(wide, wide, jax.ShapeDtypeStruct((4 * units, columns), F32)),
        in_specs=[whole()] * 3,
        out_specs=[whole()] * 3,
    )(own, across, came)


def finish_attention_kernel(real, own_ref, across_ref, came_ref, q_ref, k_ref, v_ref, out_ref, buf):
    part = own_ref.shape[1]
    pieces = (own_ref, across_ref, came_ref.at[0], came_ref.at[1])
    for kind, ref in enumerate((q_ref, k_ref, v_ref, out_ref)):
        for place, piece in zip(quarter_places(), pieces):
            buf[pl.ds(pl.multiple_of(place * part, 16), part), :] = piece[kind].astype(F32)
        ref[...] = buf[:real, :] if kind == 3 else jnp.transpose(buf[...])[:, :real]


def finish_attention(own, across, came, real):
    _, part, columns = own.shape
    into = jax.ShapeDtypeStruct((columns, real), F32)
    return call(
        functools.partial(finish_attention_kernel, real),
        "finish_attention",
        0,
        own.size * 24,
        out_shape=(into, into, into, jax.ShapeDtypeStruct((real, columns), F32)),
        in_specs=[whole()] * 3,
        out_specs=[whole()] * 4,
        scratch_shapes=[pltpu.VMEM((4 * part, columns), F32)],
    )(own, across, came)


def normalize_back(values, inverse, gain, grad_rows):
    scaled = grad_rows * gain
    return inverse * scaled - values * inverse**3 * jnp.mean(scaled * values, axis=-1, keepdims=True)


def inverse_rms(values):
    return lax.rsqrt(jnp.mean(values * values, axis=-1, keepdims=True) + EPSILON)


def pull_fsdp(values, step):
    count = lax.axis_size("fsdp")
    return lax.ppermute(values, "fsdp", [(i, (i - step) % count) for i in range(count)])


def gather_gains(gains):
    count = lax.axis_size("fsdp")
    rolled = jnp.concatenate([gains] + [pull_fsdp(gains, step) for step in range(1, count)], axis=1).astype(F32)
    twice = jnp.concatenate([rolled, rolled], axis=1)
    at = (count - lax.axis_index("fsdp")) % count * gains.shape[1]
    return lax.dynamic_slice_in_dim(twice, at, rolled.shape[1], 1)


def gain_totals(gains):
    if lax.axis_size("tp") == 2:
        gains = gains + swap_tp(gains)
    else:
        gains = lax.psum(gains, "tp")
    gains = gains + swap_core(gains)
    gains = gains + swap_chip(gains)
    count = lax.axis_size("fsdp")
    blocks = jnp.stack(jnp.split(gains, count, axis=1))
    return jnp.sum(lax.all_to_all(blocks, "fsdp", 0, 0, tiled=True), axis=0)


def scatter_fsdp(values):
    shape = values.shape
    flat = values.reshape((shape[0] * shape[1],) + shape[2:])
    return lax.psum_scatter(flat, "fsdp", scatter_dimension=0, tiled=True)


def shards(tokens, segment_ids, wq, wk, wv, wo, w_gate, w_up, w_down, gain_attn, gain_ffn, cotangent):
    tokens, cotangent, segment_ids = tokens[0], cotangent[0], segment_ids[0]
    fsdp = lax.axis_size("fsdp")
    chip, core = lax.axis_index("chip"), lax.axis_index("core")
    place = 2 * chip + core
    rows = 4 * segment_ids.shape[0]
    real_width = wq.shape[1]
    part = -(-real_width // (4 * HEAD_DIM)) * HEAD_DIM
    heads = part // HEAD_DIM
    width = -(-part // LANES) * LANES
    keys = -(-rows // TILE) * TILE
    both_links = lax.axis_size("tp") == 2

    pad = ((0, 0), (0, 4 * part - real_width))
    own_piece = cut_attention(*[jnp.pad(w, pad) for w in (wq, wk, wv)], jnp.pad(wo, pad[::-1]))
    feed_piece = jnp.stack([take_quarter(w_gate, place, 1), take_quarter(w_up, place, 1), jnp.transpose(take_quarter(w_down, place, 0))])

    position = after(jnp.arange(keys, dtype=jnp.int32), own_piece).astype(F32)
    pair_index = (jnp.arange(LANES, dtype=jnp.int32) % (HEAD_DIM // 2)).astype(F32)
    angles = position[:, None] * (10000.0 ** (-pair_index * 2.0 / HEAD_DIM))[None, :]

    def normed(values):
        values = values.astype(F32)
        return (values * inverse_rms(values) * gain_one).astype(BF16)

    if both_links:
        first = lambda values: [values, swap_tp(values), swap_chip(values)]
        second = lambda blocks: widen_core(blocks) + far_block(*blocks)[3:]
        third = lambda blocks: blocks[:3] + blocks[6:] + blocks[3:6] + [swap_core(blocks[6])]
    else:
        first, second, third = widen_planes, widen_core, lambda blocks: blocks
    ring = [own_piece]
    block, own, gains, ids_other, cos, sin = together(
        pull_fsdp(ring[0], 1),
        first(tokens),
        gather_gains(jnp.stack([gain_attn, gain_ffn])),
        swap_core(segment_ids),
        jnp.cos(angles),
        jnp.sin(angles),
    )
    ring.append(block)
    gain_one, gain_two = gains
    ids_chip = jnp.concatenate(in_order(segment_ids, ids_other, core == 0))
    block, own, ids_across = together(pull_fsdp(ring[-1], 1), second(own), swap_chip(ids_chip))
    ring.append(block)
    feed_weight = lax.all_gather(after(feed_piece, block), "fsdp", axis=0, tiled=False)
    ids = jnp.concatenate(in_order(ids_chip, ids_across, chip == 0))
    start = jnp.sum((ids[None, :] < ids[:, None]).astype(jnp.int32), axis=1)
    dy = cotangent
    for step in range(2, fsdp - 1):
        if step == 2:
            early = [normed(values) for values in own[:6]]
            block, own, early, dy = together(pull_fsdp(ring[-1], 1), third(own), early, first(after(cotangent, block)))
        else:
            block = pull_fsdp(ring[-1], 1)
        ring.append(block)
    weights = place_weights(ring, width)
    tiles = -(-rows // TILE)
    ends = [-(-min((t + 1) * TILE, rows) // TILE) for t in range(tiles)]
    bounds = jnp.stack([start[::TILE] // TILE, jnp.array(ends, jnp.int32)])
    start = jnp.pad(start, (0, tiles * TILE - rows), constant_values=2 * keys)[None]

    if both_links:
        blocks = early[:3] + [normed(own[3])] + early[3:] + [normed(own[7])]
    else:
        blocks = early
    count = len(blocks)
    inputs = tokens.astype(F32)
    inv_one = inverse_rms(inputs)
    q, k, v = project(blocks, weights, cos, sin, keys)
    dy = second(after(dy, q))
    attended, lse = attend(bounds, q, k, v, start, heads)
    attended, dy = together(attended, dy)
    dy = third(dy)
    leaving = narrow_first(*out_project(attended, weights, count), feed_weight)
    attention_rows, dy = narrow_second(leaving, lambda rows, dy=dy: dy)
    residual = inputs + attention_rows

    inv_two = inverse_rms(residual)
    normed_two = widen((residual * inv_two * gain_two).astype(BF16))
    hidden, gate_grad, up_grad, kept, sent, gain_two_sums = feed(normed_two, dy, feed_weight)
    normed_two_grad, feed_grads = narrow(
        kept, sent, lambda leaving: feed_weights(normed_two, dy, after(gate_grad, leaving), up_grad, hidden, fsdp)
    )
    feed_sums = scatter_fsdp(feed_grads)
    resid_grad = cotangent.astype(F32) + normalize_back(residual, inv_two, gain_two, normed_two_grad)
    resid_low = resid_grad.astype(BF16)

    out_kept, out_sent = feed_out(after(hidden, resid_low), feed_weight, count)
    grad_blocks = widen_core(widen_planes(resid_low, out_sent))
    out_grad, out_grads = out_back(attended, weights, grad_blocks, fsdp, part)
    leaving = narrow_first(out_kept, out_sent, out_grad)
    dq, dk, dv = attend_back(bounds, q, k, v, attended, after(out_grad, leaving), lse, start, cos, sin, heads)
    layer_out = residual + narrow_second(leaving, lambda rows: dq)[0]
    project_grads = project_weights(dq, dk, after(dv, layer_out), out_grads, blocks)
    sums = scatter_fsdp(project_grads)
    kept, sent, gain_one_sums = project_back(after(dq, project_grads), dk, dv, weights, blocks)
    gate_all, up_all, down_all = finish_feed(*all_quarters(after(feed_sums, dq)))
    gain_sums = jnp.stack([jnp.sum(gain_one_sums, axis=0) / gain_one, jnp.sum(gain_two_sums, axis=0) / gain_two])
    normed_grad, gain_own = narrow(kept, sent, lambda leaving: gain_totals(after(gain_sums, leaving)))
    grad_input = resid_grad + normalize_back(inputs, inv_one, gain_one, normed_grad)

    q_all, k_all, v_all, out_all = finish_attention(*all_quarters(sums), real_width)
    return (
        layer_out.astype(BF16)[None],
        grad_input[None],
        q_all,
        k_all,
        v_all,
        out_all,
        gate_all,
        up_all,
        down_all,
        gain_own[0],
        gain_own[1],
    )


def solution(mesh):
    devices = mesh.devices.reshape(mesh.shape["fsdp"], mesh.shape["ctx"] // 2, 2, mesh.shape["tp"])
    split = jax.sharding.Mesh(devices, ("fsdp", "chip", "core", "tp"))
    rows = P("fsdp", ("chip", "core", "tp"), None)
    into, outof, gain = P("fsdp", "tp"), P("tp", "fsdp"), P("fsdp")
    return jax.shard_map(
        shards,
        mesh=split,
        in_specs=(rows, P("fsdp", ("chip", "core")), into, into, into, outof, into, into, outof, gain, gain, rows),
        out_specs=(rows, rows, into, into, into, outof, into, into, outof, gain, gain),
        check_vma=False,
    )
```

```python
import functools

import jax
import jax.numpy as jnp
from jax import lax
from jax.experimental import pallas as pl
from jax.experimental.pallas import tpu as pltpu
from jax.sharding import PartitionSpec as P

HEAD_DIM = 64
EPSILON = 1e-05
MASKED = -1e30
BF16 = jnp.bfloat16
F32 = jnp.float32
TILE = 256
LANES = 128
VMEM_BYTES = 60 * 1024 * 1024


def dot(left, right):
    return jnp.dot(left, right, preferred_element_type=F32)


def dot_nt(left, right):
    return lax.dot_general(left, right, (((1,), (1,)), ((), ())), preferred_element_type=F32)


def dot_tn(left, right):
    return lax.dot_general(left, right, (((0,), (0,)), ((), ())), preferred_element_type=F32)


def swap_chip(values):
    return lax.ppermute(values, "chip", [(0, 1), (1, 0)])


def swap_core(values):
    return lax.ppermute(values, "core", [(0, 1), (1, 0)])


def swap_tp(values):
    return lax.ppermute(values, "tp", [(0, 1), (1, 0)])


def in_order(mine, other, mine_first):
    return [jnp.where(mine_first, mine, other), jnp.where(mine_first, other, mine)]


def together(*values):
    return lax.optimization_barrier(values)


def after(values, *earlier):
    return lax.optimization_barrier((values, earlier))[0]


def widen_planes(rows, meanwhile=None):
    if lax.axis_size("tp") != 2:
        gathered = lax.all_gather(rows, "tp", axis=0, tiled=True)
        return [gathered, swap_chip(gathered)], meanwhile
    (beside, across), meanwhile = together((swap_tp(rows), swap_chip(rows)), meanwhile)
    return far_block(rows, beside, across), meanwhile


def meet(beside, across, meanwhile):
    return (beside, across) if meanwhile is None else after((beside, across), meanwhile)


def far_block(rows, beside, across):
    cut = rows.shape[0] // 32 * 16
    far = jnp.concatenate([swap_tp(across[:cut]), swap_chip(beside[cut:])], axis=0)
    return [rows, beside, across, far]


def widen_core(blocks):
    return blocks + [swap_core(block) for block in blocks]


def widen(rows):
    return widen_core(widen_planes(rows)[0])


def block_offset(index, half):
    chip, core = lax.axis_index("chip"), lax.axis_index("core")
    if lax.axis_size("tp") != 2:
        return (chip ^ index % 2) * 2 * half + (core ^ index // 2) * half
    place = lax.axis_index("tp")
    return (chip ^ index // 2 % 2) * 2 * half + (core ^ index // 4) * half + (place ^ index % 2) * (half // 2)


def narrow_first(kept, sent, meanwhile=None):
    came = swap_core(sent)
    if lax.axis_size("tp") != 2:
        rows = kept.shape[0] // 2
        total = kept.astype(F32) + came.astype(F32)
        return ((total[:rows] + swap_chip(total[rows:].astype(BF16)).astype(F32)).astype(BF16),)
    rows = kept.shape[0] // 4
    cut = rows // 32 * 16

    def block(index, first, last):
        where = slice(index * rows + first, index * rows + last)
        return kept[where].astype(F32) + came[where].astype(F32)

    top, bottom = meet(swap_chip(block(3, 0, cut).astype(BF16)), swap_tp(block(3, cut, rows).astype(BF16)), meanwhile)
    beside = jnp.concatenate([block(1, 0, cut) + top.astype(F32), block(1, cut, rows)], axis=0).astype(BF16)
    across = jnp.concatenate([block(2, 0, cut), block(2, cut, rows) + bottom.astype(F32)], axis=0).astype(BF16)
    return beside, across, block(0, 0, rows)


def narrow_second(leaving, meanwhile=None):
    done = None
    if len(leaving) == 1:
        if meanwhile is not None:
            done = meanwhile(leaving)
        return lax.psum_scatter(leaving[0], "tp", scatter_dimension=0, tiled=True).astype(F32), done
    from_tp, from_chip = swap_tp(leaving[0]), swap_chip(leaving[1])
    if meanwhile is not None:
        (from_tp, from_chip), done = together((from_tp, from_chip), meanwhile(leaving[:2]))
    return leaving[2] + from_tp.astype(F32) + from_chip.astype(F32), done


def narrow(kept, sent, meanwhile=None):
    return narrow_second(narrow_first(kept, sent), meanwhile)


def take_quarter(values, index, axis):
    size = values.shape[axis] // 4
    return lax.dynamic_slice_in_dim(values, index * size, size, axis)


def call(kernel, name, flops, moved, **rest):
    return pl.pallas_call(
        kernel,
        name=name,
        cost_estimate=pl.CostEstimate(flops=flops, bytes_accessed=moved, transcendentals=0),
        compiler_params=pltpu.CompilerParams(vmem_limit_bytes=VMEM_BYTES),
        **rest,
    )


def whole():
    return pl.BlockSpec(memory_space=pltpu.VMEM)


def turn(values, cos, sin, direction):
    lane = lax.broadcasted_iota(jnp.int32, (1, LANES), 1)
    partner = jnp.where((lane // 32) % 2 == 0, pltpu.roll(values, 96, 1) * -direction, pltpu.roll(values, 32, 1) * direction)
    return values * cos + partner * sin


def block_spans(count, rows):
    block = rows // count
    return [pl.ds(pl.multiple_of(block_offset(i, rows // 4), 16), block) for i in range(count)]


def project_kernel(count, rows, *refs):
    blocks = refs[:count]
    weight_ref, cos_ref, sin_ref, q_ref, k_ref, v_ref = refs[count:]
    width = q_ref.shape[1]
    for ref in (k_ref, v_ref):
        ref[rows:, :] = jnp.zeros((ref.shape[0] - rows, width), BF16)
    for block, span in zip(blocks, block_spans(count, rows)):
        cos, sin = cos_ref[span, :], sin_ref[span, :]
        for kind, out_ref in ((0, q_ref), (1, k_ref)):
            values = dot_nt(block[...], weight_ref[kind])
            for c in range(0, width, LANES):
                out_ref[span, c : c + LANES] = turn(values[:, c : c + LANES], cos, sin, 1.0).astype(BF16)
        v_ref[span, :] = dot_nt(block[...], weight_ref[2]).astype(BF16)


def project(blocks, weights, cos, sin, keys):
    count = len(blocks)
    block, depth = blocks[0].shape
    rows = count * block
    width = weights.shape[1]
    tall = jax.ShapeDtypeStruct((keys, width), BF16)
    return call(
        functools.partial(project_kernel, count, rows),
        "project",
        rows * depth * width * 6,
        rows * depth * 2,
        out_shape=(jax.ShapeDtypeStruct((rows, width), BF16), tall, tall),
        in_specs=[whole()] * (count + 3),
        out_specs=[whole()] * 3,
    )(*blocks, weights, cos, sin)


def cut_kernel(q_ref, k_ref, v_ref, out_ref, piece_ref, buf):
    part = piece_ref.shape[1]
    span = pl.ds(pl.multiple_of(quarter_places()[0] * part, 16), part)
    for kind, ref in enumerate((q_ref, k_ref, v_ref)):
        buf[...] = jnp.transpose(ref[...])
        piece_ref[kind] = buf[span, :]
    piece_ref[3] = out_ref[span, :]


def cut_attention(wq, wk, wv, wo):
    width, columns = wo.shape
    return call(
        cut_kernel,
        "cut_attention",
        0,
        width * columns * 8,
        out_shape=jax.ShapeDtypeStruct((4, width // 4, columns), BF16),
        in_specs=[whole()] * 4,
        out_specs=whole(),
        scratch_shapes=[pltpu.VMEM((width, columns), BF16)],
    )(wq, wk, wv, wo)


def place_kernel(*refs):
    blocks, out_ref = refs[:-1], refs[-1]
    kinds, part, columns = blocks[0].shape
    me = lax.axis_index("fsdp")
    if part < out_ref.shape[1]:
        out_ref[:, part:, :] = jnp.zeros((kinds, out_ref.shape[1] - part, out_ref.shape[2]), BF16)
    for i, block in enumerate(blocks):
        at = pl.multiple_of((me + i) % len(blocks) * columns, LANES)
        out_ref[:, :part, pl.ds(at, columns)] = block[...]


def place_weights(blocks, width):
    kinds, _, columns = blocks[0].shape
    depth = len(blocks) * columns
    return call(
        place_kernel,
        "place_weights",
        0,
        kinds * width * depth * 4,
        out_shape=jax.ShapeDtypeStruct((kinds, width, depth), BF16),
        in_specs=[whole()] * len(blocks),
        out_specs=whole(),
    )(*blocks)


def store_block(kept_ref, sent_ref, i, block, values):
    half = kept_ref.shape[0]
    at = i * block
    if at < half:
        kept_ref[at : at + block, :] = values.astype(BF16)
    else:
        sent_ref[at - half : at - half + block, :] = values.astype(BF16)


def halves(rows, depth):
    return [jax.ShapeDtypeStruct((rows // 2, depth), BF16)] * 2


def out_kernel(count, o_ref, weight_ref, kept_ref, sent_ref):
    rows = o_ref.shape[0]
    for i, span in enumerate(block_spans(count, rows)):
        store_block(kept_ref, sent_ref, i, rows // count, dot(o_ref[span, :], weight_ref[3]))


def out_project(attended, weights, count):
    rows, width = attended.shape
    depth = weights.shape[2]
    return call(
        functools.partial(out_kernel, count),
        "out_project",
        rows * width * depth * 2,
        rows * depth * 2,
        out_shape=halves(rows, depth),
        in_specs=[whole(), whole()],
        out_specs=[whole(), whole()],
    )(attended, weights)


def out_back_kernel(count, o_ref, weight_ref, *refs):
    blocks, (grad_ref, out_ref, all_rows) = refs[:count], refs[count:]
    rows = o_ref.shape[0]
    for block, span in zip(blocks, block_spans(count, rows)):
        grad = block[...]
        grad_ref[span, :] = dot_nt(grad, weight_ref[3]).astype(BF16)
        all_rows[span, :] = grad
    total = dot_tn(o_ref[...], all_rows[...])
    fsdp, _, part, columns = out_ref.shape
    for z in range(fsdp):
        out_ref[z, 0] = total[:part, z * columns : (z + 1) * columns].astype(BF16)


def out_back(attended, weights, blocks, fsdp, part):
    rows, width = attended.shape
    depth = weights.shape[2]
    return call(
        functools.partial(out_back_kernel, len(blocks)),
        "out_back",
        rows * width * depth * 4,
        rows * depth * 2,
        out_shape=(
            jax.ShapeDtypeStruct((rows, width), BF16),
            jax.ShapeDtypeStruct((fsdp, 1, part, depth // fsdp), BF16),
        ),
        in_specs=[whole()] * (2 + len(blocks)),
        out_specs=[whole()] * 2,
        scratch_shapes=[pltpu.VMEM((rows, depth), BF16)],
    )(attended, weights, *blocks)


def project_weights_kernel(count, dq_ref, dk_ref, dv_ref, done_ref, *refs):
    blocks, (out_ref, all_rows) = refs[:count], refs[count:]
    rows = all_rows.shape[0]
    for block, span in zip(blocks, block_spans(count, rows)):
        all_rows[span, :] = block[...]
    part = out_ref.shape[2]
    for kind, grad in enumerate((dq_ref, dk_ref, dv_ref)):
        out_ref[0, kind] = dot_tn(grad[:rows, :], all_rows[...])[:part].astype(BF16)
    out_ref[0, 3] = done_ref[0, 0]


def project_weights(dq, dk, dv, out_grads, blocks):
    rows, width = dq.shape
    fsdp, _, part, _ = out_grads.shape
    block, depth = blocks[0].shape
    columns = depth // fsdp
    fixed = lambda array: pl.BlockSpec(array.shape, lambda z: (0, 0))
    return call(
        functools.partial(project_weights_kernel, len(blocks)),
        "project_weights",
        rows * width * depth * 6,
        rows * depth * 2,
        grid=(fsdp,),
        out_shape=jax.ShapeDtypeStruct((fsdp, 4, part, columns), BF16),
        in_specs=[fixed(dq), fixed(dk), fixed(dv), pl.BlockSpec((1, 1, part, columns), lambda z: (z, 0, 0, 0))]
        + [pl.BlockSpec((block, columns), lambda z: (0, z))] * len(blocks),
        out_specs=pl.BlockSpec((1, 4, part, columns), lambda z: (z, 0, 0, 0)),
        scratch_shapes=[pltpu.VMEM((rows, columns), BF16)],
    )(dq, dk, dv, out_grads, *blocks)


def column_sums(grads, normed):
    product = grads * normed.astype(F32)
    return jnp.sum(product.reshape(product.shape[0] // 8, 8, product.shape[1]), axis=0)


def project_back_kernel(count, dq_ref, dk_ref, dv_ref, weight_ref, *refs):
    blocks, (kept_ref, sent_ref, gain_ref) = refs[:count], refs[count:]
    rows = dq_ref.shape[0]
    sums = 0.0
    for i, (block, span) in enumerate(zip(blocks, block_spans(count, rows))):
        total = dot(dq_ref[span, :], weight_ref[0]) + dot(dk_ref[span, :], weight_ref[1]) + dot(dv_ref[span, :], weight_ref[2])
        sums = sums + column_sums(total, block[...])
        store_block(kept_ref, sent_ref, i, rows // count, total)
    gain_ref[...] = sums


def project_back(dq, dk, dv, weights, blocks):
    rows, width = dq.shape
    depth = weights.shape[2]
    return call(
        functools.partial(project_back_kernel, len(blocks)),
        "project_back",
        rows * width * depth * 6,
        rows * depth * 4,
        out_shape=halves(rows, depth) + [jax.ShapeDtypeStruct((8, depth), F32)],
        in_specs=[whole()] * (4 + len(blocks)),
        out_specs=[whole()] * 3,
    )(dq, dk, dv, weights, *blocks)


def lane_half(head):
    return (lax.broadcasted_iota(jnp.int32, (1, LANES), 1) // HEAD_DIM) == head % 2


def forward_kernel(rows, bounds, q_ref, k_ref, v_ref, start_ref, o_ref, lse_ref, q_buf, s_buf, top_buf, sum_buf, acc_buf):
    heads = q_buf.shape[0]
    zero = jnp.zeros((), BF16)
    for t in range(-(-rows // TILE)):
        low, high = bounds[0, t], bounds[1, t]
        n = min(TILE, rows - t * TILE)
        span = slice(t * TILE, (t + 1) * TILE)
        start = start_ref[:, span]
        row = t * TILE + lax.broadcasted_iota(jnp.int32, (1, TILE), 1)
        for h in range(heads):
            c = (h // 2) * LANES
            scaled = (q_ref[t * TILE : t * TILE + n, c : c + LANES].astype(F32) * HEAD_DIM**-0.5).astype(BF16)
            q_buf[h, :n, :] = jnp.where(lane_half(h), scaled, zero)
            if n < TILE:
                q_buf[h, n:, :] = jnp.zeros((TILE - n, LANES), BF16)
        top_buf[...] = jnp.full_like(top_buf, MASKED)
        sum_buf[...] = jnp.zeros_like(sum_buf)
        acc_buf[...] = jnp.zeros_like(acc_buf)

        @pl.loop(low, high)
        def _(i):
            at = pl.multiple_of(i * TILE, TILE)
            place = at + lax.broadcasted_iota(jnp.int32, (TILE, TILE), 0)
            allowed = (place >= start) & (place <= row)
            for h in range(heads):
                c = (h // 2) * LANES
                s = jnp.where(allowed, dot_nt(k_ref[pl.ds(at, TILE), c : c + LANES], q_buf[h]), MASKED)
                s_buf[h, pl.ds(at, TILE), :] = s
                top_buf[h] = jnp.maximum(top_buf[h], jnp.max(s.reshape(TILE // 8, 8, TILE), axis=0))

        tops = [jnp.max(top_buf[h], axis=0, keepdims=True) for h in range(heads)]

        @pl.loop(low, high)
        def _(i):
            at = pl.multiple_of(i * TILE, TILE)
            for h in range(heads):
                c = (h // 2) * LANES
                p = jnp.exp(s_buf[h, pl.ds(at, TILE), :] - tops[h])
                sum_buf[h] += jnp.sum(p.reshape(TILE // 8, 8, TILE), axis=0)
                both = dot_tn(v_ref[pl.ds(at, TILE), c : c + LANES], p.astype(BF16))
                acc_buf[h] += both[HEAD_DIM * (h % 2) : HEAD_DIM * (h % 2) + HEAD_DIM]

        for h in range(heads):
            total = jnp.sum(sum_buf[h], axis=0, keepdims=True)
            lse_ref[h : h + 1, span] = tops[h] + jnp.log(total)
            acc_buf[h] = acc_buf[h] / total
        for pair in range(o_ref.shape[1] // LANES):
            second = acc_buf[2 * pair + 1] if 2 * pair + 1 < heads else jnp.zeros((HEAD_DIM, TILE), F32)
            o = jnp.transpose(jnp.concatenate([acc_buf[2 * pair], second], axis=0))
            o_ref[t * TILE : t * TILE + n, pair * LANES : (pair + 1) * LANES] = o[:n].astype(BF16)


def attend(bounds, q, k, v, start, heads):
    rows = q.shape[0]
    keys, width = k.shape
    padded = -(-rows // TILE) * TILE
    return call(
        functools.partial(forward_kernel, rows),
        "attend",
        rows * rows * heads * HEAD_DIM * 2,
        keys * width * 8,
        out_shape=(jax.ShapeDtypeStruct((rows, width), BF16), jax.ShapeDtypeStruct((heads, padded), F32)),
        in_specs=[pl.BlockSpec(memory_space=pltpu.SMEM)] + [whole()] * 4,
        out_specs=[whole(), whole()],
        scratch_shapes=[
            pltpu.VMEM((heads, TILE, LANES), BF16),
            pltpu.VMEM((heads, keys, TILE), F32),
            pltpu.VMEM((heads, 8, TILE), F32),
            pltpu.VMEM((heads, 8, TILE), F32),
            pltpu.VMEM((heads, HEAD_DIM, TILE), F32),
        ],
    )(bounds, q, k, v, start)


def backward_kernel(
    rows, bounds, q_ref, k_ref, v_ref, o_ref, g_ref, lse_ref, start_ref, cos_ref, sin_ref,
    dq_ref, dk_ref, dv_ref, q_buf, g_buf, d_buf, dq_acc, dk_acc, dv_acc,
):
    heads = q_buf.shape[0]
    zero = jnp.zeros((), BF16)
    scale = HEAD_DIM**-0.5
    dk_acc[...] = jnp.zeros_like(dk_acc)
    dv_acc[...] = jnp.zeros_like(dv_acc)
    for t in range(-(-rows // TILE)):
        low, high = bounds[0, t], bounds[1, t]
        n = min(TILE, rows - t * TILE)
        span = slice(t * TILE, (t + 1) * TILE)
        here = slice(t * TILE, t * TILE + n)
        start = start_ref[:, span]
        row = t * TILE + lax.broadcasted_iota(jnp.int32, (1, TILE), 1)
        for pair in range(-(-heads // 2)):
            c = pair * LANES
            scaled = (q_ref[here, c : c + LANES].astype(F32) * scale).astype(BF16)
            grad = g_ref[here, c : c + LANES]
            product = grad.astype(F32) * o_ref[here, c : c + LANES].astype(F32)
            if n < TILE:
                product = jnp.concatenate([product, jnp.zeros((TILE - n, LANES), F32)], axis=0)
            product = jnp.transpose(product)
            for h in range(2 * pair, min(heads, 2 * pair + 2)):
                q_buf[h, :n, :] = jnp.where(lane_half(h), scaled, zero)
                g_buf[h, :n, :] = jnp.where(lane_half(h), grad, zero)
                if n < TILE:
                    q_buf[h, n:, :] = jnp.zeros((TILE - n, LANES), BF16)
                    g_buf[h, n:, :] = jnp.zeros((TILE - n, LANES), BF16)
                d_buf[h : h + 1, :] = jnp.sum(product[HEAD_DIM * (h % 2) : HEAD_DIM * (h % 2) + HEAD_DIM], axis=0, keepdims=True)
        dq_acc[...] = jnp.zeros_like(dq_acc)

        @pl.loop(low, high)
        def _(i):
            at = pl.multiple_of(i * TILE, TILE)
            place = at + lax.broadcasted_iota(jnp.int32, (TILE, TILE), 0)
            allowed = (place >= start) & (place <= row)
            for pair in range(-(-heads // 2)):
                c = pair * LANES
                k = k_ref[pl.ds(at, TILE), c : c + LANES]
                v = v_ref[pl.ds(at, TILE), c : c + LANES]
                dq = dk = dv = 0.0
                for h in range(2 * pair, min(heads, 2 * pair + 2)):
                    p = jnp.where(allowed, jnp.exp(dot_nt(k, q_buf[h]) - lse_ref[h : h + 1, span]), 0.0)
                    ds = (p * (dot_nt(v, g_buf[h]) - d_buf[h : h + 1, :])).astype(BF16)
                    dv = dv + dot(p.astype(BF16), g_buf[h])
                    dk = dk + dot(ds, q_buf[h])
                    dq = dq + dot_tn(ds, jnp.where(lane_half(h), k, zero))
                dk_acc[pl.ds(at, TILE), c : c + LANES] += dk
                dv_acc[pl.ds(at, TILE), c : c + LANES] += dv
                dq_acc[:, c : c + LANES] += dq

        for c in range(0, dk_ref.shape[1], LANES):
            dq = dq_acc[:n, c : c + LANES] * scale
            dq_ref[here, c : c + LANES] = turn(dq, cos_ref[here, :], sin_ref[here, :], -1.0).astype(BF16)
    for c in range(0, dk_ref.shape[1], LANES):
        dk_ref[:, c : c + LANES] = turn(dk_acc[:, c : c + LANES], cos_ref[...], sin_ref[...], -1.0).astype(BF16)
    dv_ref[...] = dv_acc[...].astype(BF16)


def attend_back(bounds, q, k, v, o, grad, lse, start, cos, sin, heads):
    rows = q.shape[0]
    keys, width = k.shape
    tall = jax.ShapeDtypeStruct((keys, width), BF16)
    return call(
        functools.partial(backward_kernel, rows),
        "attend_back",
        rows * rows * heads * HEAD_DIM * 5,
        keys * width * 16,
        out_shape=(jax.ShapeDtypeStruct((rows, width), BF16), tall, tall),
        in_specs=[pl.BlockSpec(memory_space=pltpu.SMEM)] + [whole()] * 9,
        out_specs=[whole()] * 3,
        scratch_shapes=[
            pltpu.VMEM((heads, TILE, LANES), BF16),
            pltpu.VMEM((heads, TILE, LANES), BF16),
            pltpu.VMEM((heads, TILE), F32),
            pltpu.VMEM((TILE, width), F32),
            pltpu.VMEM((keys, width), F32),
            pltpu.VMEM((keys, width), F32),
        ],
    )(bounds, q, k, v, o, grad, lse, start, cos, sin)


def joined(ref):
    shape = ref.shape
    return ref[...].reshape(shape[0] * shape[2], shape[3])


def once(shape):
    return pl.BlockSpec(shape, lambda i: (0,) * len(shape), pipeline_mode=pl.Buffered(1))


def feed_kernel(count, *refs):
    n_refs, dy_refs, weights = refs[:count], refs[count : 2 * count], refs[2 * count : 2 * count + 3]
    hidden_ref, gate_ref, up_ref, kept_ref, sent_ref, gain_ref, acc = refs[2 * count + 3 :]
    step = pl.program_id(0)
    block = n_refs[0].shape[0]

    @pl.when(step == 0)
    def _():
        acc[...] = jnp.zeros_like(acc)

    gate_w, up_w, down_w = (joined(ref) for ref in weights)
    for i in range(count):
        rows = slice(i * block, (i + 1) * block)
        normed = n_refs[i][...]
        gate = dot(normed, gate_w)
        up = dot(normed, up_w)
        grad = dot(dy_refs[i][...], down_w)
        sig = 1.0 / (1.0 + jnp.exp(-gate))
        silu = gate * sig
        hidden_ref[rows, :] = (silu * up).astype(BF16)
        gate_grad = (grad * up * sig * (1.0 + gate * (1.0 - sig))).astype(BF16)
        up_grad = (grad * silu).astype(BF16)
        gate_ref[rows, :] = gate_grad
        up_ref[rows, :] = up_grad
        acc[rows, :] += dot_nt(gate_grad, gate_w) + dot_nt(up_grad, up_w)

    @pl.when(step == pl.num_programs(0) - 1)
    def _():
        total = 0.0
        for i in range(count):
            values = acc[i * block : (i + 1) * block, :]
            store_block(kept_ref, sent_ref, i, block, values)
            total = total + column_sums(values, n_refs[i][...])
        gain_ref[...] = total


def feed(normed, dy, weights):
    count = len(normed)
    block, depth = normed[0].shape
    rows = count * block
    fsdp, _, columns, units = weights.shape
    tile = min(TILE, units)
    kind = lambda k: pl.BlockSpec((fsdp, 1, columns, tile), lambda i: (0, k, 0, i))
    out = pl.BlockSpec((rows, tile), lambda i: (0, i))
    wide = jax.ShapeDtypeStruct((rows, units), BF16)
    half = once((rows // 2, depth))
    return call(
        functools.partial(feed_kernel, count),
        "feed",
        rows * depth * units * 10,
        depth * units * 6,
        grid=(units // tile,),
        out_shape=[wide, wide, wide] + halves(rows, depth) + [jax.ShapeDtypeStruct((8, depth), F32)],
        in_specs=[once((block, depth))] * (2 * count) + [kind(0), kind(1), kind(2)],
        out_specs=[out, out, out, half, half, once((8, depth))],
        scratch_shapes=[pltpu.VMEM((rows, depth), F32)],
    )(*normed, *dy, weights, weights, weights)


def feed_weights_kernel(count, *refs):
    blocks = refs[: 2 * count]
    gate_ref, up_ref, hidden_ref, out_ref, normed, dy = refs[2 * count :]
    block = blocks[0].shape[0]
    fsdp, _, columns, tile = out_ref.shape

    @pl.when(pl.program_id(0) == 0)
    def _():
        for i in range(count):
            normed[i * block : (i + 1) * block, :] = blocks[i][...]
            dy[i * block : (i + 1) * block, :] = blocks[count + i][...]

    for kind, (left, right) in enumerate(((normed, gate_ref), (normed, up_ref), (dy, hidden_ref))):
        out_ref[:, kind] = dot_tn(left[...], right[...]).astype(BF16).reshape(fsdp, columns, tile)


def feed_weights(normed, dy, gate_grad, up_grad, hidden, fsdp):
    count = len(normed)
    block, depth = normed[0].shape
    rows, units = hidden.shape
    columns = depth // fsdp
    tile = min(TILE, units)
    return call(
        functools.partial(feed_weights_kernel, count),
        "feed_weights",
        rows * depth * units * 6,
        depth * units * 6,
        grid=(units // tile,),
        out_shape=jax.ShapeDtypeStruct((fsdp, 3, columns, units), BF16),
        in_specs=[once((block, depth))] * (2 * count) + [pl.BlockSpec((rows, tile), lambda i: (0, i))] * 3,
        out_specs=pl.BlockSpec((fsdp, 3, columns, tile), lambda i: (0, 0, 0, i)),
        scratch_shapes=[pltpu.VMEM((rows, depth), BF16)] * 2,
    )(*normed, *dy, gate_grad, up_grad, hidden)


def feed_out_kernel(count, hidden_ref, weight_ref, kept_ref, sent_ref):
    weight = joined(weight_ref)
    block = hidden_ref.shape[0] // count
    for i in range(count):
        values = dot_nt(hidden_ref[i * block : (i + 1) * block, :], weight)
        store_block(kept_ref, sent_ref, i, block, values)


def feed_out(hidden, weights, count):
    rows = hidden.shape[0]
    fsdp, _, columns, units = weights.shape
    depth = fsdp * columns
    return call(
        functools.partial(feed_out_kernel, count),
        "feed_out",
        rows * depth * units * 2,
        rows * depth * 2,
        grid=(1,),
        out_shape=halves(rows, depth),
        in_specs=[once((rows, units)), pl.BlockSpec((fsdp, 1, columns, units), lambda i: (0, 2, 0, 0))],
        out_specs=[once((rows // 2, depth))] * 2,
    )(hidden, weights)


def quarter_places():
    place = 2 * lax.axis_index("chip") + lax.axis_index("core")
    return place, place ^ 2, place ^ 1, place ^ 3


def finish_feed_kernel(own_ref, across_ref, came_ref, gate_ref, up_ref, down_ref):
    units = own_ref.shape[2]
    for place, piece in zip(quarter_places(), (own_ref, across_ref, came_ref.at[0], came_ref.at[1])):
        span = pl.ds(pl.multiple_of(place * units, LANES), units)
        gate_ref[:, span] = piece[0].astype(F32)
        up_ref[:, span] = piece[1].astype(F32)
        down_ref[span, :] = jnp.transpose(piece[2].astype(F32))


def finish_feed(own, across, came):
    _, columns, units = own.shape
    wide = jax.ShapeDtypeStruct((columns, 4 * units), F32)
    return call(
        finish_feed_kernel,
        "finish_feed",
        0,
        own.size * 24,
        out_shape=(wide, wide, jax.ShapeDtypeStruct((4 * units, columns), F32)),
        in_specs=[whole()] * 3,
        out_specs=[whole()] * 3,
    )(own, across, came)


def finish_attention_kernel(real, own_ref, across_ref, came_ref, q_ref, k_ref, v_ref, out_ref, buf):
    part = own_ref.shape[1]
    pieces = (own_ref, across_ref, came_ref.at[0], came_ref.at[1])
    for kind, ref in enumerate((q_ref, k_ref, v_ref, out_ref)):
        for place, piece in zip(quarter_places(), pieces):
            buf[pl.ds(pl.multiple_of(place * part, 16), part), :] = piece[kind].astype(F32)
        ref[...] = buf[:real, :] if kind == 3 else jnp.transpose(buf[...])[:, :real]


def finish_attention(own, across, came, real):
    _, part, columns = own.shape
    into = jax.ShapeDtypeStruct((columns, real), F32)
    return call(
        functools.partial(finish_attention_kernel, real),
        "finish_attention",
        0,
        own.size * 24,
        out_shape=(into, into, into, jax.ShapeDtypeStruct((real, columns), F32)),
        in_specs=[whole()] * 3,
        out_specs=[whole()] * 4,
        scratch_shapes=[pltpu.VMEM((4 * part, columns), F32)],
    )(own, across, came)


def normalize_back(values, inverse, gain, grad_rows):
    scaled = grad_rows * gain
    return inverse * scaled - values * inverse**3 * jnp.mean(scaled * values, axis=-1, keepdims=True)


def inverse_rms(values):
    return lax.rsqrt(jnp.mean(values * values, axis=-1, keepdims=True) + EPSILON)


def pull_fsdp(values, step):
    count = lax.axis_size("fsdp")
    return lax.ppermute(values, "fsdp", [(i, (i - step) % count) for i in range(count)])


def gather_gains(gains):
    count = lax.axis_size("fsdp")
    rolled = jnp.concatenate([gains] + [pull_fsdp(gains, step) for step in range(1, count)], axis=1).astype(F32)
    twice = jnp.concatenate([rolled, rolled], axis=1)
    at = (count - lax.axis_index("fsdp")) % count * gains.shape[1]
    return lax.dynamic_slice_in_dim(twice, at, rolled.shape[1], 1)


def over_tp(gains):
    if lax.axis_size("tp") == 2:
        return gains + swap_tp(gains)
    return lax.psum(gains, "tp")


def over_fsdp(gains):
    blocks = jnp.stack(jnp.split(gains, lax.axis_size("fsdp"), axis=1))
    return jnp.sum(lax.all_to_all(blocks, "fsdp", 0, 0, tiled=True), axis=0)


def scatter_fsdp(values):
    shape = values.shape
    flat = values.reshape((shape[0] * shape[1],) + shape[2:])
    return lax.psum_scatter(flat, "fsdp", scatter_dimension=0, tiled=True)


def shards(tokens, segment_ids, wq, wk, wv, wo, w_gate, w_up, w_down, gain_attn, gain_ffn, cotangent):
    tokens, cotangent, segment_ids = tokens[0], cotangent[0], segment_ids[0]
    fsdp = lax.axis_size("fsdp")
    chip, core = lax.axis_index("chip"), lax.axis_index("core")
    place = 2 * chip + core
    rows = 4 * segment_ids.shape[0]
    real_width = wq.shape[1]
    part = -(-real_width // (4 * HEAD_DIM)) * HEAD_DIM
    heads = part // HEAD_DIM
    width = -(-part // LANES) * LANES
    keys = -(-rows // TILE) * TILE
    both_links = lax.axis_size("tp") == 2

    pad = ((0, 0), (0, 4 * part - real_width))
    own_piece = cut_attention(*[jnp.pad(w, pad) for w in (wq, wk, wv)], jnp.pad(wo, pad[::-1]))
    feed_piece = jnp.stack([take_quarter(w_gate, place, 1), take_quarter(w_up, place, 1), jnp.transpose(take_quarter(w_down, place, 0))])

    position = after(jnp.arange(keys, dtype=jnp.int32), own_piece).astype(F32)
    pair_index = (jnp.arange(LANES, dtype=jnp.int32) % (HEAD_DIM // 2)).astype(F32)
    angles = position[:, None] * (10000.0 ** (-pair_index * 2.0 / HEAD_DIM))[None, :]

    def normed(values):
        values = values.astype(F32)
        return (values * inverse_rms(values) * gain_one).astype(BF16)

    if both_links:
        first = lambda values: [values, swap_tp(values), swap_chip(values)]
        second = lambda blocks: widen_core(blocks) + far_block(*blocks)[3:]
        third = lambda blocks: blocks[:3] + blocks[6:] + blocks[3:6] + [swap_core(blocks[6])]
    else:
        first, second, third = lambda values: widen_planes(values)[0], widen_core, lambda blocks: blocks
    ring = [own_piece]
    block, own, gains, ids_other, cos, sin = together(
        pull_fsdp(ring[0], 1),
        first(tokens),
        gather_gains(jnp.stack([gain_attn, gain_ffn])),
        swap_core(segment_ids),
        jnp.cos(angles),
        jnp.sin(angles),
    )
    ring.append(block)
    gain_one, gain_two = gains
    ids_chip = jnp.concatenate(in_order(segment_ids, ids_other, core == 0))
    block, own, ids_across = together(pull_fsdp(ring[-1], 1), second(own), swap_chip(ids_chip))
    ring.append(block)
    feed_weight = lax.all_gather(after(feed_piece, block), "fsdp", axis=0, tiled=False)
    ids = jnp.concatenate(in_order(ids_chip, ids_across, chip == 0))
    start = jnp.sum((ids[None, :] < ids[:, None]).astype(jnp.int32), axis=1)
    dy = cotangent
    for step in range(2, fsdp - 1):
        if step == 2:
            early = [normed(values) for values in own[:6]]
            block, own, early, dy = together(pull_fsdp(ring[-1], 1), third(own), early, first(after(cotangent, block)))
        else:
            block = pull_fsdp(ring[-1], 1)
        ring.append(block)
    weights = place_weights(ring, width)
    tiles = -(-rows // TILE)
    ends = [-(-min((t + 1) * TILE, rows) // TILE) for t in range(tiles)]
    bounds = jnp.stack([start[::TILE] // TILE, jnp.array(ends, jnp.int32)])
    start = jnp.pad(start, (0, tiles * TILE - rows), constant_values=2 * keys)[None]

    if both_links:
        blocks = early[:3] + [normed(own[3])] + early[3:] + [normed(own[7])]
    else:
        blocks = early
    count = len(blocks)
    inputs = tokens.astype(F32)
    inv_one = inverse_rms(inputs)
    q, k, v = project(blocks, weights, cos, sin, keys)
    dy = second(after(dy, q))
    attended, lse = attend(bounds, q, k, v, start, heads)
    attended, dy = together(attended, dy)
    dy = third(dy)
    leaving = narrow_first(*out_project(attended, weights, count), feed_weight)
    attention_rows, dy = narrow_second(leaving, lambda rows, dy=dy: dy)
    residual = inputs + attention_rows

    inv_two = inverse_rms(residual)
    normed_two = widen((residual * inv_two * gain_two).astype(BF16))
    hidden, gate_grad, up_grad, kept, sent, gain_two_sums = feed(normed_two, dy, feed_weight)
    normed_two_grad, feed_grads = narrow(
        kept, sent, lambda leaving: feed_weights(normed_two, dy, after(gate_grad, leaving), up_grad, hidden, fsdp)
    )
    feed_sums = scatter_fsdp(feed_grads)
    resid_grad = cotangent.astype(F32) + normalize_back(residual, inv_two, gain_two, normed_two_grad)
    resid_low = resid_grad.astype(BF16)

    out_partial = feed_out(after(hidden, resid_low), feed_weight, count)
    planes, (out_kept, out_sent) = widen_planes(resid_low, tuple(out_partial))
    grad_blocks = widen_core(planes)
    out_grad, out_grads = out_back(attended, weights, grad_blocks, fsdp, part)
    leaving = narrow_first(out_kept, out_sent, out_grad)
    dq, dk, dv = attend_back(bounds, q, k, v, attended, after(out_grad, leaving), lse, start, cos, sin, heads)
    layer_rows, (dq, feed_sums) = narrow_second(leaving, lambda rows, dq=dq, sums=feed_sums: (dq, sums))
    layer_out = residual + layer_rows
    feed_across = swap_chip(feed_sums)
    kept, sent, gain_one_sums = project_back(dq, dk, dv, weights, blocks)
    gains = jnp.stack([jnp.sum(gain_one_sums, axis=0) / gain_one, jnp.sum(gain_two_sums, axis=0) / gain_two])
    gains_tp = over_tp(gains)
    project_grads = project_weights(after(dq, sent), dk, dv, out_grads, blocks)
    sums = scatter_fsdp(project_grads)
    (sent, feed_across, gains), _ = together((sent, feed_across, gains_tp), project_grads)
    gains_core = swap_core(gains)
    feed_came = swap_core(jnp.stack([feed_sums, feed_across]))
    leaving, (gains, gains_core, feed_came) = together(narrow_first(kept, sent), (gains, gains_core, feed_came))
    gains = gains + gains_core
    gains_chip = swap_chip(gains)
    normed_grad, gains = narrow_second(leaving, lambda rows: gains + gains_chip)
    gain_own = over_fsdp(gains)
    grad_input = resid_grad + normalize_back(inputs, inv_one, gain_one, normed_grad)

    sums = after(sums, grad_input, gain_own)
    across = swap_chip(sums)
    feed_all = finish_feed(feed_sums, feed_across, after(feed_came, sums))
    across, (gate_all, up_all, down_all) = together(across, tuple(feed_all))
    q_all, k_all, v_all, out_all = finish_attention(sums, across, swap_core(jnp.stack([sums, across])), real_width)
    return (
        layer_out.astype(BF16)[None],
        grad_input[None],
        q_all,
        k_all,
        v_all,
        out_all,
        gate_all,
        up_all,
        down_all,
        gain_own[0],
        gain_own[1],
    )


def solution(mesh):
    devices = mesh.devices.reshape(mesh.shape["fsdp"], mesh.shape["ctx"] // 2, 2, mesh.shape["tp"])
    split = jax.sharding.Mesh(devices, ("fsdp", "chip", "core", "tp"))
    rows = P("fsdp", ("chip", "core", "tp"), None)
    into, outof, gain = P("fsdp", "tp"), P("tp", "fsdp"), P("fsdp")
    return jax.shard_map(
        shards,
        mesh=split,
        in_specs=(rows, P("fsdp", ("chip", "core")), into, into, into, outof, into, into, outof, gain, gain, rows),
        out_specs=(rows, rows, into, into, into, outof, into, into, outof, gain, gain),
        check_vma=False,
    )
```

```python
import functools

import jax
import jax.numpy as jnp
from jax import lax
from jax.experimental import pallas as pl
from jax.experimental.pallas import tpu as pltpu
from jax.sharding import PartitionSpec as P

HEAD_DIM = 64
EPSILON = 1e-05
MASKED = -1e30
BF16 = jnp.bfloat16
F32 = jnp.float32
TILE = 256
LANES = 128
VMEM_BYTES = 60 * 1024 * 1024


def dot(left, right):
    return jnp.dot(left, right, preferred_element_type=F32)


def dot_nt(left, right):
    return lax.dot_general(left, right, (((1,), (1,)), ((), ())), preferred_element_type=F32)


def dot_tn(left, right):
    return lax.dot_general(left, right, (((0,), (0,)), ((), ())), preferred_element_type=F32)


def swap_chip(values):
    return lax.ppermute(values, "chip", [(0, 1), (1, 0)])


def swap_core(values):
    return lax.ppermute(values, "core", [(0, 1), (1, 0)])


def swap_tp(values):
    return lax.ppermute(values, "tp", [(0, 1), (1, 0)])


def in_order(mine, other, mine_first):
    return [jnp.where(mine_first, mine, other), jnp.where(mine_first, other, mine)]


def together(*values):
    return lax.optimization_barrier(values)


def after(values, *earlier):
    return lax.optimization_barrier((values, earlier))[0]


def widen_planes(rows, meanwhile=None):
    if lax.axis_size("tp") != 2:
        gathered = lax.all_gather(rows, "tp", axis=0, tiled=True)
        return [gathered, swap_chip(gathered)], meanwhile
    (beside, across), meanwhile = together((swap_tp(rows), swap_chip(rows)), meanwhile)
    return far_block(rows, beside, across), meanwhile


def meet(beside, across, meanwhile):
    return (beside, across) if meanwhile is None else after((beside, across), meanwhile)


def far_block(rows, beside, across):
    cut = rows.shape[0] // 32 * 16
    far = jnp.concatenate([swap_tp(across[:cut]), swap_chip(beside[cut:])], axis=0)
    return [rows, beside, across, far]


def widen_core(blocks):
    return blocks + [swap_core(block) for block in blocks]


def widen(rows):
    return widen_core(widen_planes(rows)[0])


def block_offset(index, half):
    chip, core = lax.axis_index("chip"), lax.axis_index("core")
    if lax.axis_size("tp") != 2:
        return (chip ^ index % 2) * 2 * half + (core ^ index // 2) * half
    place = lax.axis_index("tp")
    return (chip ^ index // 2 % 2) * 2 * half + (core ^ index // 4) * half + (place ^ index % 2) * (half // 2)


def narrow_first(kept, sent, meanwhile=None):
    came = swap_core(sent)
    if lax.axis_size("tp") != 2:
        rows = kept.shape[0] // 2
        total = kept.astype(F32) + came.astype(F32)
        return ((total[:rows] + swap_chip(total[rows:].astype(BF16)).astype(F32)).astype(BF16),)
    rows = kept.shape[0] // 4
    cut = rows // 32 * 16

    def block(index, first, last):
        where = slice(index * rows + first, index * rows + last)
        return kept[where].astype(F32) + came[where].astype(F32)

    top, bottom = meet(swap_chip(block(3, 0, cut).astype(BF16)), swap_tp(block(3, cut, rows).astype(BF16)), meanwhile)
    beside = jnp.concatenate([block(1, 0, cut) + top.astype(F32), block(1, cut, rows)], axis=0).astype(BF16)
    across = jnp.concatenate([block(2, 0, cut), block(2, cut, rows) + bottom.astype(F32)], axis=0).astype(BF16)
    return beside, across, block(0, 0, rows)


def narrow_second(leaving, meanwhile=None):
    done = None
    if len(leaving) == 1:
        if meanwhile is not None:
            done = meanwhile(leaving)
        return lax.psum_scatter(leaving[0], "tp", scatter_dimension=0, tiled=True).astype(F32), done
    from_tp, from_chip = swap_tp(leaving[0]), swap_chip(leaving[1])
    if meanwhile is not None:
        (from_tp, from_chip), done = together((from_tp, from_chip), meanwhile(leaving[:2]))
    return leaving[2] + from_tp.astype(F32) + from_chip.astype(F32), done


def narrow(kept, sent, meanwhile=None):
    return narrow_second(narrow_first(kept, sent), meanwhile)


def take_quarter(values, index, axis):
    size = values.shape[axis] // 4
    return lax.dynamic_slice_in_dim(values, index * size, size, axis)


def call(kernel, name, flops, moved, **rest):
    return pl.pallas_call(
        kernel,
        name=name,
        cost_estimate=pl.CostEstimate(flops=flops, bytes_accessed=moved, transcendentals=0),
        compiler_params=pltpu.CompilerParams(vmem_limit_bytes=VMEM_BYTES),
        **rest,
    )


def whole():
    return pl.BlockSpec(memory_space=pltpu.VMEM)


def turn(values, cos, sin, direction):
    lane = lax.broadcasted_iota(jnp.int32, (1, LANES), 1)
    partner = jnp.where((lane // 32) % 2 == 0, pltpu.roll(values, 96, 1) * -direction, pltpu.roll(values, 32, 1) * direction)
    return values * cos + partner * sin


def block_spans(count, rows):
    block = rows // count
    return [pl.ds(pl.multiple_of(block_offset(i, rows // 4), 16), block) for i in range(count)]


def project_kernel(count, rows, *refs):
    blocks = refs[:count]
    weight_ref, cos_ref, sin_ref, q_ref, k_ref, v_ref = refs[count:]
    width = q_ref.shape[1]
    for ref in (k_ref, v_ref):
        ref[rows:, :] = jnp.zeros((ref.shape[0] - rows, width), BF16)
    for block, span in zip(blocks, block_spans(count, rows)):
        cos, sin = cos_ref[span, :], sin_ref[span, :]
        for kind, out_ref in ((0, q_ref), (1, k_ref)):
            values = dot_nt(block[...], weight_ref[kind])
            for c in range(0, width, LANES):
                out_ref[span, c : c + LANES] = turn(values[:, c : c + LANES], cos, sin, 1.0).astype(BF16)
        v_ref[span, :] = dot_nt(block[...], weight_ref[2]).astype(BF16)


def project(blocks, weights, cos, sin, keys):
    count = len(blocks)
    block, depth = blocks[0].shape
    rows = count * block
    width = weights.shape[1]
    tall = jax.ShapeDtypeStruct((keys, width), BF16)
    return call(
        functools.partial(project_kernel, count, rows),
        "project",
        rows * depth * width * 6,
        rows * depth * 2,
        out_shape=(jax.ShapeDtypeStruct((rows, width), BF16), tall, tall),
        in_specs=[whole()] * (count + 3),
        out_specs=[whole()] * 3,
    )(*blocks, weights, cos, sin)


def cut_kernel(q_ref, k_ref, v_ref, out_ref, piece_ref, buf):
    part = piece_ref.shape[1]
    span = pl.ds(pl.multiple_of(quarter_places()[0] * part, 16), part)
    for kind, ref in enumerate((q_ref, k_ref, v_ref)):
        buf[...] = jnp.transpose(ref[...])
        piece_ref[kind] = buf[span, :]
    piece_ref[3] = out_ref[span, :]


def cut_attention(wq, wk, wv, wo):
    width, columns = wo.shape
    return call(
        cut_kernel,
        "cut_attention",
        0,
        width * columns * 8,
        out_shape=jax.ShapeDtypeStruct((4, width // 4, columns), BF16),
        in_specs=[whole()] * 4,
        out_specs=whole(),
        scratch_shapes=[pltpu.VMEM((width, columns), BF16)],
    )(wq, wk, wv, wo)


def place_kernel(*refs):
    blocks, out_ref = refs[:-1], refs[-1]
    kinds, part, columns = blocks[0].shape
    me = lax.axis_index("fsdp")
    if part < out_ref.shape[1]:
        out_ref[:, part:, :] = jnp.zeros((kinds, out_ref.shape[1] - part, out_ref.shape[2]), BF16)
    for i, block in enumerate(blocks):
        at = pl.multiple_of((me + i) % len(blocks) * columns, LANES)
        out_ref[:, :part, pl.ds(at, columns)] = block[...]


def place_weights(blocks, width):
    kinds, _, columns = blocks[0].shape
    depth = len(blocks) * columns
    return call(
        place_kernel,
        "place_weights",
        0,
        kinds * width * depth * 4,
        out_shape=jax.ShapeDtypeStruct((kinds, width, depth), BF16),
        in_specs=[whole()] * len(blocks),
        out_specs=whole(),
    )(*blocks)


def store_block(kept_ref, sent_ref, i, block, values):
    half = kept_ref.shape[0]
    at = i * block
    if at < half:
        kept_ref[at : at + block, :] = values.astype(BF16)
    else:
        sent_ref[at - half : at - half + block, :] = values.astype(BF16)


def halves(rows, depth):
    return [jax.ShapeDtypeStruct((rows // 2, depth), BF16)] * 2


def out_kernel(count, o_ref, weight_ref, kept_ref, sent_ref):
    rows = o_ref.shape[0]
    for i, span in enumerate(block_spans(count, rows)):
        store_block(kept_ref, sent_ref, i, rows // count, dot(o_ref[span, :], weight_ref[3]))


def out_project(attended, weights, count):
    rows, width = attended.shape
    depth = weights.shape[2]
    return call(
        functools.partial(out_kernel, count),
        "out_project",
        rows * width * depth * 2,
        rows * depth * 2,
        out_shape=halves(rows, depth),
        in_specs=[whole(), whole()],
        out_specs=[whole(), whole()],
    )(attended, weights)


def out_back_kernel(count, o_ref, weight_ref, *refs):
    blocks, (grad_ref, out_ref, all_rows) = refs[:count], refs[count:]
    rows = o_ref.shape[0]
    for block, span in zip(blocks, block_spans(count, rows)):
        grad = block[...]
        grad_ref[span, :] = dot_nt(grad, weight_ref[3]).astype(BF16)
        all_rows[span, :] = grad
    total = dot_tn(o_ref[...], all_rows[...])
    fsdp, _, part, columns = out_ref.shape
    for z in range(fsdp):
        out_ref[z, 0] = total[:part, z * columns : (z + 1) * columns].astype(BF16)


def out_back(attended, weights, blocks, fsdp, part):
    rows, width = attended.shape
    depth = weights.shape[2]
    return call(
        functools.partial(out_back_kernel, len(blocks)),
        "out_back",
        rows * width * depth * 4,
        rows * depth * 2,
        out_shape=(
            jax.ShapeDtypeStruct((rows, width), BF16),
            jax.ShapeDtypeStruct((fsdp, 1, part, depth // fsdp), BF16),
        ),
        in_specs=[whole()] * (2 + len(blocks)),
        out_specs=[whole()] * 2,
        scratch_shapes=[pltpu.VMEM((rows, depth), BF16)],
    )(attended, weights, *blocks)


def project_weights_kernel(count, dq_ref, dk_ref, dv_ref, done_ref, *refs):
    blocks, (out_ref, all_rows) = refs[:count], refs[count:]
    rows = all_rows.shape[0]
    for block, span in zip(blocks, block_spans(count, rows)):
        all_rows[span, :] = block[...]
    part = out_ref.shape[2]
    for kind, grad in enumerate((dq_ref, dk_ref, dv_ref)):
        out_ref[0, kind] = dot_tn(grad[:rows, :], all_rows[...])[:part].astype(BF16)
    out_ref[0, 3] = done_ref[0, 0]


def project_weights(dq, dk, dv, out_grads, blocks):
    rows, width = dq.shape
    fsdp, _, part, _ = out_grads.shape
    block, depth = blocks[0].shape
    columns = depth // fsdp
    fixed = lambda array: pl.BlockSpec(array.shape, lambda z: (0, 0))
    return call(
        functools.partial(project_weights_kernel, len(blocks)),
        "project_weights",
        rows * width * depth * 6,
        rows * depth * 2,
        grid=(fsdp,),
        out_shape=jax.ShapeDtypeStruct((fsdp, 4, part, columns), BF16),
        in_specs=[fixed(dq), fixed(dk), fixed(dv), pl.BlockSpec((1, 1, part, columns), lambda z: (z, 0, 0, 0))]
        + [pl.BlockSpec((block, columns), lambda z: (0, z))] * len(blocks),
        out_specs=pl.BlockSpec((1, 4, part, columns), lambda z: (z, 0, 0, 0)),
        scratch_shapes=[pltpu.VMEM((rows, columns), BF16)],
    )(dq, dk, dv, out_grads, *blocks)


def column_sums(grads, normed):
    product = grads * normed.astype(F32)
    return jnp.sum(product.reshape(product.shape[0] // 8, 8, product.shape[1]), axis=0)


def project_back_kernel(count, dq_ref, dk_ref, dv_ref, weight_ref, *refs):
    blocks, (kept_ref, sent_ref, gain_ref) = refs[:count], refs[count:]
    rows = dq_ref.shape[0]
    sums = 0.0
    for i, (block, span) in enumerate(zip(blocks, block_spans(count, rows))):
        total = dot(dq_ref[span, :], weight_ref[0]) + dot(dk_ref[span, :], weight_ref[1]) + dot(dv_ref[span, :], weight_ref[2])
        sums = sums + column_sums(total, block[...])
        store_block(kept_ref, sent_ref, i, rows // count, total)
    gain_ref[...] = sums


def project_back(dq, dk, dv, weights, blocks):
    rows, width = dq.shape
    depth = weights.shape[2]
    return call(
        functools.partial(project_back_kernel, len(blocks)),
        "project_back",
        rows * width * depth * 6,
        rows * depth * 4,
        out_shape=halves(rows, depth) + [jax.ShapeDtypeStruct((8, depth), F32)],
        in_specs=[whole()] * (4 + len(blocks)),
        out_specs=[whole()] * 3,
    )(dq, dk, dv, weights, *blocks)


def lane_half(head):
    return (lax.broadcasted_iota(jnp.int32, (1, LANES), 1) // HEAD_DIM) == head % 2


def forward_kernel(rows, bounds, q_ref, k_ref, v_ref, start_ref, o_ref, lse_ref, q_buf, s_buf, top_buf, sum_buf, acc_buf):
    heads = q_buf.shape[0]
    zero = jnp.zeros((), BF16)
    for t in range(-(-rows // TILE)):
        low, high = bounds[0, t], bounds[1, t]
        n = min(TILE, rows - t * TILE)
        span = slice(t * TILE, (t + 1) * TILE)
        start = start_ref[:, span]
        row = t * TILE + lax.broadcasted_iota(jnp.int32, (1, TILE), 1)
        for h in range(heads):
            c = (h // 2) * LANES
            scaled = (q_ref[t * TILE : t * TILE + n, c : c + LANES].astype(F32) * HEAD_DIM**-0.5).astype(BF16)
            q_buf[h, :n, :] = jnp.where(lane_half(h), scaled, zero)
            if n < TILE:
                q_buf[h, n:, :] = jnp.zeros((TILE - n, LANES), BF16)
        top_buf[...] = jnp.full_like(top_buf, MASKED)
        sum_buf[...] = jnp.zeros_like(sum_buf)
        acc_buf[...] = jnp.zeros_like(acc_buf)

        @pl.loop(low, high)
        def _(i):
            at = pl.multiple_of(i * TILE, TILE)
            place = at + lax.broadcasted_iota(jnp.int32, (TILE, TILE), 0)
            allowed = (place >= start) & (place <= row)
            for h in range(heads):
                c = (h // 2) * LANES
                s = jnp.where(allowed, dot_nt(k_ref[pl.ds(at, TILE), c : c + LANES], q_buf[h]), MASKED)
                s_buf[h, pl.ds(at, TILE), :] = s
                top_buf[h] = jnp.maximum(top_buf[h], jnp.max(s.reshape(TILE // 8, 8, TILE), axis=0))

        tops = [jnp.max(top_buf[h], axis=0, keepdims=True) for h in range(heads)]

        @pl.loop(low, high)
        def _(i):
            at = pl.multiple_of(i * TILE, TILE)
            for h in range(heads):
                c = (h // 2) * LANES
                p = jnp.exp(s_buf[h, pl.ds(at, TILE), :] - tops[h])
                sum_buf[h] += jnp.sum(p.reshape(TILE // 8, 8, TILE), axis=0)
                both = dot_tn(v_ref[pl.ds(at, TILE), c : c + LANES], p.astype(BF16))
                acc_buf[h] += both[HEAD_DIM * (h % 2) : HEAD_DIM * (h % 2) + HEAD_DIM]

        for h in range(heads):
            total = jnp.sum(sum_buf[h], axis=0, keepdims=True)
            lse_ref[h : h + 1, span] = tops[h] + jnp.log(total)
            acc_buf[h] = acc_buf[h] / total
        for pair in range(o_ref.shape[1] // LANES):
            second = acc_buf[2 * pair + 1] if 2 * pair + 1 < heads else jnp.zeros((HEAD_DIM, TILE), F32)
            o = jnp.transpose(jnp.concatenate([acc_buf[2 * pair], second], axis=0))
            o_ref[t * TILE : t * TILE + n, pair * LANES : (pair + 1) * LANES] = o[:n].astype(BF16)


def attend(bounds, q, k, v, start, heads):
    rows = q.shape[0]
    keys, width = k.shape
    padded = -(-rows // TILE) * TILE
    return call(
        functools.partial(forward_kernel, rows),
        "attend",
        rows * rows * heads * HEAD_DIM * 2,
        keys * width * 8,
        out_shape=(jax.ShapeDtypeStruct((rows, width), BF16), jax.ShapeDtypeStruct((heads, padded), F32)),
        in_specs=[pl.BlockSpec(memory_space=pltpu.SMEM)] + [whole()] * 4,
        out_specs=[whole(), whole()],
        scratch_shapes=[
            pltpu.VMEM((heads, TILE, LANES), BF16),
            pltpu.VMEM((heads, keys, TILE), F32),
            pltpu.VMEM((heads, 8, TILE), F32),
            pltpu.VMEM((heads, 8, TILE), F32),
            pltpu.VMEM((heads, HEAD_DIM, TILE), F32),
        ],
    )(bounds, q, k, v, start)


def backward_kernel(
    rows, bounds, q_ref, k_ref, v_ref, o_ref, g_ref, lse_ref, start_ref, cos_ref, sin_ref,
    dq_ref, dk_ref, dv_ref, q_buf, g_buf, d_buf, dq_acc, dk_acc, dv_acc,
):
    heads = q_buf.shape[0]
    zero = jnp.zeros((), BF16)
    scale = HEAD_DIM**-0.5
    dk_acc[...] = jnp.zeros_like(dk_acc)
    dv_acc[...] = jnp.zeros_like(dv_acc)
    for t in range(-(-rows // TILE)):
        low, high = bounds[0, t], bounds[1, t]
        n = min(TILE, rows - t * TILE)
        span = slice(t * TILE, (t + 1) * TILE)
        here = slice(t * TILE, t * TILE + n)
        start = start_ref[:, span]
        row = t * TILE + lax.broadcasted_iota(jnp.int32, (1, TILE), 1)
        for pair in range(-(-heads // 2)):
            c = pair * LANES
            scaled = (q_ref[here, c : c + LANES].astype(F32) * scale).astype(BF16)
            grad = g_ref[here, c : c + LANES]
            product = grad.astype(F32) * o_ref[here, c : c + LANES].astype(F32)
            if n < TILE:
                product = jnp.concatenate([product, jnp.zeros((TILE - n, LANES), F32)], axis=0)
            product = jnp.transpose(product)
            for h in range(2 * pair, min(heads, 2 * pair + 2)):
                q_buf[h, :n, :] = jnp.where(lane_half(h), scaled, zero)
                g_buf[h, :n, :] = jnp.where(lane_half(h), grad, zero)
                if n < TILE:
                    q_buf[h, n:, :] = jnp.zeros((TILE - n, LANES), BF16)
                    g_buf[h, n:, :] = jnp.zeros((TILE - n, LANES), BF16)
                d_buf[h : h + 1, :] = jnp.sum(product[HEAD_DIM * (h % 2) : HEAD_DIM * (h % 2) + HEAD_DIM], axis=0, keepdims=True)
        dq_acc[...] = jnp.zeros_like(dq_acc)

        @pl.loop(low, high)
        def _(i):
            at = pl.multiple_of(i * TILE, TILE)
            place = at + lax.broadcasted_iota(jnp.int32, (TILE, TILE), 0)
            allowed = (place >= start) & (place <= row)
            for pair in range(-(-heads // 2)):
                c = pair * LANES
                k = k_ref[pl.ds(at, TILE), c : c + LANES]
                v = v_ref[pl.ds(at, TILE), c : c + LANES]
                dq = dk = dv = 0.0
                for h in range(2 * pair, min(heads, 2 * pair + 2)):
                    p = jnp.where(allowed, jnp.exp(dot_nt(k, q_buf[h]) - lse_ref[h : h + 1, span]), 0.0)
                    ds = (p * (dot_nt(v, g_buf[h]) - d_buf[h : h + 1, :])).astype(BF16)
                    dv = dv + dot(p.astype(BF16), g_buf[h])
                    dk = dk + dot(ds, q_buf[h])
                    dq = dq + dot_tn(ds, jnp.where(lane_half(h), k, zero))
                dk_acc[pl.ds(at, TILE), c : c + LANES] += dk
                dv_acc[pl.ds(at, TILE), c : c + LANES] += dv
                dq_acc[:, c : c + LANES] += dq

        for c in range(0, dk_ref.shape[1], LANES):
            dq = dq_acc[:n, c : c + LANES] * scale
            dq_ref[here, c : c + LANES] = turn(dq, cos_ref[here, :], sin_ref[here, :], -1.0).astype(BF16)
    for c in range(0, dk_ref.shape[1], LANES):
        dk_ref[:, c : c + LANES] = turn(dk_acc[:, c : c + LANES], cos_ref[...], sin_ref[...], -1.0).astype(BF16)
    dv_ref[...] = dv_acc[...].astype(BF16)


def attend_back(bounds, q, k, v, o, grad, lse, start, cos, sin, heads):
    rows = q.shape[0]
    keys, width = k.shape
    tall = jax.ShapeDtypeStruct((keys, width), BF16)
    return call(
        functools.partial(backward_kernel, rows),
        "attend_back",
        rows * rows * heads * HEAD_DIM * 5,
        keys * width * 16,
        out_shape=(jax.ShapeDtypeStruct((rows, width), BF16), tall, tall),
        in_specs=[pl.BlockSpec(memory_space=pltpu.SMEM)] + [whole()] * 9,
        out_specs=[whole()] * 3,
        scratch_shapes=[
            pltpu.VMEM((heads, TILE, LANES), BF16),
            pltpu.VMEM((heads, TILE, LANES), BF16),
            pltpu.VMEM((heads, TILE), F32),
            pltpu.VMEM((TILE, width), F32),
            pltpu.VMEM((keys, width), F32),
            pltpu.VMEM((keys, width), F32),
        ],
    )(bounds, q, k, v, o, grad, lse, start, cos, sin)


def joined(ref):
    shape = ref.shape
    return ref[...].reshape(shape[0] * shape[2], shape[3])


def once(shape):
    return pl.BlockSpec(shape, lambda i: (0,) * len(shape), pipeline_mode=pl.Buffered(1))


def feed_kernel(count, *refs):
    sources, weight_ref = refs[: 2 * count], refs[2 * count]
    hidden_ref, gate_ref, up_ref, kept_ref, sent_ref, gain_ref, rows_buf, weight_buf, sems = refs[2 * count + 1 :]
    block = sources[0].shape[0]
    fsdp, _, columns, units = weight_ref.shape

    def weight_copy(k):
        return pltpu.make_async_copy(weight_ref.at[:, k], weight_buf.at[k], sems.at[2 * count + k])

    def row_copy(i):
        return pltpu.make_async_copy(sources[i], rows_buf.at[i], sems.at[i])

    order = [i for pair in zip(range(count), range(count, 2 * count)) for i in pair]
    row_copy(0).start()
    for k in range(3):
        weight_copy(k).start()
    for i in order[1:]:
        row_copy(i).start()
    row_copy(0).wait()
    total = 0.0
    for i in range(count):
        rows = slice(i * block, (i + 1) * block)
        if i > 0:
            row_copy(i).wait()
        normed = rows_buf[i]

        def weight(k):
            if i == 0:
                weight_copy(k).wait()
            return weight_buf[k].reshape(fsdp * columns, units)

        gate_w = weight(0)
        gate = dot(normed, gate_w)
        up_w = weight(1)
        up = dot(normed, up_w)
        down_w = weight(2)
        row_copy(count + i).wait()
        grad = dot(rows_buf[count + i], down_w)
        sig = 1.0 / (1.0 + jnp.exp(-gate))
        silu = gate * sig
        hidden_ref[rows, :] = (silu * up).astype(BF16)
        gate_grad = (grad * up * sig * (1.0 + gate * (1.0 - sig))).astype(BF16)
        up_grad = (grad * silu).astype(BF16)
        gate_ref[rows, :] = gate_grad
        up_ref[rows, :] = up_grad
        values = dot_nt(gate_grad, gate_w) + dot_nt(up_grad, up_w)
        store_block(kept_ref, sent_ref, i, block, values)
        total = total + column_sums(values, normed)
    gain_ref[...] = total


def feed(normed, dy, weights):
    count = len(normed)
    block, depth = normed[0].shape
    rows = count * block
    fsdp, kinds, columns, units = weights.shape
    wide = jax.ShapeDtypeStruct((rows, units), BF16)
    return call(
        functools.partial(feed_kernel, count),
        "feed",
        rows * depth * units * 10,
        depth * units * 6,
        out_shape=[wide, wide, wide] + halves(rows, depth) + [jax.ShapeDtypeStruct((8, depth), F32)],
        in_specs=[pl.BlockSpec(memory_space=pl.ANY)] * (2 * count + 1),
        out_specs=[whole()] * 6,
        scratch_shapes=[
            pltpu.VMEM((2 * count, block, depth), BF16),
            pltpu.VMEM((kinds, fsdp, columns, units), BF16),
            pltpu.SemaphoreType.DMA((2 * count + kinds,)),
        ],
    )(*normed, *dy, weights)


def feed_weights_kernel(count, *refs):
    blocks = refs[: 2 * count]
    gate_ref, up_ref, hidden_ref, out_ref, normed, dy = refs[2 * count :]
    block = blocks[0].shape[0]
    fsdp, _, columns, tile = out_ref.shape

    @pl.when(pl.program_id(0) == 0)
    def _():
        for i in range(count):
            normed[i * block : (i + 1) * block, :] = blocks[i][...]
            dy[i * block : (i + 1) * block, :] = blocks[count + i][...]

    for kind, (left, right) in enumerate(((normed, gate_ref), (normed, up_ref), (dy, hidden_ref))):
        out_ref[:, kind] = dot_tn(left[...], right[...]).astype(BF16).reshape(fsdp, columns, tile)


def feed_weights(normed, dy, gate_grad, up_grad, hidden, fsdp):
    count = len(normed)
    block, depth = normed[0].shape
    rows, units = hidden.shape
    columns = depth // fsdp
    tile = min(TILE, units)
    return call(
        functools.partial(feed_weights_kernel, count),
        "feed_weights",
        rows * depth * units * 6,
        depth * units * 6,
        grid=(units // tile,),
        out_shape=jax.ShapeDtypeStruct((fsdp, 3, columns, units), BF16),
        in_specs=[once((block, depth))] * (2 * count) + [pl.BlockSpec((rows, tile), lambda i: (0, i))] * 3,
        out_specs=pl.BlockSpec((fsdp, 3, columns, tile), lambda i: (0, 0, 0, i)),
        scratch_shapes=[pltpu.VMEM((rows, depth), BF16)] * 2,
    )(*normed, *dy, gate_grad, up_grad, hidden)


def feed_out_kernel(count, hidden_ref, weight_ref, kept_ref, sent_ref):
    weight = joined(weight_ref)
    block = hidden_ref.shape[0] // count
    for i in range(count):
        values = dot_nt(hidden_ref[i * block : (i + 1) * block, :], weight)
        store_block(kept_ref, sent_ref, i, block, values)


def feed_out(hidden, weights, count):
    rows = hidden.shape[0]
    fsdp, _, columns, units = weights.shape
    depth = fsdp * columns
    return call(
        functools.partial(feed_out_kernel, count),
        "feed_out",
        rows * depth * units * 2,
        rows * depth * 2,
        grid=(1,),
        out_shape=halves(rows, depth),
        in_specs=[once((rows, units)), pl.BlockSpec((fsdp, 1, columns, units), lambda i: (0, 2, 0, 0))],
        out_specs=[once((rows // 2, depth))] * 2,
    )(hidden, weights)


def quarter_places():
    place = 2 * lax.axis_index("chip") + lax.axis_index("core")
    return place, place ^ 2, place ^ 1, place ^ 3


def finish_feed_kernel(own_ref, across_ref, came_ref, gate_ref, up_ref, down_ref):
    units = own_ref.shape[2]
    for place, piece in zip(quarter_places(), (own_ref, across_ref, came_ref.at[0], came_ref.at[1])):
        span = pl.ds(pl.multiple_of(place * units, LANES), units)
        gate_ref[:, span] = piece[0].astype(F32)
        up_ref[:, span] = piece[1].astype(F32)
        down_ref[span, :] = jnp.transpose(piece[2].astype(F32))


def finish_feed(own, across, came):
    _, columns, units = own.shape
    wide = jax.ShapeDtypeStruct((columns, 4 * units), F32)
    return call(
        finish_feed_kernel,
        "finish_feed",
        0,
        own.size * 24,
        out_shape=(wide, wide, jax.ShapeDtypeStruct((4 * units, columns), F32)),
        in_specs=[whole()] * 3,
        out_specs=[whole()] * 3,
    )(own, across, came)


def finish_attention_kernel(real, own_ref, across_ref, came_ref, q_ref, k_ref, v_ref, out_ref, buf):
    part = own_ref.shape[1]
    pieces = (own_ref, across_ref, came_ref.at[0], came_ref.at[1])
    for kind, ref in enumerate((q_ref, k_ref, v_ref, out_ref)):
        for place, piece in zip(quarter_places(), pieces):
            buf[pl.ds(pl.multiple_of(place * part, 16), part), :] = piece[kind].astype(F32)
        ref[...] = buf[:real, :] if kind == 3 else jnp.transpose(buf[...])[:, :real]


def finish_attention(own, across, came, real):
    _, part, columns = own.shape
    into = jax.ShapeDtypeStruct((columns, real), F32)
    return call(
        functools.partial(finish_attention_kernel, real),
        "finish_attention",
        0,
        own.size * 24,
        out_shape=(into, into, into, jax.ShapeDtypeStruct((real, columns), F32)),
        in_specs=[whole()] * 3,
        out_specs=[whole()] * 4,
        scratch_shapes=[pltpu.VMEM((4 * part, columns), F32)],
    )(own, across, came)


def normalize_back(values, inverse, gain, grad_rows):
    scaled = grad_rows * gain
    return inverse * scaled - values * inverse**3 * jnp.mean(scaled * values, axis=-1, keepdims=True)


def inverse_rms(values):
    return lax.rsqrt(jnp.mean(values * values, axis=-1, keepdims=True) + EPSILON)


def pull_fsdp(values, step):
    count = lax.axis_size("fsdp")
    return lax.ppermute(values, "fsdp", [(i, (i - step) % count) for i in range(count)])


def gather_gains(gains):
    count = lax.axis_size("fsdp")
    rolled = jnp.concatenate([gains] + [pull_fsdp(gains, step) for step in range(1, count)], axis=1).astype(F32)
    twice = jnp.concatenate([rolled, rolled], axis=1)
    at = (count - lax.axis_index("fsdp")) % count * gains.shape[1]
    return lax.dynamic_slice_in_dim(twice, at, rolled.shape[1], 1)


def over_tp(gains):
    if lax.axis_size("tp") == 2:
        return gains + swap_tp(gains)
    return lax.psum(gains, "tp")


def over_fsdp(gains):
    blocks = jnp.stack(jnp.split(gains, lax.axis_size("fsdp"), axis=1))
    return jnp.sum(lax.all_to_all(blocks, "fsdp", 0, 0, tiled=True), axis=0)


def scatter_fsdp(values):
    shape = values.shape
    flat = values.reshape((shape[0] * shape[1],) + shape[2:])
    return lax.psum_scatter(flat, "fsdp", scatter_dimension=0, tiled=True)


def shards(tokens, segment_ids, wq, wk, wv, wo, w_gate, w_up, w_down, gain_attn, gain_ffn, cotangent):
    tokens, cotangent, segment_ids = tokens[0], cotangent[0], segment_ids[0]
    fsdp = lax.axis_size("fsdp")
    chip, core = lax.axis_index("chip"), lax.axis_index("core")
    place = 2 * chip + core
    rows = 4 * segment_ids.shape[0]
    real_width = wq.shape[1]
    part = -(-real_width // (4 * HEAD_DIM)) * HEAD_DIM
    heads = part // HEAD_DIM
    width = -(-part // LANES) * LANES
    keys = -(-rows // TILE) * TILE
    both_links = lax.axis_size("tp") == 2

    pad = ((0, 0), (0, 4 * part - real_width))
    own_piece = cut_attention(*[jnp.pad(w, pad) for w in (wq, wk, wv)], jnp.pad(wo, pad[::-1]))
    feed_piece = jnp.stack([take_quarter(w_gate, place, 1), take_quarter(w_up, place, 1), jnp.transpose(take_quarter(w_down, place, 0))])

    def normed(values):
        values = values.astype(F32)
        return (values * inverse_rms(values) * gain_one).astype(BF16)

    if both_links:
        first = lambda values: [values, swap_tp(values), swap_chip(values)]
        second = lambda blocks: widen_core(blocks) + far_block(*blocks)[3:]
        third = lambda blocks: blocks[:3] + blocks[6:] + blocks[3:6] + [swap_core(blocks[6])]
    else:
        first, second, third = lambda values: widen_planes(values)[0], widen_core, lambda blocks: blocks
    ring = [own_piece]
    position = after(jnp.arange(keys, dtype=jnp.int32), own_piece).astype(F32)
    pair_index = (jnp.arange(LANES, dtype=jnp.int32) % (HEAD_DIM // 2)).astype(F32)
    angles = position[:, None] * (10000.0 ** (-pair_index * 2.0 / HEAD_DIM))[None, :]
    block, own, ids_other, cos, sin = together(
        pull_fsdp(ring[0], 1), first(tokens), swap_core(segment_ids), jnp.cos(angles), jnp.sin(angles)
    )
    ring.append(block)
    ids_chip = jnp.concatenate(in_order(segment_ids, ids_other, core == 0))
    block, own, ids_across, gains = together(
        pull_fsdp(ring[-1], 1),
        second(own),
        swap_chip(ids_chip),
        gather_gains(after(jnp.stack([gain_attn, gain_ffn]), ids_other)),
    )
    gain_one, gain_two = gains
    ring.append(block)
    feed_weight = lax.all_gather(after(feed_piece, block), "fsdp", axis=0, tiled=False)
    ids = jnp.concatenate(in_order(ids_chip, ids_across, chip == 0))
    start = jnp.sum((ids[None, :] < ids[:, None]).astype(jnp.int32), axis=1)
    dy = cotangent
    for step in range(2, fsdp - 1):
        if step == 2:
            early = [normed(values) for values in own[:6]]
            block, own, early, dy = together(pull_fsdp(ring[-1], 1), third(own), early, first(after(cotangent, block)))
        else:
            block = pull_fsdp(ring[-1], 1)
        ring.append(block)
    weights = place_weights(ring, width)
    tiles = -(-rows // TILE)
    ends = [-(-min((t + 1) * TILE, rows) // TILE) for t in range(tiles)]
    bounds = jnp.stack([start[::TILE] // TILE, jnp.array(ends, jnp.int32)])
    start = jnp.pad(start, (0, tiles * TILE - rows), constant_values=2 * keys)[None]

    if both_links:
        blocks = early[:3] + [normed(own[3])] + early[3:] + [normed(own[7])]
    else:
        blocks = early
    count = len(blocks)
    inputs = tokens.astype(F32)
    inv_one = inverse_rms(inputs)
    q, k, v = project(blocks, weights, cos, sin, keys)
    dy = second(after(dy, q))
    attended, lse = attend(bounds, q, k, v, start, heads)
    attended, dy = together(attended, dy)
    dy = third(dy)
    leaving = narrow_first(*out_project(attended, weights, count), feed_weight)
    attention_rows, dy = narrow_second(leaving, lambda rows, dy=dy: dy)
    residual = inputs + attention_rows

    inv_two = inverse_rms(residual)
    normed_two = widen((residual * inv_two * gain_two).astype(BF16))
    hidden, gate_grad, up_grad, kept, sent, gain_two_sums = feed(normed_two, dy, feed_weight)
    normed_two_grad, feed_grads = narrow(
        kept, sent, lambda leaving: feed_weights(normed_two, dy, after(gate_grad, leaving), up_grad, hidden, fsdp)
    )
    feed_sums = scatter_fsdp(feed_grads)
    resid_grad = cotangent.astype(F32) + normalize_back(residual, inv_two, gain_two, normed_two_grad)
    resid_low = resid_grad.astype(BF16)

    out_partial = feed_out(after(hidden, resid_low), feed_weight, count)
    planes, (out_kept, out_sent) = widen_planes(resid_low, tuple(out_partial))
    grad_blocks = widen_core(planes)
    out_grad, out_grads = out_back(attended, weights, grad_blocks, fsdp, part)
    leaving = narrow_first(out_kept, out_sent, out_grad)
    dq, dk, dv = attend_back(bounds, q, k, v, attended, after(out_grad, leaving), lse, start, cos, sin, heads)
    layer_rows, (dq, feed_sums) = narrow_second(leaving, lambda rows, dq=dq, sums=feed_sums: (dq, sums))
    layer_out = residual + layer_rows
    feed_across = swap_chip(feed_sums)
    kept, sent, gain_one_sums = project_back(dq, dk, dv, weights, blocks)
    gains = jnp.stack([jnp.sum(gain_one_sums, axis=0) / gain_one, jnp.sum(gain_two_sums, axis=0) / gain_two])
    gains_tp = over_tp(gains)
    project_grads = project_weights(after(dq, sent), dk, dv, out_grads, blocks)
    sums = scatter_fsdp(project_grads)
    (sent, feed_across, gains), _ = together((sent, feed_across, gains_tp), project_grads)
    gains_core = swap_core(gains)
    feed_came = swap_core(jnp.stack([feed_sums, feed_across]))
    leaving, (gains, gains_core, feed_came) = together(narrow_first(kept, sent), (gains, gains_core, feed_came))
    gains = gains + gains_core
    gains_chip = swap_chip(gains)
    normed_grad, gains = narrow_second(leaving, lambda rows: gains + gains_chip)
    gain_own = over_fsdp(gains)
    grad_input = resid_grad + normalize_back(inputs, inv_one, gain_one, normed_grad)

    sums = after(sums, grad_input, gain_own)
    across = swap_chip(sums)
    feed_all = finish_feed(feed_sums, feed_across, after(feed_came, sums))
    across, (gate_all, up_all, down_all) = together(across, tuple(feed_all))
    q_all, k_all, v_all, out_all = finish_attention(sums, across, swap_core(jnp.stack([sums, across])), real_width)
    return (
        layer_out.astype(BF16)[None],
        grad_input[None],
        q_all,
        k_all,
        v_all,
        out_all,
        gate_all,
        up_all,
        down_all,
        gain_own[0],
        gain_own[1],
    )


def solution(mesh):
    devices = mesh.devices.reshape(mesh.shape["fsdp"], mesh.shape["ctx"] // 2, 2, mesh.shape["tp"])
    split = jax.sharding.Mesh(devices, ("fsdp", "chip", "core", "tp"))
    rows = P("fsdp", ("chip", "core", "tp"), None)
    into, outof, gain = P("fsdp", "tp"), P("tp", "fsdp"), P("fsdp")
    return jax.shard_map(
        shards,
        mesh=split,
        in_specs=(rows, P("fsdp", ("chip", "core")), into, into, into, outof, into, into, outof, gain, gain, rows),
        out_specs=(rows, rows, into, into, into, outof, into, into, outof, gain, gain),
        check_vma=False,
    )
```

```python
import functools

import jax
import jax.numpy as jnp
from jax import lax
from jax.experimental import pallas as pl
from jax.experimental.pallas import tpu as pltpu
from jax.sharding import PartitionSpec as P

HEAD_DIM = 64
EPSILON = 1e-05
MASKED = -1e30
BF16 = jnp.bfloat16
F32 = jnp.float32
TILE = 256
LANES = 128
VMEM_BYTES = 60 * 1024 * 1024


def dot(left, right):
    return jnp.dot(left, right, preferred_element_type=F32)


def dot_nt(left, right):
    return lax.dot_general(left, right, (((1,), (1,)), ((), ())), preferred_element_type=F32)


def dot_tn(left, right):
    return lax.dot_general(left, right, (((0,), (0,)), ((), ())), preferred_element_type=F32)


def swap_chip(values):
    return lax.ppermute(values, "chip", [(0, 1), (1, 0)])


def swap_core(values):
    return lax.ppermute(values, "core", [(0, 1), (1, 0)])


def swap_tp(values):
    return lax.ppermute(values, "tp", [(0, 1), (1, 0)])


def in_order(mine, other, mine_first):
    return [jnp.where(mine_first, mine, other), jnp.where(mine_first, other, mine)]


def together(*values):
    return lax.optimization_barrier(values)


def after(values, *earlier):
    return lax.optimization_barrier((values, earlier))[0]


def widen_planes(rows, meanwhile=None):
    if lax.axis_size("tp") != 2:
        gathered = lax.all_gather(rows, "tp", axis=0, tiled=True)
        return [gathered, swap_chip(gathered)], meanwhile
    (beside, across), meanwhile = together((swap_tp(rows), swap_chip(rows)), meanwhile)
    return far_block(rows, beside, across), meanwhile


def meet(beside, across, meanwhile):
    return (beside, across) if meanwhile is None else after((beside, across), meanwhile)


def far_block(rows, beside, across):
    cut = rows.shape[0] // 32 * 16
    far = jnp.concatenate([swap_tp(across[:cut]), swap_chip(beside[cut:])], axis=0)
    return [rows, beside, across, far]


def widen_core(blocks):
    return blocks + [swap_core(block) for block in blocks]


def widen(rows):
    return widen_core(widen_planes(rows)[0])


def block_offset(index, half):
    chip, core = lax.axis_index("chip"), lax.axis_index("core")
    if lax.axis_size("tp") != 2:
        return (chip ^ index % 2) * 2 * half + (core ^ index // 2) * half
    place = lax.axis_index("tp")
    return (chip ^ index // 2 % 2) * 2 * half + (core ^ index // 4) * half + (place ^ index % 2) * (half // 2)


def narrow_first(kept, sent, meanwhile=None):
    came = swap_core(sent)
    if lax.axis_size("tp") != 2:
        rows = kept.shape[0] // 2
        total = kept.astype(F32) + came.astype(F32)
        return ((total[:rows] + swap_chip(total[rows:].astype(BF16)).astype(F32)).astype(BF16),)
    rows = kept.shape[0] // 4
    cut = rows // 32 * 16

    def block(index, first, last):
        where = slice(index * rows + first, index * rows + last)
        return kept[where].astype(F32) + came[where].astype(F32)

    top, bottom = meet(swap_chip(block(3, 0, cut).astype(BF16)), swap_tp(block(3, cut, rows).astype(BF16)), meanwhile)
    beside = jnp.concatenate([block(1, 0, cut) + top.astype(F32), block(1, cut, rows)], axis=0).astype(BF16)
    across = jnp.concatenate([block(2, 0, cut), block(2, cut, rows) + bottom.astype(F32)], axis=0).astype(BF16)
    return beside, across, block(0, 0, rows)


def narrow_second(leaving, meanwhile=None):
    done = None
    if len(leaving) == 1:
        if meanwhile is not None:
            done = meanwhile(leaving)
        return lax.psum_scatter(leaving[0], "tp", scatter_dimension=0, tiled=True).astype(F32), done
    from_tp, from_chip = swap_tp(leaving[0]), swap_chip(leaving[1])
    if meanwhile is not None:
        (from_tp, from_chip), done = together((from_tp, from_chip), meanwhile(leaving[:2]))
    return leaving[2] + from_tp.astype(F32) + from_chip.astype(F32), done


def narrow(kept, sent, meanwhile=None):
    return narrow_second(narrow_first(kept, sent), meanwhile)


def take_quarter(values, index, axis):
    size = values.shape[axis] // 4
    return lax.dynamic_slice_in_dim(values, index * size, size, axis)


def call(kernel, name, flops, moved, **rest):
    return pl.pallas_call(
        kernel,
        name=name,
        cost_estimate=pl.CostEstimate(flops=flops, bytes_accessed=moved, transcendentals=0),
        compiler_params=pltpu.CompilerParams(vmem_limit_bytes=VMEM_BYTES),
        **rest,
    )


def whole():
    return pl.BlockSpec(memory_space=pltpu.VMEM)


def turn(values, cos, sin, direction):
    lane = lax.broadcasted_iota(jnp.int32, (1, LANES), 1)
    partner = jnp.where((lane // 32) % 2 == 0, pltpu.roll(values, 96, 1) * -direction, pltpu.roll(values, 32, 1) * direction)
    return values * cos + partner * sin


def block_spans(count, rows):
    block = rows // count
    return [pl.ds(pl.multiple_of(block_offset(i, rows // 4), 16), block) for i in range(count)]


def project_kernel(count, rows, *refs):
    blocks = refs[:count]
    weight_ref, cos_ref, sin_ref, q_ref, k_ref, v_ref = refs[count:]
    width = q_ref.shape[1]
    for ref in (k_ref, v_ref):
        ref[rows:, :] = jnp.zeros((ref.shape[0] - rows, width), BF16)
    for block, span in zip(blocks, block_spans(count, rows)):
        cos, sin = cos_ref[span, :], sin_ref[span, :]
        for kind, out_ref in ((0, q_ref), (1, k_ref)):
            values = dot_nt(block[...], weight_ref[kind])
            for c in range(0, width, LANES):
                out_ref[span, c : c + LANES] = turn(values[:, c : c + LANES], cos, sin, 1.0).astype(BF16)
        v_ref[span, :] = dot_nt(block[...], weight_ref[2]).astype(BF16)


def project(blocks, weights, cos, sin, keys):
    count = len(blocks)
    block, depth = blocks[0].shape
    rows = count * block
    width = weights.shape[1]
    tall = jax.ShapeDtypeStruct((keys, width), BF16)
    return call(
        functools.partial(project_kernel, count, rows),
        "project",
        rows * depth * width * 6,
        rows * depth * 2,
        out_shape=(jax.ShapeDtypeStruct((rows, width), BF16), tall, tall),
        in_specs=[whole()] * (count + 3),
        out_specs=[whole()] * 3,
    )(*blocks, weights, cos, sin)


def cut_kernel(q_ref, k_ref, v_ref, out_ref, piece_ref, buf):
    part = piece_ref.shape[1]
    span = pl.ds(pl.multiple_of(quarter_places()[0] * part, 16), part)
    for kind, ref in enumerate((q_ref, k_ref, v_ref)):
        buf[...] = jnp.transpose(ref[...])
        piece_ref[kind] = buf[span, :]
    piece_ref[3] = out_ref[span, :]


def cut_attention(wq, wk, wv, wo):
    width, columns = wo.shape
    return call(
        cut_kernel,
        "cut_attention",
        0,
        width * columns * 8,
        out_shape=jax.ShapeDtypeStruct((4, width // 4, columns), BF16),
        in_specs=[whole()] * 4,
        out_specs=whole(),
        scratch_shapes=[pltpu.VMEM((width, columns), BF16)],
    )(wq, wk, wv, wo)


def place_kernel(*refs):
    blocks, out_ref = refs[:-1], refs[-1]
    kinds, part, columns = blocks[0].shape
    me = lax.axis_index("fsdp")
    if part < out_ref.shape[1]:
        out_ref[:, part:, :] = jnp.zeros((kinds, out_ref.shape[1] - part, out_ref.shape[2]), BF16)
    for i, block in enumerate(blocks):
        at = pl.multiple_of((me + i) % len(blocks) * columns, LANES)
        out_ref[:, :part, pl.ds(at, columns)] = block[...]


def place_weights(blocks, width):
    kinds, _, columns = blocks[0].shape
    depth = len(blocks) * columns
    return call(
        place_kernel,
        "place_weights",
        0,
        kinds * width * depth * 4,
        out_shape=jax.ShapeDtypeStruct((kinds, width, depth), BF16),
        in_specs=[whole()] * len(blocks),
        out_specs=whole(),
    )(*blocks)


def store_block(kept_ref, sent_ref, i, block, values):
    half = kept_ref.shape[0]
    at = i * block
    if at < half:
        kept_ref[at : at + block, :] = values.astype(BF16)
    else:
        sent_ref[at - half : at - half + block, :] = values.astype(BF16)


def halves(rows, depth):
    return [jax.ShapeDtypeStruct((rows // 2, depth), BF16)] * 2


def out_kernel(count, o_ref, weight_ref, kept_ref, sent_ref):
    rows = o_ref.shape[0]
    for i, span in enumerate(block_spans(count, rows)):
        store_block(kept_ref, sent_ref, i, rows // count, dot(o_ref[span, :], weight_ref[3]))


def out_project(attended, weights, count):
    rows, width = attended.shape
    depth = weights.shape[2]
    return call(
        functools.partial(out_kernel, count),
        "out_project",
        rows * width * depth * 2,
        rows * depth * 2,
        out_shape=halves(rows, depth),
        in_specs=[whole(), whole()],
        out_specs=[whole(), whole()],
    )(attended, weights)


def out_back_kernel(count, o_ref, weight_ref, *refs):
    blocks, (grad_ref, out_ref, all_rows) = refs[:count], refs[count:]
    rows = o_ref.shape[0]
    for block, span in zip(blocks, block_spans(count, rows)):
        grad = block[...]
        grad_ref[span, :] = dot_nt(grad, weight_ref[3]).astype(BF16)
        all_rows[span, :] = grad
    total = dot_tn(o_ref[...], all_rows[...])
    fsdp, _, part, columns = out_ref.shape
    for z in range(fsdp):
        out_ref[z, 0] = total[:part, z * columns : (z + 1) * columns].astype(BF16)


def out_back(attended, weights, blocks, fsdp, part):
    rows, width = attended.shape
    depth = weights.shape[2]
    return call(
        functools.partial(out_back_kernel, len(blocks)),
        "out_back",
        rows * width * depth * 4,
        rows * depth * 2,
        out_shape=(
            jax.ShapeDtypeStruct((rows, width), BF16),
            jax.ShapeDtypeStruct((fsdp, 1, part, depth // fsdp), BF16),
        ),
        in_specs=[whole()] * (2 + len(blocks)),
        out_specs=[whole()] * 2,
        scratch_shapes=[pltpu.VMEM((rows, depth), BF16)],
    )(attended, weights, *blocks)


def project_weights_kernel(count, dq_ref, dk_ref, dv_ref, done_ref, *refs):
    blocks, (out_ref, all_rows) = refs[:count], refs[count:]
    rows = all_rows.shape[0]
    for block, span in zip(blocks, block_spans(count, rows)):
        all_rows[span, :] = block[...]
    part = out_ref.shape[2]
    for kind, grad in enumerate((dq_ref, dk_ref, dv_ref)):
        out_ref[0, kind] = dot_tn(grad[:rows, :], all_rows[...])[:part].astype(BF16)
    out_ref[0, 3] = done_ref[0, 0]


def project_weights(dq, dk, dv, out_grads, blocks):
    rows, width = dq.shape
    fsdp, _, part, _ = out_grads.shape
    block, depth = blocks[0].shape
    columns = depth // fsdp
    fixed = lambda array: pl.BlockSpec(array.shape, lambda z: (0, 0))
    return call(
        functools.partial(project_weights_kernel, len(blocks)),
        "project_weights",
        rows * width * depth * 6,
        rows * depth * 2,
        grid=(fsdp,),
        out_shape=jax.ShapeDtypeStruct((fsdp, 4, part, columns), BF16),
        in_specs=[fixed(dq), fixed(dk), fixed(dv), pl.BlockSpec((1, 1, part, columns), lambda z: (z, 0, 0, 0))]
        + [pl.BlockSpec((block, columns), lambda z: (0, z))] * len(blocks),
        out_specs=pl.BlockSpec((1, 4, part, columns), lambda z: (z, 0, 0, 0)),
        scratch_shapes=[pltpu.VMEM((rows, columns), BF16)],
    )(dq, dk, dv, out_grads, *blocks)


def column_sums(grads, normed):
    product = grads * normed.astype(F32)
    return jnp.sum(product.reshape(product.shape[0] // 8, 8, product.shape[1]), axis=0)


def project_back_kernel(count, dq_ref, dk_ref, dv_ref, weight_ref, *refs):
    blocks, (kept_ref, sent_ref, gain_ref) = refs[:count], refs[count:]
    rows = dq_ref.shape[0]
    sums = 0.0
    for i, (block, span) in enumerate(zip(blocks, block_spans(count, rows))):
        total = dot(dq_ref[span, :], weight_ref[0]) + dot(dk_ref[span, :], weight_ref[1]) + dot(dv_ref[span, :], weight_ref[2])
        sums = sums + column_sums(total, block[...])
        store_block(kept_ref, sent_ref, i, rows // count, total)
    gain_ref[...] = sums


def project_back(dq, dk, dv, weights, blocks):
    rows, width = dq.shape
    depth = weights.shape[2]
    return call(
        functools.partial(project_back_kernel, len(blocks)),
        "project_back",
        rows * width * depth * 6,
        rows * depth * 4,
        out_shape=halves(rows, depth) + [jax.ShapeDtypeStruct((8, depth), F32)],
        in_specs=[whole()] * (4 + len(blocks)),
        out_specs=[whole()] * 3,
    )(dq, dk, dv, weights, *blocks)


def lane_half(head):
    return (lax.broadcasted_iota(jnp.int32, (1, LANES), 1) // HEAD_DIM) == head % 2


def forward_kernel(rows, bounds, q_ref, k_ref, v_ref, start_ref, o_ref, lse_ref, q_buf, s_buf, top_buf, sum_buf, acc_buf):
    heads = q_buf.shape[0]
    zero = jnp.zeros((), BF16)
    for t in range(-(-rows // TILE)):
        low, high = bounds[0, t], bounds[1, t]
        n = min(TILE, rows - t * TILE)
        span = slice(t * TILE, (t + 1) * TILE)
        start = start_ref[:, span]
        row = t * TILE + lax.broadcasted_iota(jnp.int32, (1, TILE), 1)
        for h in range(heads):
            c = (h // 2) * LANES
            scaled = (q_ref[t * TILE : t * TILE + n, c : c + LANES].astype(F32) * HEAD_DIM**-0.5).astype(BF16)
            q_buf[h, :n, :] = jnp.where(lane_half(h), scaled, zero)
            if n < TILE:
                q_buf[h, n:, :] = jnp.zeros((TILE - n, LANES), BF16)
        top_buf[...] = jnp.full_like(top_buf, MASKED)
        sum_buf[...] = jnp.zeros_like(sum_buf)
        acc_buf[...] = jnp.zeros_like(acc_buf)

        @pl.loop(low, high)
        def _(i):
            at = pl.multiple_of(i * TILE, TILE)
            place = at + lax.broadcasted_iota(jnp.int32, (TILE, TILE), 0)
            allowed = (place >= start) & (place <= row)
            for h in range(heads):
                c = (h // 2) * LANES
                s = jnp.where(allowed, dot_nt(k_ref[pl.ds(at, TILE), c : c + LANES], q_buf[h]), MASKED)
                s_buf[h, pl.ds(at, TILE), :] = s
                top_buf[h] = jnp.maximum(top_buf[h], jnp.max(s.reshape(TILE // 8, 8, TILE), axis=0))

        tops = [jnp.max(top_buf[h], axis=0, keepdims=True) for h in range(heads)]

        @pl.loop(low, high)
        def _(i):
            at = pl.multiple_of(i * TILE, TILE)
            for h in range(heads):
                c = (h // 2) * LANES
                p = jnp.exp(s_buf[h, pl.ds(at, TILE), :] - tops[h])
                sum_buf[h] += jnp.sum(p.reshape(TILE // 8, 8, TILE), axis=0)
                both = dot_tn(v_ref[pl.ds(at, TILE), c : c + LANES], p.astype(BF16))
                acc_buf[h] += both[HEAD_DIM * (h % 2) : HEAD_DIM * (h % 2) + HEAD_DIM]

        for h in range(heads):
            total = jnp.sum(sum_buf[h], axis=0, keepdims=True)
            lse_ref[h : h + 1, span] = tops[h] + jnp.log(total)
            acc_buf[h] = acc_buf[h] / total
        for pair in range(o_ref.shape[1] // LANES):
            second = acc_buf[2 * pair + 1] if 2 * pair + 1 < heads else jnp.zeros((HEAD_DIM, TILE), F32)
            o = jnp.transpose(jnp.concatenate([acc_buf[2 * pair], second], axis=0))
            o_ref[t * TILE : t * TILE + n, pair * LANES : (pair + 1) * LANES] = o[:n].astype(BF16)


def attend(bounds, q, k, v, start, heads):
    rows = q.shape[0]
    keys, width = k.shape
    padded = -(-rows // TILE) * TILE
    return call(
        functools.partial(forward_kernel, rows),
        "attend",
        rows * rows * heads * HEAD_DIM * 2,
        keys * width * 8,
        out_shape=(jax.ShapeDtypeStruct((rows, width), BF16), jax.ShapeDtypeStruct((heads, padded), F32)),
        in_specs=[pl.BlockSpec(memory_space=pltpu.SMEM)] + [whole()] * 4,
        out_specs=[whole(), whole()],
        scratch_shapes=[
            pltpu.VMEM((heads, TILE, LANES), BF16),
            pltpu.VMEM((heads, keys, TILE), F32),
            pltpu.VMEM((heads, 8, TILE), F32),
            pltpu.VMEM((heads, 8, TILE), F32),
            pltpu.VMEM((heads, HEAD_DIM, TILE), F32),
        ],
    )(bounds, q, k, v, start)


def backward_kernel(
    rows, bounds, q_ref, k_ref, v_ref, o_ref, g_ref, lse_ref, start_ref, cos_ref, sin_ref,
    dq_ref, dk_ref, dv_ref, q_buf, g_buf, d_buf, dq_acc, dk_acc, dv_acc,
):
    heads = q_buf.shape[0]
    zero = jnp.zeros((), BF16)
    scale = HEAD_DIM**-0.5
    dk_acc[...] = jnp.zeros_like(dk_acc)
    dv_acc[...] = jnp.zeros_like(dv_acc)
    for t in range(-(-rows // TILE)):
        low, high = bounds[0, t], bounds[1, t]
        n = min(TILE, rows - t * TILE)
        span = slice(t * TILE, (t + 1) * TILE)
        here = slice(t * TILE, t * TILE + n)
        start = start_ref[:, span]
        row = t * TILE + lax.broadcasted_iota(jnp.int32, (1, TILE), 1)
        for pair in range(-(-heads // 2)):
            c = pair * LANES
            scaled = (q_ref[here, c : c + LANES].astype(F32) * scale).astype(BF16)
            grad = g_ref[here, c : c + LANES]
            product = grad.astype(F32) * o_ref[here, c : c + LANES].astype(F32)
            if n < TILE:
                product = jnp.concatenate([product, jnp.zeros((TILE - n, LANES), F32)], axis=0)
            product = jnp.transpose(product)
            for h in range(2 * pair, min(heads, 2 * pair + 2)):
                q_buf[h, :n, :] = jnp.where(lane_half(h), scaled, zero)
                g_buf[h, :n, :] = jnp.where(lane_half(h), grad, zero)
                if n < TILE:
                    q_buf[h, n:, :] = jnp.zeros((TILE - n, LANES), BF16)
                    g_buf[h, n:, :] = jnp.zeros((TILE - n, LANES), BF16)
                d_buf[h : h + 1, :] = jnp.sum(product[HEAD_DIM * (h % 2) : HEAD_DIM * (h % 2) + HEAD_DIM], axis=0, keepdims=True)
        dq_acc[...] = jnp.zeros_like(dq_acc)

        @pl.loop(low, high)
        def _(i):
            at = pl.multiple_of(i * TILE, TILE)
            place = at + lax.broadcasted_iota(jnp.int32, (TILE, TILE), 0)
            allowed = (place >= start) & (place <= row)
            for pair in range(-(-heads // 2)):
                c = pair * LANES
                k = k_ref[pl.ds(at, TILE), c : c + LANES]
                v = v_ref[pl.ds(at, TILE), c : c + LANES]
                dq = dk = dv = 0.0
                for h in range(2 * pair, min(heads, 2 * pair + 2)):
                    p = jnp.where(allowed, jnp.exp(dot_nt(k, q_buf[h]) - lse_ref[h : h + 1, span]), 0.0)
                    ds = (p * (dot_nt(v, g_buf[h]) - d_buf[h : h + 1, :])).astype(BF16)
                    dv = dv + dot(p.astype(BF16), g_buf[h])
                    dk = dk + dot(ds, q_buf[h])
                    dq = dq + dot_tn(ds, jnp.where(lane_half(h), k, zero))
                dk_acc[pl.ds(at, TILE), c : c + LANES] += dk
                dv_acc[pl.ds(at, TILE), c : c + LANES] += dv
                dq_acc[:, c : c + LANES] += dq

        for c in range(0, dk_ref.shape[1], LANES):
            dq = dq_acc[:n, c : c + LANES] * scale
            dq_ref[here, c : c + LANES] = turn(dq, cos_ref[here, :], sin_ref[here, :], -1.0).astype(BF16)
    for c in range(0, dk_ref.shape[1], LANES):
        dk_ref[:, c : c + LANES] = turn(dk_acc[:, c : c + LANES], cos_ref[...], sin_ref[...], -1.0).astype(BF16)
    dv_ref[...] = dv_acc[...].astype(BF16)


def attend_back(bounds, q, k, v, o, grad, lse, start, cos, sin, heads):
    rows = q.shape[0]
    keys, width = k.shape
    tall = jax.ShapeDtypeStruct((keys, width), BF16)
    return call(
        functools.partial(backward_kernel, rows),
        "attend_back",
        rows * rows * heads * HEAD_DIM * 5,
        keys * width * 16,
        out_shape=(jax.ShapeDtypeStruct((rows, width), BF16), tall, tall),
        in_specs=[pl.BlockSpec(memory_space=pltpu.SMEM)] + [whole()] * 9,
        out_specs=[whole()] * 3,
        scratch_shapes=[
            pltpu.VMEM((heads, TILE, LANES), BF16),
            pltpu.VMEM((heads, TILE, LANES), BF16),
            pltpu.VMEM((heads, TILE), F32),
            pltpu.VMEM((TILE, width), F32),
            pltpu.VMEM((keys, width), F32),
            pltpu.VMEM((keys, width), F32),
        ],
    )(bounds, q, k, v, o, grad, lse, start, cos, sin)


def joined(ref):
    shape = ref.shape
    return ref[...].reshape(shape[0] * shape[2], shape[3])


def once(shape):
    return pl.BlockSpec(shape, lambda i: (0,) * len(shape), pipeline_mode=pl.Buffered(1))


def feed_kernel(count, *refs):
    sources, weight_ref = refs[: 2 * count], refs[2 * count]
    hidden_ref, gate_ref, up_ref, kept_ref, sent_ref, gain_ref, rows_buf, weight_buf, sems = refs[2 * count + 1 :]
    block = sources[0].shape[0]
    fsdp, _, columns, units = weight_ref.shape

    def weight_copy(k):
        return pltpu.make_async_copy(weight_ref.at[:, k], weight_buf.at[k], sems.at[2 * count + k])

    def row_copy(i):
        return pltpu.make_async_copy(sources[i], rows_buf.at[i], sems.at[i])

    order = [i for pair in zip(range(count), range(count, 2 * count)) for i in pair]
    row_copy(0).start()
    for k in range(3):
        weight_copy(k).start()
    for i in order[1:]:
        row_copy(i).start()
    row_copy(0).wait()
    total = 0.0
    for i in range(count):
        rows = slice(i * block, (i + 1) * block)
        if i > 0:
            row_copy(i).wait()
        normed = rows_buf[i]

        def weight(k):
            if i == 0:
                weight_copy(k).wait()
            return weight_buf[k].reshape(fsdp * columns, units)

        gate_w = weight(0)
        gate = dot(normed, gate_w)
        up_w = weight(1)
        up = dot(normed, up_w)
        down_w = weight(2)
        row_copy(count + i).wait()
        grad = dot(rows_buf[count + i], down_w)
        sig = 1.0 / (1.0 + jnp.exp(-gate))
        silu = gate * sig
        hidden_ref[rows, :] = (silu * up).astype(BF16)
        gate_grad = (grad * up * sig * (1.0 + gate * (1.0 - sig))).astype(BF16)
        up_grad = (grad * silu).astype(BF16)
        gate_ref[rows, :] = gate_grad
        up_ref[rows, :] = up_grad
        values = dot_nt(gate_grad, gate_w) + dot_nt(up_grad, up_w)
        store_block(kept_ref, sent_ref, i, block, values)
        total = total + column_sums(values, normed)
    gain_ref[...] = total


def feed(normed, dy, weights):
    count = len(normed)
    block, depth = normed[0].shape
    rows = count * block
    fsdp, kinds, columns, units = weights.shape
    wide = jax.ShapeDtypeStruct((rows, units), BF16)
    return call(
        functools.partial(feed_kernel, count),
        "feed",
        rows * depth * units * 10,
        depth * units * 6,
        out_shape=[wide, wide, wide] + halves(rows, depth) + [jax.ShapeDtypeStruct((8, depth), F32)],
        in_specs=[pl.BlockSpec(memory_space=pl.ANY)] * (2 * count + 1),
        out_specs=[whole()] * 6,
        scratch_shapes=[
            pltpu.VMEM((2 * count, block, depth), BF16),
            pltpu.VMEM((kinds, fsdp, columns, units), BF16),
            pltpu.SemaphoreType.DMA((2 * count + kinds,)),
        ],
    )(*normed, *dy, weights)


def feed_weights_kernel(count, *refs):
    blocks = refs[: 2 * count]
    gate_ref, up_ref, hidden_ref, out_ref, normed, dy = refs[2 * count :]
    block = blocks[0].shape[0]
    fsdp, _, columns, tile = out_ref.shape

    @pl.when(pl.program_id(0) == 0)
    def _():
        for i in range(count):
            normed[i * block : (i + 1) * block, :] = blocks[i][...]
            dy[i * block : (i + 1) * block, :] = blocks[count + i][...]

    for kind, (left, right) in enumerate(((normed, gate_ref), (normed, up_ref), (dy, hidden_ref))):
        out_ref[:, kind] = dot_tn(left[...], right[...]).astype(BF16).reshape(fsdp, columns, tile)


def feed_weights(normed, dy, gate_grad, up_grad, hidden, fsdp):
    count = len(normed)
    block, depth = normed[0].shape
    rows, units = hidden.shape
    columns = depth // fsdp
    tile = min(TILE, units)
    return call(
        functools.partial(feed_weights_kernel, count),
        "feed_weights",
        rows * depth * units * 6,
        depth * units * 6,
        grid=(units // tile,),
        out_shape=jax.ShapeDtypeStruct((fsdp, 3, columns, units), BF16),
        in_specs=[once((block, depth))] * (2 * count) + [pl.BlockSpec((rows, tile), lambda i: (0, i))] * 3,
        out_specs=pl.BlockSpec((fsdp, 3, columns, tile), lambda i: (0, 0, 0, i)),
        scratch_shapes=[pltpu.VMEM((rows, depth), BF16)] * 2,
    )(*normed, *dy, gate_grad, up_grad, hidden)


def feed_out_kernel(count, hidden_ref, weight_ref, kept_ref, sent_ref):
    weight = joined(weight_ref)
    block = hidden_ref.shape[0] // count
    for i in range(count):
        values = dot_nt(hidden_ref[i * block : (i + 1) * block, :], weight)
        store_block(kept_ref, sent_ref, i, block, values)


def feed_out(hidden, weights, count):
    rows = hidden.shape[0]
    fsdp, _, columns, units = weights.shape
    depth = fsdp * columns
    return call(
        functools.partial(feed_out_kernel, count),
        "feed_out",
        rows * depth * units * 2,
        rows * depth * 2,
        grid=(1,),
        out_shape=halves(rows, depth),
        in_specs=[once((rows, units)), pl.BlockSpec((fsdp, 1, columns, units), lambda i: (0, 2, 0, 0))],
        out_specs=[once((rows // 2, depth))] * 2,
    )(hidden, weights)


def quarter_places():
    place = 2 * lax.axis_index("chip") + lax.axis_index("core")
    return place, place ^ 2, place ^ 1, place ^ 3


def finish_feed_kernel(own_ref, across_ref, came_ref, gate_ref, up_ref, down_ref):
    units = own_ref.shape[2]
    for place, piece in zip(quarter_places(), (own_ref, across_ref, came_ref.at[0], came_ref.at[1])):
        span = pl.ds(pl.multiple_of(place * units, LANES), units)
        gate_ref[:, span] = piece[0].astype(F32)
        up_ref[:, span] = piece[1].astype(F32)
        down_ref[span, :] = jnp.transpose(piece[2].astype(F32))


def finish_feed(own, across, came):
    _, columns, units = own.shape
    wide = jax.ShapeDtypeStruct((columns, 4 * units), F32)
    return call(
        finish_feed_kernel,
        "finish_feed",
        0,
        own.size * 24,
        out_shape=(wide, wide, jax.ShapeDtypeStruct((4 * units, columns), F32)),
        in_specs=[whole()] * 3,
        out_specs=[whole()] * 3,
    )(own, across, came)


def finish_attention_kernel(real, own_ref, across_ref, came_ref, q_ref, k_ref, v_ref, out_ref, buf):
    part = own_ref.shape[1]
    pieces = (own_ref, across_ref, came_ref.at[0], came_ref.at[1])
    for kind, ref in enumerate((q_ref, k_ref, v_ref, out_ref)):
        for place, piece in zip(quarter_places(), pieces):
            buf[pl.ds(pl.multiple_of(place * part, 16), part), :] = piece[kind].astype(F32)
        ref[...] = buf[:real, :] if kind == 3 else jnp.transpose(buf[...])[:, :real]


def finish_attention(own, across, came, real):
    _, part, columns = own.shape
    into = jax.ShapeDtypeStruct((columns, real), F32)
    return call(
        functools.partial(finish_attention_kernel, real),
        "finish_attention",
        0,
        own.size * 24,
        out_shape=(into, into, into, jax.ShapeDtypeStruct((real, columns), F32)),
        in_specs=[whole()] * 3,
        out_specs=[whole()] * 4,
        scratch_shapes=[pltpu.VMEM((4 * part, columns), F32)],
    )(own, across, came)


def normalize_back(values, inverse, gain, grad_rows):
    scaled = grad_rows * gain
    return inverse * scaled - values * inverse**3 * jnp.mean(scaled * values, axis=-1, keepdims=True)


def inverse_rms(values):
    return lax.rsqrt(jnp.mean(values * values, axis=-1, keepdims=True) + EPSILON)


def pull_fsdp(values, step):
    count = lax.axis_size("fsdp")
    return lax.ppermute(values, "fsdp", [(i, (i - step) % count) for i in range(count)])


def gather_gains(gains):
    count = lax.axis_size("fsdp")
    rolled = jnp.concatenate([gains] + [pull_fsdp(gains, step) for step in range(1, count)], axis=1).astype(F32)
    twice = jnp.concatenate([rolled, rolled], axis=1)
    at = (count - lax.axis_index("fsdp")) % count * gains.shape[1]
    return lax.dynamic_slice_in_dim(twice, at, rolled.shape[1], 1)


def over_tp(gains):
    if lax.axis_size("tp") == 2:
        return gains + swap_tp(gains)
    return lax.psum(gains, "tp")


def over_fsdp(gains):
    blocks = jnp.stack(jnp.split(gains, lax.axis_size("fsdp"), axis=1))
    return jnp.sum(lax.all_to_all(blocks, "fsdp", 0, 0, tiled=True), axis=0)


def scatter_fsdp(values):
    shape = values.shape
    flat = values.reshape((shape[0] * shape[1],) + shape[2:])
    return lax.psum_scatter(flat, "fsdp", scatter_dimension=0, tiled=True)


def shards(tokens, segment_ids, wq, wk, wv, wo, w_gate, w_up, w_down, gain_attn, gain_ffn, cotangent):
    tokens, cotangent, segment_ids = tokens[0], cotangent[0], segment_ids[0]
    fsdp = lax.axis_size("fsdp")
    chip, core = lax.axis_index("chip"), lax.axis_index("core")
    place = 2 * chip + core
    rows = 4 * segment_ids.shape[0]
    real_width = wq.shape[1]
    part = -(-real_width // (4 * HEAD_DIM)) * HEAD_DIM
    heads = part // HEAD_DIM
    width = -(-part // LANES) * LANES
    keys = -(-rows // TILE) * TILE
    both_links = lax.axis_size("tp") == 2

    pad = ((0, 0), (0, 4 * part - real_width))
    own_piece = cut_attention(*[jnp.pad(w, pad) for w in (wq, wk, wv)], jnp.pad(wo, pad[::-1]))
    feed_piece = jnp.stack([take_quarter(w_gate, place, 1), take_quarter(w_up, place, 1), jnp.transpose(take_quarter(w_down, place, 0))])

    def normed(values):
        values = values.astype(F32)
        return (values * inverse_rms(values) * gain_one).astype(BF16)

    if both_links:
        first = lambda values: [values, swap_tp(values), swap_chip(values)]
        second = lambda blocks, *earlier: widen_core(after(blocks, *earlier)) + far_block(*blocks)[3:]
        third = lambda blocks: blocks[:3] + blocks[6:] + blocks[3:6] + [swap_core(blocks[6])]
    else:
        first, third = lambda values: widen_planes(values)[0], lambda blocks: blocks
        second = lambda blocks, *earlier: widen_core(after(blocks, *earlier))
    ring = [own_piece]
    position = after(jnp.arange(keys, dtype=jnp.int32), own_piece).astype(F32)
    pair_index = (jnp.arange(LANES, dtype=jnp.int32) % (HEAD_DIM // 2)).astype(F32)
    angles = position[:, None] * (10000.0 ** (-pair_index * 2.0 / HEAD_DIM))[None, :]
    block, own, ids_other, cos, sin = together(
        pull_fsdp(ring[0], 1), first(tokens), swap_core(segment_ids), jnp.cos(angles), jnp.sin(angles)
    )
    ring.append(block)
    ids_chip = jnp.concatenate(in_order(segment_ids, ids_other, core == 0))
    hop = pull_fsdp(ring[-1], 1)
    block, own, ids_across, gains = together(
        hop,
        second(own, hop),
        swap_chip(ids_chip),
        gather_gains(after(jnp.stack([gain_attn, gain_ffn]), ids_other)),
    )
    gain_one, gain_two = gains
    ring.append(block)
    feed_weight = lax.all_gather(after(feed_piece, block), "fsdp", axis=0, tiled=False)
    ids = jnp.concatenate(in_order(ids_chip, ids_across, chip == 0))
    start = jnp.sum((ids[None, :] < ids[:, None]).astype(jnp.int32), axis=1)
    dy = cotangent
    for step in range(2, fsdp - 1):
        if step == 2:
            early = [normed(values) for values in own[:6]]
            block, own, early, dy = together(pull_fsdp(ring[-1], 1), third(own), early, first(after(cotangent, block)))
        else:
            block = pull_fsdp(ring[-1], 1)
        ring.append(block)
    weights = place_weights(ring, width)
    tiles = -(-rows // TILE)
    ends = [-(-min((t + 1) * TILE, rows) // TILE) for t in range(tiles)]
    bounds = jnp.stack([start[::TILE] // TILE, jnp.array(ends, jnp.int32)])
    start = jnp.pad(start, (0, tiles * TILE - rows), constant_values=2 * keys)[None]

    if both_links:
        blocks = early[:3] + [normed(own[3])] + early[3:] + [normed(own[7])]
    else:
        blocks = early
    count = len(blocks)
    inputs = tokens.astype(F32)
    inv_one = inverse_rms(inputs)
    q, k, v = project(blocks, weights, cos, sin, keys)
    dy = second(after(dy, q))
    attended, lse = attend(bounds, q, k, v, start, heads)
    attended, dy = together(attended, dy)
    dy = third(dy)
    leaving = narrow_first(*out_project(attended, weights, count), feed_weight)
    attention_rows, dy = narrow_second(leaving, lambda rows, dy=dy: dy)
    residual = inputs + attention_rows

    inv_two = inverse_rms(residual)
    normed_two = widen((residual * inv_two * gain_two).astype(BF16))
    hidden, gate_grad, up_grad, kept, sent, gain_two_sums = feed(normed_two, dy, feed_weight)
    normed_two_grad, feed_grads = narrow(
        kept, sent, lambda leaving: feed_weights(normed_two, dy, after(gate_grad, leaving), up_grad, hidden, fsdp)
    )
    feed_sums = scatter_fsdp(feed_grads)
    resid_grad = cotangent.astype(F32) + normalize_back(residual, inv_two, gain_two, normed_two_grad)
    resid_low = resid_grad.astype(BF16)

    out_partial = feed_out(after(hidden, resid_low), feed_weight, count)
    planes, (out_kept, out_sent) = widen_planes(resid_low, tuple(out_partial))
    grad_blocks = widen_core(planes)
    out_grad, out_grads = out_back(attended, weights, grad_blocks, fsdp, part)
    leaving = narrow_first(out_kept, out_sent, out_grad)
    dq, dk, dv = attend_back(bounds, q, k, v, attended, after(out_grad, leaving), lse, start, cos, sin, heads)
    layer_rows, (dq, feed_sums) = narrow_second(leaving, lambda rows, dq=dq, sums=feed_sums: (dq, sums))
    layer_out = residual + layer_rows
    feed_across = swap_chip(feed_sums)
    kept, sent, gain_one_sums = project_back(dq, dk, dv, weights, blocks)
    gains = jnp.stack([jnp.sum(gain_one_sums, axis=0) / gain_one, jnp.sum(gain_two_sums, axis=0) / gain_two])
    gains_tp = over_tp(gains)
    project_grads = project_weights(after(dq, sent), dk, dv, out_grads, blocks)
    sums = scatter_fsdp(project_grads)
    (sent, feed_across, gains), _ = together((sent, feed_across, gains_tp), project_grads)
    gains_core = swap_core(gains)
    feed_came = swap_core(jnp.stack([feed_sums, feed_across]))
    leaving, (gains, gains_core, feed_came) = together(narrow_first(kept, sent), (gains, gains_core, feed_came))
    gains = gains + gains_core
    gains_chip = swap_chip(gains)
    normed_grad, gains = narrow_second(leaving, lambda rows: gains + gains_chip)
    gain_own = over_fsdp(gains)
    grad_input = resid_grad + normalize_back(inputs, inv_one, gain_one, normed_grad)

    sums = after(sums, grad_input, gain_own)
    across = swap_chip(sums)
    feed_all = finish_feed(feed_sums, feed_across, after(feed_came, sums))
    across, (gate_all, up_all, down_all) = together(across, tuple(feed_all))
    q_all, k_all, v_all, out_all = finish_attention(sums, across, swap_core(jnp.stack([sums, across])), real_width)
    return (
        layer_out.astype(BF16)[None],
        grad_input[None],
        q_all,
        k_all,
        v_all,
        out_all,
        gate_all,
        up_all,
        down_all,
        gain_own[0],
        gain_own[1],
    )


def solution(mesh):
    devices = mesh.devices.reshape(mesh.shape["fsdp"], mesh.shape["ctx"] // 2, 2, mesh.shape["tp"])
    split = jax.sharding.Mesh(devices, ("fsdp", "chip", "core", "tp"))
    rows = P("fsdp", ("chip", "core", "tp"), None)
    into, outof, gain = P("fsdp", "tp"), P("tp", "fsdp"), P("fsdp")
    return jax.shard_map(
        shards,
        mesh=split,
        in_specs=(rows, P("fsdp", ("chip", "core")), into, into, into, outof, into, into, outof, gain, gain, rows),
        out_specs=(rows, rows, into, into, into, outof, into, into, outof, gain, gain),
        check_vma=False,
    )
```
